256 devices in a mesh: inst: 16 (over x, y_lo, core), space: 16 (over z, y_hi).
Axes of the slice: x: 4, y: 4 (y_hi: 2, y_lo: 2; y = y_hi * 2 + y_lo), z: 8, core: 2. Of those that a mesh axis runs over, the one named last changes fastest.
Arguments:
- adjoint: float32 [16, 5, 64, 16, 128], P('inst', None, 'space'), may hold values from -6 to 6
- jacobian: float32 [16, 7, 5, 5, 64, 16, 128], P('inst', None, None, None, 'space'), may hold values from -4 to 4
- volume: float32 [64, 16, 128], P('space'), may hold values from 0.5 to 2
- source: float32 [16, 5, 64, 16, 128], P('inst', None, 'space'), may hold values from -6 to 6
- surface_out: float32 [5, 64, 128], P(None, 'space'), may hold values from -0.5 to 0.5
- surface_in: float32 [5, 64, 128], P(None, 'space'), may hold values from -6 to 6
- station: int32 [64, 128], P('space'), may hold values from 0 to 255
- phi: float32 [40, 256], replicated, may hold values from -0.375 to 0.375
- inv_stiff: float32 [40], replicated, may hold values from 0.5 to 8
Outputs:
- residual: float32 [16, 5, 64, 16, 128], P('inst', None, 'space')
- modal: float32 [16, 40], P('inst')
The draws below stay inside these ranges and needn't reach their ends.
All inputs are finite; a program needn't handle non-finite values.
Results may differ from the reference program's by a relative error of at most 0.000078.
Values sent between devices are 32-bit elements; how exact they have to be, the bound alone decides.
A program may use at most 64 MiB of HBM per device.

```python
import math
import jax
import jax.numpy as jnp
from jax import lax

NV = 5
M = 40
NS = 256
NY = 16
NZ = 128
NT = 16
NX = 64


def plant(drawn, stream_key, least, largest):
    shape = drawn.shape
    place = [jax.random.randint(jax.random.fold_in(stream_key, axis), (), 0, shape[axis]) for axis in range(len(shape))]
    drawn = drawn.at[tuple(place)].set(least)
    longest = shape.index(max(shape))
    place[longest] = (place[longest] + 1) % shape[longest]
    return drawn.at[tuple(place)].set(largest)


def shard_levels(key, shape, cuts, least, largest):
    gain = 1.0
    for dim, shards_of in cuts:
        heights = jax.random.uniform(jax.random.fold_in(jax.random.fold_in(key, 6), dim), (shards_of,), jnp.float32, least / len(cuts), largest / len(cuts))
        gain = gain * jnp.repeat(jnp.exp(heights), shape[dim] // shards_of).reshape((-1,) + (1,) * (len(shape) - 1 - dim))
    return gain


def bell_draw(rng, shape, width, reach, cuts=(), dtype=jnp.bfloat16):
    level = shard_levels(rng, shape, cuts, -0.22, 0.18) if cuts else 1.0
    drawn = jax.random.normal(rng, shape, jnp.float32) * width * level
    return jnp.minimum(jnp.maximum(drawn, -reach), reach).astype(dtype)


def setup_inputs(seed: int = 0) -> dict:
    key_of = jax.random.split(jax.random.key(seed), 10)
    return {
        "adjoint": bell_draw(key_of[0], (NT, NV, NX, NY, NZ), 1.0, 6.0, ((0, 16), (2, 16)), jnp.float32),
        "jacobian": bell_draw(key_of[1], (NT, 7, NV, NV, NX, NY, NZ), 0.3, 4.0, ((0, 16), (4, 16)), jnp.float32),
        "volume": jnp.clip(jnp.exp(math.log(2.0) - 1.3862944 * jax.random.uniform(key_of[2], (NX, NY, NZ), jnp.float32) ** shard_levels(key_of[2], (NX, NY, NZ), ((0, 16),), -0.2, 0.2)), 0.5, 2.0),
        "source": bell_draw(key_of[3], (NT, NV, NX, NY, NZ), 1.0, 6.0, ((0, 16), (2, 16)), jnp.float32),
        "surface_out": bell_draw(key_of[4], (NV, NX, NZ), (NV * NX * NZ // NS) ** -0.5, 0.5, ((1, 16),), jnp.float32),
        "surface_in": bell_draw(key_of[5], (NV, NX, NZ), 1.0, 6.0, ((1, 16),), jnp.float32),
        "station": plant(jax.random.randint(key_of[6], (NX, NZ), 0, NS), jax.random.fold_in(key_of[6], 1), 0, NS - 1).astype(jnp.int32),
        "phi": bell_draw(key_of[7], (M, NS), NS ** -0.5, 0.375, (), jnp.float32),
        "inv_stiff": jnp.clip(jnp.exp(jax.random.uniform(key_of[8], (M,), jnp.float32, math.log(0.5), math.log(8.0))), 0.5, 8.0),
    }


def time_weights(count):
    index = jnp.arange(count)
    diff = index[:, None] - index[None, :]
    angle = jnp.pi * diff.astype(jnp.float32) / count
    parity = (1 - 2 * (diff % 2)).astype(jnp.float32)
    offdiag = diff != 0
    safe_sin = jnp.where(offdiag, jnp.sin(angle), jnp.float32(1.0))
    first = jnp.where(offdiag, 0.5 * parity * jnp.cos(angle) / safe_sin, jnp.float32(0.0))
    second = jnp.where(offdiag, -0.5 * parity / (safe_sin * safe_sin), -(count * count + 2) / 12.0)
    return first - 0.25 * second


def stencil(pair):
    blocks, lam = pair
    prod = jnp.einsum('dijxyz,ixyz->djxyz', blocks, lam, precision=lax.Precision.HIGHEST)
    flux = prod[0] + jnp.roll(prod[1], 1, axis=1) + jnp.roll(prod[2], -1, axis=1)
    flux = flux + jnp.pad(prod[3], ((0, 0), (0, 0), (1, 0), (0, 0)))[:, :, :-1]
    flux = flux + jnp.pad(prod[4], ((0, 0), (0, 0), (0, 1), (0, 0)))[:, :, 1:]
    flux = flux + jnp.pad(prod[5], ((0, 0), (0, 0), (0, 0), (1, 0)))[:, :, :, :-1]
    flux = flux + jnp.pad(prod[6], ((0, 0), (0, 0), (0, 0), (0, 1)))[:, :, :, 1:]
    return flux


def reference(adjoint, jacobian, volume, source, surface_out, surface_in, station, phi, inv_stiff):
    count = adjoint.shape[0]
    weights = time_weights(count)
    flux = lax.map(stencil, (jacobian, adjoint))
    spectral = volume[None, None] * jnp.einsum('mn,mjxyz->njxyz', weights, adjoint, precision=lax.Precision.HIGHEST)
    face = jnp.einsum('jxz,njxz->nxz', surface_out, adjoint[:, :, :, 0, :], precision=lax.Precision.HIGHEST)
    flat_station = station.reshape(-1)
    loads = jax.ops.segment_sum(face.reshape(count, -1).T, flat_station, phi.shape[1]).T
    modal = inv_stiff[None, :] * jnp.dot(loads, phi.T, precision=lax.Precision.HIGHEST)
    back = jnp.dot(modal, phi[:, flat_station], precision=lax.Precision.HIGHEST).reshape(face.shape)
    residual = flux + spectral - source
    residual = residual.at[:, :, :, 0, :].add(surface_in[None] * back[:, None])
    return residual, modal
```

```python
import functools

import numpy as np
import jax
import jax.numpy as jnp
from jax import lax
from jax.experimental import pallas as pl
from jax.experimental.pallas import tpu as pltpu
from jax.sharding import PartitionSpec as P

MESH = pl.DeviceIdType.MESH
FIRST = (0, 3)
COUNT = (3, 2)


def time_weight(count):
    k = np.arange(count)
    angle = np.pi * k / count
    parity = 1.0 - 2.0 * (k % 2)
    safe = np.where(k != 0, np.sin(angle), 1.0)
    first = np.where(k != 0, 0.5 * parity * np.cos(angle) / safe, 0.0)
    second = np.where(k != 0, -0.5 * parity / (safe * safe), -(count * count + 2) / 12.0)
    return first - 0.25 * second


def kernel(
    ni, ns,
    adj_hbm, jac_hbm, vol_hbm, src_hbm, so_hbm, si_hbm, st_hbm, phi_hbm, inv_hbm,
    res, modal,
    adj, jac, vol, src, so, si, st, phi, inv,
    inbox, outbox, mixed, halo_out, halo_in, gmat, row_out, row_in,
    local_sem, jac_sem, a_send, a_recv, b_send, b_recv, h_send, h_recv, m_send, m_recv,
):
    me = lax.axis_index("inst")
    sp = lax.axis_index("space")
    core = lax.rem(me, 2)
    chip = lax.div(me, 2)
    nc = ni // 2
    nv, nx, ny, nz = adj.shape
    halves = ny // 8

    def spot(c):
        return lax.div(c, halves), pl.multiple_of(lax.rem(c, halves) * 8, 8)

    small = [(adj_hbm.at[0], adj), (st_hbm, st), (phi_hbm, phi), (so_hbm, so), (inv_hbm, inv),
             (si_hbm, si), (vol_hbm, vol), (src_hbm.at[0], src)]
    copies = [pltpu.make_async_copy(a, b, local_sem.at[n]) for n, (a, b) in enumerate(small)]
    edge1 = pltpu.make_async_copy(jac_hbm.at[0, 1, :, :, nx - 1], jac.at[1, :, :, nx - 1], jac_sem.at[7])
    edge2 = pltpu.make_async_copy(jac_hbm.at[0, 2, :, :, 0], jac.at[2, :, :, 0], jac_sem.at[8])
    rest1 = pltpu.make_async_copy(jac_hbm.at[0, 1, :, :, 0:nx - 1], jac.at[1, :, :, 0:nx - 1], jac_sem.at[1])
    rest2 = pltpu.make_async_copy(jac_hbm.at[0, 2, :, :, 1:nx], jac.at[2, :, :, 1:nx], jac_sem.at[2])
    bulk = [pltpu.make_async_copy(jac_hbm.at[0, d], jac.at[d], jac_sem.at[d]) for d in (0, 3, 4, 5, 6)]
    for c in copies[:4]:
        c.start()
    edge1.start()
    edge2.start()
    for c in copies[4:]:
        c.start()
    rest1.start()
    rest2.start()
    for c in bulk:
        c.start()

    barrier = pltpu.get_barrier_semaphore()
    for k in range(1, ni):
        pl.semaphore_signal(barrier, inc=1, device_id={"inst": lax.rem(me + k, ni)}, device_id_type=MESH)
    for k in range(1, ns):
        pl.semaphore_signal(barrier, inc=1, device_id={"space": lax.rem(sp + k, ns)}, device_id_type=MESH)

    copies[1].wait()
    copies[2].wait()
    hi = phi[...].astype(jnp.bfloat16)
    lo = (phi[...] - hi.astype(jnp.float32)).astype(jnp.bfloat16)
    stations = phi.shape[1]
    modes = phi.shape[0]
    row_id = lax.broadcasted_iota(jnp.int32, (stations, nz), 0)
    for x in range(nx):
        onehot = (row_id == st[x:x + 1, :]).astype(jnp.float32).astype(jnp.bfloat16)
        gmat[x] = (jnp.dot(hi, onehot, preferred_element_type=jnp.float32)
                   + jnp.dot(lo, onehot, preferred_element_type=jnp.float32))

    copies[0].wait()
    pl.semaphore_wait(barrier, ni - 1 + ns - 1)

    def to_mixer(dc, cc):
        other = lax.rem(chip + dc, nc)
        peer = other * 2 + cc
        x, y = spot(other)
        return pltpu.make_async_remote_copy(
            src_ref=adj.at[pl.ds(FIRST[cc], COUNT[cc]), x, pl.ds(y, 8), :],
            dst_ref=inbox.at[me, pl.ds(0, COUNT[cc])],
            send_sem=a_send.at[dc * 2 + cc], recv_sem=a_recv.at[me],
            device_id={"inst": peer}, device_id_type=MESH)

    def others(act):
        for dc in range(1, nc):
            for cc in range(2):
                act(dc, cc)
        for cc in range(2):
            @pl.when(core != cc)
            def _():
                act(0, cc)

    others(lambda dc, cc: to_mixer(dc, cc).start())

    def halo(side):
        step = 1 if side == 0 else ns - 1
        return pltpu.make_async_remote_copy(
            src_ref=halo_out.at[side], dst_ref=halo_in.at[side],
            send_sem=h_send.at[side], recv_sem=h_recv.at[side],
            device_id={"space": lax.rem(sp + step, ns)}, device_id_type=MESH)

    def product(d, j, x):
        total = jac[d, 0, j, x] * adj[0, x]
        for i in range(1, nv):
            total = total + jac[d, i, j, x] * adj[i, x]
        return total

    edge1.wait()
    edge2.wait()
    for side, d, x in ((0, 1, nx - 1), (1, 2, 0)):
        for j in range(nv):
            halo_out[side, j] = product(d, j, x)
        halo(side).start()

    copies[3].wait()
    col = jnp.zeros((modes, nz), jnp.float32)
    for x in range(nx):
        face = so[0, x:x + 1, :] * adj[0, x, 0:1, :]
        for j in range(1, nv):
            face = face + so[j, x:x + 1, :] * adj[j, x, 0:1, :]
        col = col + gmat[x] * face
    col = jnp.sum(col, axis=1, keepdims=True)
    diag = (lax.broadcasted_iota(jnp.int32, (modes, nz), 0)
            == lax.broadcasted_iota(jnp.int32, (modes, nz), 1))
    share = jnp.sum(jnp.where(diag, col, 0.0), axis=0, keepdims=True)
    row_out[...] = share
    row_in[sp] = share

    def to_block(k):
        return pltpu.make_async_remote_copy(
            src_ref=row_out, dst_ref=row_in.at[sp],
            send_sem=m_send.at[k], recv_sem=m_recv.at[sp],
            device_id={"space": lax.rem(sp + k, ns)}, device_id_type=MESH)

    for k in range(1, ns):
        to_block(k).start()

    rest1.wait()
    rest2.wait()
    for c in bulk:
        c.wait()
    copies[7].wait()
    row = lax.broadcasted_iota(jnp.int32, (ny, nz), 0)
    lane = lax.broadcasted_iota(jnp.int32, (ny, nz), 1)

    def flux(j, carry):
        for x in range(nx):
            total = product(0, j, x) - src[j, x]
            if x > 0:
                total = total + product(1, j, x - 1)
            if x < nx - 1:
                total = total + product(2, j, x + 1)
            total = total + jnp.where(row == 0, 0.0, pltpu.roll(product(3, j, x), 1, 0))
            total = total + jnp.where(row == ny - 1, 0.0, pltpu.roll(product(4, j, x), ny - 1, 0))
            total = total + jnp.where(lane == 0, 0.0, pltpu.roll(product(5, j, x), 1, 1))
            total = total + jnp.where(lane == nz - 1, 0.0, pltpu.roll(product(6, j, x), nz - 1, 1))
            res[j, x] = total
        return carry

    lax.fori_loop(0, nv, flux, 0)

    my_x, my_y = spot(chip)
    for cc in range(2):
        @pl.when(core == cc)
        def _():
            inbox[me, 0:COUNT[cc]] = adj[FIRST[cc]:FIRST[cc] + COUNT[cc], my_x, pl.ds(my_y, 8), :]

            def arrival(dc, oc):
                source = lax.rem(chip + dc, nc) * 2 + oc
                block = inbox.at[source, pl.ds(0, COUNT[cc])]
                return pltpu.make_async_remote_copy(
                    src_ref=block, dst_ref=block, send_sem=a_send.at[dc * 2 + oc], recv_sem=a_recv.at[source],
                    device_id={"inst": source}, device_id_type=MESH)

            others(lambda dc, oc: arrival(dc, oc).wait_recv())

    weight = time_weight(ni)
    half = ni // 2

    def mix(t, carry):
        a = [inbox[lax.rem(me + k, ni), t] for k in range(ni)]
        even = [a[k] + a[k + half] for k in range(half)]
        odd = [a[k] - a[k + half] for k in range(half)]
        for d in range(half):
            near = [float(weight[(k - d) % ni]) for k in range(half)]
            far = [float(weight[(k - d + half) % ni]) for k in range(half)]
            plus = sum(even[k] * np.float32(0.5 * (near[k] + far[k])) for k in range(half))
            minus = sum(odd[k] * np.float32(0.5 * (near[k] - far[k])) for k in range(half))
            outbox[lax.rem(me + d, ni), t] = plus + minus
            outbox[lax.rem(me + d + half, ni), t] = plus - minus
        return carry

    lax.fori_loop(0, 3 - core, mix, 0)

    def back_home(cc, dc, oc):
        peer = lax.rem(chip + dc, nc) * 2 + oc
        return pltpu.make_async_remote_copy(
            src_ref=outbox.at[peer, pl.ds(0, COUNT[cc])],
            dst_ref=mixed.at[pl.ds(FIRST[cc], COUNT[cc]), my_x, pl.ds(my_y, 8), :],
            send_sem=b_send.at[dc * 2 + oc], recv_sem=b_recv.at[me],
            device_id={"inst": peer}, device_id_type=MESH)

    for cc in range(2):
        @pl.when(core == cc)
        def _():
            others(lambda dc, oc: back_home(cc, dc, oc).start())
            mixed[FIRST[cc]:FIRST[cc] + COUNT[cc], my_x, pl.ds(my_y, 8), :] = outbox[me, 0:COUNT[cc]]

    def row_arrival(k):
        source = lax.rem(sp + k, ns)
        return pltpu.make_async_remote_copy(
            src_ref=row_out, dst_ref=row_in.at[source], send_sem=m_send.at[k], recv_sem=m_recv.at[source],
            device_id={"space": source}, device_id_type=MESH)

    for k in range(1, ns):
        row_arrival(k).wait_recv()
    copies[4].wait()
    copies[5].wait()
    copies[6].wait()
    sums = jnp.sum(row_in[...], axis=0)
    coords = sums[:, 0:modes] * inv[...]
    modal[...] = coords
    square = (lax.broadcasted_iota(jnp.int32, (modes, modes), 0)
              == lax.broadcasted_iota(jnp.int32, (modes, modes), 1))
    column = jnp.sum(jnp.where(square, coords, 0.0), axis=1, keepdims=True)
    for x in range(nx):
        back = jnp.sum(gmat[x] * column, axis=0, keepdims=True)
        for j in range(nv):
            res[j, x, 0:1, :] = res[j, x, 0:1, :] + si[j, x:x + 1, :] * back

    halo(0).wait_recv()
    halo(1).wait_recv()
    for j in range(nv):
        res[j, 0] = res[j, 0] + halo_in[0, j]
        res[j, nx - 1] = res[j, nx - 1] + halo_in[1, j]

    def home_arrival(dc, oc):
        other = lax.rem(chip + dc, nc)
        x, y = spot(other)
        block = mixed.at[pl.ds(FIRST[oc], COUNT[oc]), x, pl.ds(y, 8), :]
        return pltpu.make_async_remote_copy(
            src_ref=block, dst_ref=block, send_sem=b_send.at[dc * 2 + oc], recv_sem=b_recv.at[other * 2 + oc],
            device_id={"inst": other * 2 + oc}, device_id_type=MESH)

    others(lambda dc, oc: home_arrival(dc, oc).wait_recv())
    for j in range(nv):
        for x in range(nx):
            res[j, x] = res[j, x] + vol[x] * mixed[j, x]

    others(lambda dc, cc: to_mixer(dc, cc).wait_send())
    for cc in range(2):
        @pl.when(core == cc)
        def _():
            others(lambda dc, oc: back_home(cc, dc, oc).wait_send())
    halo(0).wait_send()
    halo(1).wait_send()
    for k in range(1, ns):
        to_block(k).wait_send()


def solution(mesh):
    ni, ns = mesh.shape["inst"], mesh.shape["space"]
    placed = (
        P("inst", None, "space", None, None),
        P("inst", None, None, None, "space", None, None),
        P("space", None, None),
        P("inst", None, "space", None, None),
        P(None, "space", None),
        P(None, "space", None),
        P("space", None),
        P(),
        P(),
    )

    def body(adjoint, jacobian, volume, source, surface_out, surface_in, station, phi, inv_stiff):
        _, nv, nx, ny, nz = adjoint.shape
        modes, stations = phi.shape
        inv_row = inv_stiff.reshape(1, modes)
        f32 = jnp.float32
        operands = (adjoint, jacobian, volume, source, surface_out, surface_in, station, phi, inv_row)
        vmem = pltpu.VMEM
        sem = pltpu.SemaphoreType.DMA
        residual, modal = pl.pallas_call(
            functools.partial(kernel, ni, ns),
            out_shape=(jax.ShapeDtypeStruct((nv, nx, ny, nz), f32), jax.ShapeDtypeStruct((1, modes), f32)),
            in_specs=[pl.BlockSpec(memory_space=pltpu.HBM)] * len(operands),
            out_specs=(pl.BlockSpec(memory_space=pltpu.VMEM), pl.BlockSpec(memory_space=pltpu.VMEM)),
            scratch_shapes=[
                vmem((nv, nx, ny, nz), f32), vmem(jacobian.shape[1:], f32), vmem((nx, ny, nz), f32),
                vmem((nv, nx, ny, nz), f32), vmem((nv, nx, nz), f32), vmem((nv, nx, nz), f32),
                vmem((nx, nz), jnp.int32), vmem((modes, stations), f32), vmem((1, modes), f32),
                vmem((ni, 3, 8, nz), f32), vmem((ni, 3, 8, nz), f32), vmem((nv, nx, ny, nz), f32),
                vmem((2, nv, ny, nz), f32), vmem((2, nv, ny, nz), f32), vmem((nx, modes, nz), f32),
                vmem((1, nz), f32), vmem((ns, 1, nz), f32),
                sem((8,)), sem((9,)), sem((ni,)), sem((ni,)), sem((ni,)), sem((ni,)),
                sem((2,)), sem((2,)), sem((ns,)), sem((ns,)),
            ],
            compiler_params=pltpu.CompilerParams(
                collective_id=0, has_side_effects=True, vmem_limit_bytes=24 << 20),
        )(*[pltpu.with_memory_space_constraint(x, pltpu.HBM) for x in operands])
        return residual[None], modal

    return jax.shard_map(
        body, mesh=mesh, in_specs=placed,
        out_specs=(P("inst", None, "space", None, None), P("inst", None)), check_vma=False)
```

```python
import functools

import numpy as np
import jax
import jax.numpy as jnp
from jax import lax
from jax.experimental import pallas as pl
from jax.experimental.pallas import tpu as pltpu
from jax.sharding import PartitionSpec as P

MESH = pl.DeviceIdType.MESH
FIRST = (0, 3)
COUNT = (3, 2)


def time_weight(count):
    k = np.arange(count)
    angle = np.pi * k / count
    parity = 1.0 - 2.0 * (k % 2)
    safe = np.where(k != 0, np.sin(angle), 1.0)
    first = np.where(k != 0, 0.5 * parity * np.cos(angle) / safe, 0.0)
    second = np.where(k != 0, -0.5 * parity / (safe * safe), -(count * count + 2) / 12.0)
    return first - 0.25 * second


def kernel(
    ni, ns,
    adj_hbm, jac_hbm, vol_hbm, src_hbm, so_hbm, si_hbm, st_hbm, phi_hbm, inv_hbm,
    res, modal,
    adj, jac, vol, src, so, si, st, phi, inv,
    inbox, outbox, mixed, halo_out, halo_in, gmat, row_out, row_in,
    local_sem, jac_sem, a_send, a_recv, b_send, b_recv, h_send, h_recv, m_send, m_recv,
    ready_inst, ready_space,
):
    me = lax.axis_index("inst")
    sp = lax.axis_index("space")
    core = lax.rem(me, 2)
    chip = lax.div(me, 2)
    nc = ni // 2
    nv, nx, ny, nz = adj.shape
    halves = ny // 8

    def spot(c):
        return lax.div(c, halves), pl.multiple_of(lax.rem(c, halves) * 8, 8)

    small = [(adj_hbm.at[0], adj), (st_hbm, st), (phi_hbm, phi), (so_hbm, so), (inv_hbm, inv),
             (si_hbm, si), (vol_hbm, vol), (src_hbm.at[0], src)]
    copies = [pltpu.make_async_copy(a, b, local_sem.at[n]) for n, (a, b) in enumerate(small)]
    edge1 = pltpu.make_async_copy(jac_hbm.at[0, 1, :, :, nx - 1], jac.at[1, :, :, nx - 1], jac_sem.at[7])
    edge2 = pltpu.make_async_copy(jac_hbm.at[0, 2, :, :, 0], jac.at[2, :, :, 0], jac_sem.at[8])
    rest1 = pltpu.make_async_copy(jac_hbm.at[0, 1, :, :, 0:nx - 1], jac.at[1, :, :, 0:nx - 1], jac_sem.at[1])
    rest2 = pltpu.make_async_copy(jac_hbm.at[0, 2, :, :, 1:nx], jac.at[2, :, :, 1:nx], jac_sem.at[2])
    bulk = [pltpu.make_async_copy(jac_hbm.at[0, d], jac.at[d], jac_sem.at[d]) for d in (0, 3, 4, 5, 6)]
    for c in copies[:4]:
        c.start()
    edge1.start()
    edge2.start()
    for c in copies[4:]:
        c.start()
    rest1.start()
    rest2.start()
    for c in bulk:
        c.start()

    barrier = pltpu.get_barrier_semaphore()


    def signal_range(semaphore, axis, start, end):
        @pl.loop(start, end)
        def _(peer):
            pl.semaphore_signal(semaphore, inc=1, device_id={axis: peer}, device_id_type=MESH)

    signal_range(barrier, "space", sp + 1, ns)
    signal_range(barrier, "inst", me + 1, ni)

    copies[1].wait()
    copies[2].wait()
    hi = phi[...].astype(jnp.bfloat16)
    lo = (phi[...] - hi.astype(jnp.float32)).astype(jnp.bfloat16)
    stations = phi.shape[1]
    modes = phi.shape[0]
    row_id = lax.broadcasted_iota(jnp.int32, (stations, nz), 0)
    for x in range(nx):
        onehot = (row_id == st[x:x + 1, :]).astype(jnp.float32).astype(jnp.bfloat16)
        gmat[x] = (jnp.dot(hi, onehot, preferred_element_type=jnp.float32)
                   + jnp.dot(lo, onehot, preferred_element_type=jnp.float32))

    copies[0].wait()
    copies[3].wait()
    col = jnp.zeros((modes, nz), jnp.float32)
    for x in range(nx):
        face = so[0, x:x + 1, :] * adj[0, x, 0:1, :]
        for j in range(1, nv):
            face = face + so[j, x:x + 1, :] * adj[j, x, 0:1, :]
        col = col + gmat[x] * face
    col = jnp.sum(col, axis=1, keepdims=True)
    diag = (lax.broadcasted_iota(jnp.int32, (modes, nz), 0)
            == lax.broadcasted_iota(jnp.int32, (modes, nz), 1))
    share = jnp.sum(jnp.where(diag, col, 0.0), axis=0, keepdims=True)
    row_out[...] = share
    row_in[sp] = share

    def to_block(peer):
        return pltpu.make_async_remote_copy(
            src_ref=row_out, dst_ref=row_in.at[sp],
            send_sem=m_send.at[peer], recv_sem=m_recv.at[sp],
            device_id={"space": peer}, device_id_type=MESH)

    @pl.when(me + sp > 0)
    def _():
        pl.semaphore_wait(barrier, me + sp)

    @pl.loop(0, sp)
    def _(peer):
        to_block(peer).start()

    signal_range(ready_inst, "inst", 0, me)
    signal_range(ready_space, "space", 0, sp)

    def to_mixer(other, cc):
        x, y = spot(other)
        return pltpu.make_async_remote_copy(
            src_ref=adj.at[pl.ds(FIRST[cc], COUNT[cc]), x, pl.ds(y, 8), :],
            dst_ref=inbox.at[me, pl.ds(0, COUNT[cc])],
            send_sem=a_send.at[other * 2 + cc], recv_sem=a_recv.at[me],
            device_id={"inst": other * 2 + cc}, device_id_type=MESH)

    def before(act):
        @pl.when(core == 1)
        def _():
            act(chip, 0)

        @pl.loop(1, chip + 1)
        def _(dc):
            act(chip - dc, 0)
            act(chip - dc, 1)

    def after(act):
        @pl.when(core == 0)
        def _():
            act(chip, 1)

        @pl.loop(1, nc - chip)
        def _(dc):
            act(chip + dc, 0)
            act(chip + dc, 1)

    def others(act):
        before(act)
        after(act)

    before(lambda c, cc: to_mixer(c, cc).start())

    def halo(side):
        step = 1 if side == 0 else ns - 1
        return pltpu.make_async_remote_copy(
            src_ref=halo_out.at[side], dst_ref=halo_in.at[side],
            send_sem=h_send.at[side], recv_sem=h_recv.at[side],
            device_id={"space": lax.rem(sp + step, ns)}, device_id_type=MESH)

    def product(d, j, x):
        total = jac[d, 0, j, x] * adj[0, x]
        for i in range(1, nv):
            total = total + jac[d, i, j, x] * adj[i, x]
        return total

    edge1.wait()
    edge2.wait()
    for side, d, x in ((0, 1, nx - 1), (1, 2, 0)):
        for j in range(nv):
            halo_out[side, j] = product(d, j, x)

    @pl.when(sp == ns - 1)
    def _():
        halo(0).start()

    @pl.when(sp > 0)
    def _():
        halo(1).start()

    @pl.when(me < ni - 1)
    def _():
        pl.semaphore_wait(ready_inst, ni - 1 - me)
    after(lambda c, cc: to_mixer(c, cc).start())

    rest1.wait()
    rest2.wait()
    for c in bulk:
        c.wait()
    copies[7].wait()
    row = lax.broadcasted_iota(jnp.int32, (ny, nz), 0)
    lane = lax.broadcasted_iota(jnp.int32, (ny, nz), 1)

    def flux(j, carry):
        for x in range(nx):
            total = product(0, j, x) - src[j, x]
            if x > 0:
                total = total + product(1, j, x - 1)
            if x < nx - 1:
                total = total + product(2, j, x + 1)
            total = total + jnp.where(row == 0, 0.0, pltpu.roll(product(3, j, x), 1, 0))
            total = total + jnp.where(row == ny - 1, 0.0, pltpu.roll(product(4, j, x), ny - 1, 0))
            total = total + jnp.where(lane == 0, 0.0, pltpu.roll(product(5, j, x), 1, 1))
            total = total + jnp.where(lane == nz - 1, 0.0, pltpu.roll(product(6, j, x), nz - 1, 1))
            res[j, x] = total
        return carry

    lax.fori_loop(0, nv, flux, 0)

    my_x, my_y = spot(chip)
    for cc in range(2):
        @pl.when(core == cc)
        def _():
            inbox[me, 0:COUNT[cc]] = adj[FIRST[cc]:FIRST[cc] + COUNT[cc], my_x, pl.ds(my_y, 8), :]

            def arrival(other, oc):
                source = other * 2 + oc
                block = inbox.at[source, pl.ds(0, COUNT[cc])]
                return pltpu.make_async_remote_copy(
                    src_ref=block, dst_ref=block, send_sem=a_send.at[source], recv_sem=a_recv.at[source],
                    device_id={"inst": source}, device_id_type=MESH)

            others(lambda c, oc: arrival(c, oc).wait_recv())

    weight = time_weight(ni)
    half = ni // 2

    def mix(t, carry):
        a = [inbox[lax.rem(me + k, ni), t] for k in range(ni)]
        even = [a[k] + a[k + half] for k in range(half)]
        odd = [a[k] - a[k + half] for k in range(half)]
        for d in range(half):
            near = [float(weight[(k - d) % ni]) for k in range(half)]
            far = [float(weight[(k - d + half) % ni]) for k in range(half)]
            plus = sum(even[k] * np.float32(0.5 * (near[k] + far[k])) for k in range(half))
            minus = sum(odd[k] * np.float32(0.5 * (near[k] - far[k])) for k in range(half))
            outbox[lax.rem(me + d, ni), t] = plus + minus
            outbox[lax.rem(me + d + half, ni), t] = plus - minus
        return carry

    lax.fori_loop(0, 3 - core, mix, 0)

    def back_home(cc, other, oc):
        peer = other * 2 + oc
        return pltpu.make_async_remote_copy(
            src_ref=outbox.at[peer, pl.ds(0, COUNT[cc])],
            dst_ref=mixed.at[pl.ds(FIRST[cc], COUNT[cc]), my_x, pl.ds(my_y, 8), :],
            send_sem=b_send.at[peer], recv_sem=b_recv.at[me],
            device_id={"inst": peer}, device_id_type=MESH)

    for cc in range(2):
        @pl.when(core == cc)
        def _():
            others(lambda c, oc: back_home(cc, c, oc).start())
            mixed[FIRST[cc]:FIRST[cc] + COUNT[cc], my_x, pl.ds(my_y, 8), :] = outbox[me, 0:COUNT[cc]]

    @pl.when(sp < ns - 1)
    def _():
        pl.semaphore_wait(ready_space, ns - 1 - sp)

    @pl.loop(sp + 1, ns)
    def _(peer):
        to_block(peer).start()

    @pl.when(sp < ns - 1)
    def _():
        halo(0).start()

    @pl.when(sp == 0)
    def _():
        halo(1).start()

    def home_arrival(other, oc):
        x, y = spot(other)
        source = other * 2 + oc
        block = mixed.at[pl.ds(FIRST[oc], COUNT[oc]), x, pl.ds(y, 8), :]
        return pltpu.make_async_remote_copy(
            src_ref=block, dst_ref=block, send_sem=b_send.at[source], recv_sem=b_recv.at[source],
            device_id={"inst": source}, device_id_type=MESH)

    copies[4].wait()
    copies[5].wait()
    copies[6].wait()
    others(lambda c, oc: home_arrival(c, oc).wait_recv())
    for j in range(nv):
        for x in range(nx):
            res[j, x] = res[j, x] + vol[x] * mixed[j, x]

    halo(0).wait_recv()
    halo(1).wait_recv()
    for j in range(nv):
        res[j, 0] = res[j, 0] + halo_in[0, j]
        res[j, nx - 1] = res[j, nx - 1] + halo_in[1, j]

    def each_block(act):
        @pl.loop(0, sp)
        def _(peer):
            act(peer)

        @pl.loop(sp + 1, ns)
        def _(peer):
            act(peer)

    def row_arrival(source):
        return pltpu.make_async_remote_copy(
            src_ref=row_out, dst_ref=row_in.at[source], send_sem=m_send.at[source], recv_sem=m_recv.at[source],
            device_id={"space": source}, device_id_type=MESH)

    each_block(lambda peer: row_arrival(peer).wait_recv())
    sums = jnp.sum(row_in[...], axis=0)
    coords = sums[:, 0:modes] * inv[...]
    modal[...] = coords
    square = (lax.broadcasted_iota(jnp.int32, (modes, modes), 0)
              == lax.broadcasted_iota(jnp.int32, (modes, modes), 1))
    column = jnp.sum(jnp.where(square, coords, 0.0), axis=1, keepdims=True)
    for x in range(nx):
        back = jnp.sum(gmat[x] * column, axis=0, keepdims=True)
        for j in range(nv):
            res[j, x, 0:1, :] = res[j, x, 0:1, :] + si[j, x:x + 1, :] * back

    others(lambda c, cc: to_mixer(c, cc).wait_send())
    for cc in range(2):
        @pl.when(core == cc)
        def _():
            others(lambda c, oc: back_home(cc, c, oc).wait_send())
    halo(0).wait_send()
    halo(1).wait_send()
    each_block(lambda peer: to_block(peer).wait_send())


def solution(mesh):
    ni, ns = mesh.shape["inst"], mesh.shape["space"]
    placed = (
        P("inst", None, "space", None, None),
        P("inst", None, None, None, "space", None, None),
        P("space", None, None),
        P("inst", None, "space", None, None),
        P(None, "space", None),
        P(None, "space", None),
        P("space", None),
        P(),
        P(),
    )

    def body(adjoint, jacobian, volume, source, surface_out, surface_in, station, phi, inv_stiff):
        _, nv, nx, ny, nz = adjoint.shape
        modes, stations = phi.shape
        inv_row = inv_stiff.reshape(1, modes)
        f32 = jnp.float32
        operands = (adjoint, jacobian, volume, source, surface_out, surface_in, station, phi, inv_row)
        vmem = pltpu.VMEM
        sem = pltpu.SemaphoreType.DMA
        residual, modal = pl.pallas_call(
            functools.partial(kernel, ni, ns),
            out_shape=(jax.ShapeDtypeStruct((nv, nx, ny, nz), f32), jax.ShapeDtypeStruct((1, modes), f32)),
            in_specs=[pl.BlockSpec(memory_space=pltpu.HBM)] * len(operands),
            out_specs=(pl.BlockSpec(memory_space=pltpu.VMEM), pl.BlockSpec(memory_space=pltpu.VMEM)),
            scratch_shapes=[
                vmem((nv, nx, ny, nz), f32), vmem(jacobian.shape[1:], f32), vmem((nx, ny, nz), f32),
                vmem((nv, nx, ny, nz), f32), vmem((nv, nx, nz), f32), vmem((nv, nx, nz), f32),
                vmem((nx, nz), jnp.int32), vmem((modes, stations), f32), vmem((1, modes), f32),
                vmem((ni, 3, 8, nz), f32), vmem((ni, 3, 8, nz), f32), vmem((nv, nx, ny, nz), f32),
                vmem((2, nv, ny, nz), f32), vmem((2, nv, ny, nz), f32), vmem((nx, modes, nz), f32),
                vmem((1, nz), f32), vmem((ns, 1, nz), f32),
                sem((8,)), sem((9,)), sem((ni,)), sem((ni,)), sem((ni,)), sem((ni,)),
                sem((2,)), sem((2,)), sem((ns,)), sem((ns,)),
                pltpu.SemaphoreType.REGULAR, pltpu.SemaphoreType.REGULAR,
            ],
            compiler_params=pltpu.CompilerParams(
                collective_id=0, has_side_effects=True, vmem_limit_bytes=24 << 20),
        )(*[pltpu.with_memory_space_constraint(x, pltpu.HBM) for x in operands])
        return residual[None], modal

    return jax.shard_map(
        body, mesh=mesh, in_specs=placed,
        out_specs=(P("inst", None, "space", None, None), P("inst", None)), check_vma=False)
```

```python
import functools

import numpy as np
import jax
import jax.numpy as jnp
from jax import lax
from jax.experimental import pallas as pl
from jax.experimental.pallas import tpu as pltpu
from jax.sharding import PartitionSpec as P

MESH = pl.DeviceIdType.MESH
FIRST = (0, 3)
COUNT = (3, 2)


def time_weight(count):
    k = np.arange(count)
    angle = np.pi * k / count
    parity = 1.0 - 2.0 * (k % 2)
    safe = np.where(k != 0, np.sin(angle), 1.0)
    first = np.where(k != 0, 0.5 * parity * np.cos(angle) / safe, 0.0)
    second = np.where(k != 0, -0.5 * parity / (safe * safe), -(count * count + 2) / 12.0)
    return first - 0.25 * second


def kernel(
    ni, ns,
    adj_hbm, jac_hbm, vol_hbm, src_hbm, so_hbm, si_hbm, st_hbm, phi_hbm, inv_hbm,
    res, modal,
    adj, jac, vol, src, so, si, st, phi, inv,
    inbox, outbox, mixed, halo_out, halo_in, gmat, row_out, row_in,
    local_sem, jac_sem, a_send, a_recv, b_send, b_recv, h_send, h_recv, m_send, m_recv,
    ready_inst, ready_space,
):
    me = lax.axis_index("inst")
    sp = lax.axis_index("space")
    core = lax.rem(me, 2)
    chip = lax.div(me, 2)
    nc = ni // 2
    nv, nx, ny, nz = adj.shape
    halves = ny // 8

    def spot(c):
        return lax.div(c, halves), pl.multiple_of(lax.rem(c, halves) * 8, 8)

    small = [(adj_hbm.at[0], adj), (st_hbm, st), (phi_hbm, phi), (so_hbm, so), (inv_hbm, inv),
             (si_hbm, si), (vol_hbm, vol), (src_hbm.at[0], src)]
    copies = [pltpu.make_async_copy(a, b, local_sem.at[n]) for n, (a, b) in enumerate(small)]
    edge1 = pltpu.make_async_copy(jac_hbm.at[0, 1, :, :, nx - 1], jac.at[1, :, :, nx - 1], jac_sem.at[7])
    edge2 = pltpu.make_async_copy(jac_hbm.at[0, 2, :, :, 0], jac.at[2, :, :, 0], jac_sem.at[8])
    rest1 = pltpu.make_async_copy(jac_hbm.at[0, 1, :, :, 0:nx - 1], jac.at[1, :, :, 0:nx - 1], jac_sem.at[1])
    rest2 = pltpu.make_async_copy(jac_hbm.at[0, 2, :, :, 1:nx], jac.at[2, :, :, 1:nx], jac_sem.at[2])
    bulk = [pltpu.make_async_copy(jac_hbm.at[0, d], jac.at[d], jac_sem.at[d]) for d in (0, 3, 4, 5, 6)]
    for c in copies[:4]:
        c.start()
    edge1.start()
    edge2.start()
    for c in copies[4:]:
        c.start()
    rest1.start()
    rest2.start()
    for c in bulk:
        c.start()

    barrier = pltpu.get_barrier_semaphore()


    def signal_range(semaphore, axis, start, end):
        @pl.loop(start, end)
        def _(peer):
            pl.semaphore_signal(semaphore, inc=1, device_id={axis: peer}, device_id_type=MESH)

    signal_range(barrier, "space", sp + 1, ns)
    signal_range(barrier, "inst", me + 1, ni)

    @pl.when(me + sp > 0)
    def _():
        pl.semaphore_wait(barrier, me + sp)

    signal_range(ready_inst, "inst", 0, me)
    signal_range(ready_space, "space", 0, sp)

    def to_mixer(other, cc):
        x, y = spot(other)
        return pltpu.make_async_remote_copy(
            src_ref=adj_hbm.at[0, pl.ds(FIRST[cc], COUNT[cc]), x, pl.ds(y, 8), :],
            dst_ref=inbox.at[me, pl.ds(0, COUNT[cc])],
            send_sem=a_send.at[other * 2 + cc], recv_sem=a_recv.at[me],
            device_id={"inst": other * 2 + cc}, device_id_type=MESH)

    def before(act):
        @pl.when(core == 1)
        def _():
            act(chip, 0)

        @pl.loop(1, chip + 1)
        def _(dc):
            act(chip - dc, 0)
            act(chip - dc, 1)

    def after(act):
        @pl.when(core == 0)
        def _():
            act(chip, 1)

        @pl.loop(1, nc - chip)
        def _(dc):
            act(chip + dc, 0)
            act(chip + dc, 1)

    def others(act):
        before(act)
        after(act)

    before(lambda c, cc: to_mixer(c, cc).start())

    copies[1].wait()
    copies[2].wait()
    stations = phi.shape[1]
    modes = phi.shape[0]
    hi = phi[...].astype(jnp.bfloat16).astype(jnp.float32)
    parts = jnp.concatenate([hi, phi[...] - hi], axis=0).astype(jnp.bfloat16)
    row_id = lax.broadcasted_iota(jnp.int32, (stations, nz), 0)
    for x in range(nx):
        onehot = (row_id == st[x:x + 1, :]).astype(jnp.float32).astype(jnp.bfloat16)
        both = jnp.dot(parts, onehot, preferred_element_type=jnp.float32)
        gmat[x] = both[:modes] + both[modes:]

    copies[0].wait()
    copies[3].wait()
    col = jnp.zeros((modes, nz), jnp.float32)
    for x in range(nx):
        face = so[0, x:x + 1, :] * adj[0, x, 0:1, :]
        for j in range(1, nv):
            face = face + so[j, x:x + 1, :] * adj[j, x, 0:1, :]
        col = col + gmat[x] * face
    col = jnp.sum(col, axis=1, keepdims=True)
    diag = (lax.broadcasted_iota(jnp.int32, (modes, nz), 0)
            == lax.broadcasted_iota(jnp.int32, (modes, nz), 1))
    share = jnp.sum(jnp.where(diag, col, 0.0), axis=0, keepdims=True)
    row_out[...] = share
    row_in[sp] = share

    def to_block(peer):
        return pltpu.make_async_remote_copy(
            src_ref=row_out, dst_ref=row_in.at[sp],
            send_sem=m_send.at[peer], recv_sem=m_recv.at[sp],
            device_id={"space": peer}, device_id_type=MESH)

    @pl.loop(0, sp)
    def _(peer):
        to_block(peer).start()

    @pl.when(me < ni - 1)
    def _():
        pl.semaphore_wait(ready_inst, ni - 1 - me)
    after(lambda c, cc: to_mixer(c, cc).start())

    def halo(side):
        step = 1 if side == 0 else ns - 1
        return pltpu.make_async_remote_copy(
            src_ref=halo_out.at[side], dst_ref=halo_in.at[side],
            send_sem=h_send.at[side], recv_sem=h_recv.at[side],
            device_id={"space": lax.rem(sp + step, ns)}, device_id_type=MESH)

    def product(d, j, x):
        total = jac[d, 0, j, x] * adj[0, x]
        for i in range(1, nv):
            total = total + jac[d, i, j, x] * adj[i, x]
        return total

    edge1.wait()
    edge2.wait()
    for side, d, x in ((0, 1, nx - 1), (1, 2, 0)):
        for j in range(nv):
            halo_out[side, j] = product(d, j, x)

    @pl.when(sp == ns - 1)
    def _():
        halo(0).start()

    @pl.when(sp > 0)
    def _():
        halo(1).start()

    rest1.wait()
    rest2.wait()
    for c in bulk:
        c.wait()
    copies[7].wait()
    row = lax.broadcasted_iota(jnp.int32, (ny, nz), 0)
    lane = lax.broadcasted_iota(jnp.int32, (ny, nz), 1)

    def flux(j, carry):
        for x in range(nx):
            total = product(0, j, x) - src[j, x]
            if x > 0:
                total = total + product(1, j, x - 1)
            if x < nx - 1:
                total = total + product(2, j, x + 1)
            total = total + jnp.where(row == 0, 0.0, pltpu.roll(product(3, j, x), 1, 0))
            total = total + jnp.where(row == ny - 1, 0.0, pltpu.roll(product(4, j, x), ny - 1, 0))
            total = total + jnp.where(lane == 0, 0.0, pltpu.roll(product(5, j, x), 1, 1))
            total = total + jnp.where(lane == nz - 1, 0.0, pltpu.roll(product(6, j, x), nz - 1, 1))
            res[j, x] = total
        return carry

    lax.fori_loop(0, nv, flux, 0)

    my_x, my_y = spot(chip)
    for cc in range(2):
        @pl.when(core == cc)
        def _():
            inbox[me, 0:COUNT[cc]] = adj[FIRST[cc]:FIRST[cc] + COUNT[cc], my_x, pl.ds(my_y, 8), :]

            def arrival(other, oc):
                source = other * 2 + oc
                block = inbox.at[source, pl.ds(0, COUNT[cc])]
                return pltpu.make_async_remote_copy(
                    src_ref=block, dst_ref=block, send_sem=a_send.at[source], recv_sem=a_recv.at[source],
                    device_id={"inst": source}, device_id_type=MESH)

            others(lambda c, oc: arrival(c, oc).wait_recv())

    weight = time_weight(ni)
    half = ni // 2

    def mix(t, carry):
        a = [inbox[lax.rem(me + k, ni), t] for k in range(ni)]
        even = [a[k] + a[k + half] for k in range(half)]
        odd = [a[k] - a[k + half] for k in range(half)]
        for d in range(half):
            near = [float(weight[(k - d) % ni]) for k in range(half)]
            far = [float(weight[(k - d + half) % ni]) for k in range(half)]
            plus = sum(even[k] * np.float32(0.5 * (near[k] + far[k])) for k in range(half))
            minus = sum(odd[k] * np.float32(0.5 * (near[k] - far[k])) for k in range(half))
            outbox[lax.rem(me + d, ni), t] = plus + minus
            outbox[lax.rem(me + d + half, ni), t] = plus - minus
        return carry

    lax.fori_loop(0, 3 - core, mix, 0)

    def back_home(cc, other, oc):
        peer = other * 2 + oc
        return pltpu.make_async_remote_copy(
            src_ref=outbox.at[peer, pl.ds(0, COUNT[cc])],
            dst_ref=mixed.at[pl.ds(FIRST[cc], COUNT[cc]), my_x, pl.ds(my_y, 8), :],
            send_sem=b_send.at[peer], recv_sem=b_recv.at[me],
            device_id={"inst": peer}, device_id_type=MESH)

    for cc in range(2):
        @pl.when(core == cc)
        def _():
            others(lambda c, oc: back_home(cc, c, oc).start())
            mixed[FIRST[cc]:FIRST[cc] + COUNT[cc], my_x, pl.ds(my_y, 8), :] = outbox[me, 0:COUNT[cc]]

    @pl.when(sp < ns - 1)
    def _():
        pl.semaphore_wait(ready_space, ns - 1 - sp)

    @pl.loop(sp + 1, ns)
    def _(peer):
        to_block(peer).start()

    @pl.when(sp < ns - 1)
    def _():
        halo(0).start()

    @pl.when(sp == 0)
    def _():
        halo(1).start()

    def home_arrival(other, oc):
        x, y = spot(other)
        source = other * 2 + oc
        block = mixed.at[pl.ds(FIRST[oc], COUNT[oc]), x, pl.ds(y, 8), :]
        return pltpu.make_async_remote_copy(
            src_ref=block, dst_ref=block, send_sem=b_send.at[source], recv_sem=b_recv.at[source],
            device_id={"inst": source}, device_id_type=MESH)

    copies[4].wait()
    copies[5].wait()
    copies[6].wait()
    others(lambda c, oc: home_arrival(c, oc).wait_recv())
    for j in range(nv):
        for x in range(nx):
            res[j, x] = res[j, x] + vol[x] * mixed[j, x]

    halo(0).wait_recv()
    halo(1).wait_recv()
    for j in range(nv):
        res[j, 0] = res[j, 0] + halo_in[0, j]
        res[j, nx - 1] = res[j, nx - 1] + halo_in[1, j]

    def each_block(act):
        @pl.loop(0, sp)
        def _(peer):
            act(peer)

        @pl.loop(sp + 1, ns)
        def _(peer):
            act(peer)

    def row_arrival(source):
        return pltpu.make_async_remote_copy(
            src_ref=row_out, dst_ref=row_in.at[source], send_sem=m_send.at[source], recv_sem=m_recv.at[source],
            device_id={"space": source}, device_id_type=MESH)

    each_block(lambda peer: row_arrival(peer).wait_recv())
    sums = jnp.sum(row_in[...], axis=0)
    coords = sums[:, 0:modes] * inv[...]
    modal[...] = coords
    square = (lax.broadcasted_iota(jnp.int32, (modes, modes), 0)
              == lax.broadcasted_iota(jnp.int32, (modes, modes), 1))
    column = jnp.sum(jnp.where(square, coords, 0.0), axis=1, keepdims=True)
    for x in range(nx):
        back = jnp.sum(gmat[x] * column, axis=0, keepdims=True)
        for j in range(nv):
            res[j, x, 0:1, :] = res[j, x, 0:1, :] + si[j, x:x + 1, :] * back

    others(lambda c, cc: to_mixer(c, cc).wait_send())
    for cc in range(2):
        @pl.when(core == cc)
        def _():
            others(lambda c, oc: back_home(cc, c, oc).wait_send())
    halo(0).wait_send()
    halo(1).wait_send()
    each_block(lambda peer: to_block(peer).wait_send())


def put_out(res, modal, res_hbm, modal_hbm, sem):
    first = pltpu.make_async_copy(res, res_hbm.at[0], sem.at[0])
    second = pltpu.make_async_copy(modal, modal_hbm, sem.at[1])
    first.start()
    second.start()
    first.wait()
    second.wait()


def solution(mesh):
    ni, ns = mesh.shape["inst"], mesh.shape["space"]
    placed = (
        P("inst", None, "space", None, None),
        P("inst", None, None, None, "space", None, None),
        P("space", None, None),
        P("inst", None, "space", None, None),
        P(None, "space", None),
        P(None, "space", None),
        P("space", None),
        P(),
        P(),
    )

    def body(adjoint, jacobian, volume, source, surface_out, surface_in, station, phi, inv_stiff):
        _, nv, nx, ny, nz = adjoint.shape
        modes, stations = phi.shape
        inv_row = inv_stiff.reshape(1, modes)
        f32 = jnp.float32
        operands = (adjoint, jacobian, volume, source, surface_out, surface_in, station, phi, inv_row)
        vmem = pltpu.VMEM
        sem = pltpu.SemaphoreType.DMA
        residual, modal = pl.pallas_call(
            functools.partial(kernel, ni, ns),
            out_shape=(jax.ShapeDtypeStruct((nv, nx, ny, nz), f32), jax.ShapeDtypeStruct((1, modes), f32)),
            in_specs=[pl.BlockSpec(memory_space=pltpu.HBM)] * len(operands),
            out_specs=(pl.BlockSpec(memory_space=pltpu.VMEM), pl.BlockSpec(memory_space=pltpu.VMEM)),
            scratch_shapes=[
                vmem((nv, nx, ny, nz), f32), vmem(jacobian.shape[1:], f32), vmem((nx, ny, nz), f32),
                vmem((nv, nx, ny, nz), f32), vmem((nv, nx, nz), f32), vmem((nv, nx, nz), f32),
                vmem((nx, nz), jnp.int32), vmem((modes, stations), f32), vmem((1, modes), f32),
                vmem((ni, 3, 8, nz), f32), vmem((ni, 3, 8, nz), f32), vmem((nv, nx, ny, nz), f32),
                vmem((2, nv, ny, nz), f32), vmem((2, nv, ny, nz), f32), vmem((nx, modes, nz), f32),
                vmem((1, nz), f32), vmem((ns, 1, nz), f32),
                sem((8,)), sem((9,)), sem((ni,)), sem((ni,)), sem((ni,)), sem((ni,)),
                sem((2,)), sem((2,)), sem((ns,)), sem((ns,)),
                pltpu.SemaphoreType.REGULAR, pltpu.SemaphoreType.REGULAR,
            ],
            compiler_params=pltpu.CompilerParams(
                collective_id=0, has_side_effects=True, vmem_limit_bytes=24 << 20),
        )(*[pltpu.with_memory_space_constraint(x, pltpu.HBM) for x in operands])
        return pl.pallas_call(
            put_out,
            out_shape=(jax.ShapeDtypeStruct((1, nv, nx, ny, nz), f32), jax.ShapeDtypeStruct((1, modes), f32)),
            in_specs=[pl.BlockSpec(memory_space=vmem)] * 2,
            out_specs=(pl.BlockSpec(memory_space=pltpu.HBM), pl.BlockSpec(memory_space=pltpu.HBM)),
            scratch_shapes=[sem((2,))],
        )(*[pltpu.with_memory_space_constraint(x, vmem) for x in (residual, modal)])

    return jax.shard_map(
        body, mesh=mesh, in_specs=placed,
        out_specs=(P("inst", None, "space", None, None), P("inst", None)), check_vma=False)
```

```python
import functools

import numpy as np
import jax
import jax.numpy as jnp
from jax import lax
from jax.experimental import pallas as pl
from jax.experimental.pallas import tpu as pltpu
from jax.sharding import PartitionSpec as P

MESH = pl.DeviceIdType.MESH
FIRST = (0, 3)
COUNT = (3, 2)


def time_weight(count):
    k = np.arange(count)
    angle = np.pi * k / count
    parity = 1.0 - 2.0 * (k % 2)
    safe = np.where(k != 0, np.sin(angle), 1.0)
    first = np.where(k != 0, 0.5 * parity * np.cos(angle) / safe, 0.0)
    second = np.where(k != 0, -0.5 * parity / (safe * safe), -(count * count + 2) / 12.0)
    return first - 0.25 * second


def turn(block):
    z, y = lax.div(block, 2), lax.rem(block, 2)
    return jnp.where(z < 4, 10 * z, 51 + z) + 16 * y


def kernel(
    ni, ns,
    adj_hbm, jac_hbm, vol_hbm, src_hbm, so_hbm, si_hbm, st_hbm, phi_hbm, inv_hbm,
    res, modal,
    adj, jac, vol, src, so, si, st, phi, inv,
    inbox, outbox, mixed, halo_out, halo_in, gmat, row_out, row_in,
    local_sem, jac_sem, a_send, a_recv, b_send, b_recv, h_send, h_recv, m_send, m_recv,
    ready_space,
):
    me = lax.axis_index("inst")
    sp = lax.axis_index("space")
    core = lax.rem(me, 2)
    chip = lax.div(me, 2)
    nc = ni // 2
    nv, nx, ny, nz = adj.shape
    halves = ny // 8

    def spot(c):
        return lax.div(c, halves), pl.multiple_of(lax.rem(c, halves) * 8, 8)

    def send_signals(semaphore, axis, peer):
        pl.semaphore_signal(semaphore, inc=1, device_id={axis: peer}, device_id_type=MESH)

    barrier = pltpu.get_barrier_semaphore()

    @pl.loop(1, ni)
    def _(k):
        send_signals(barrier, "inst", lax.rem(me + k, ni))

    my_turn = turn(sp)

    def later_blocks(act):
        @pl.loop(0, ns)
        def _(peer):
            @pl.when(turn(peer) > my_turn)
            def _():
                act(peer)

    def earlier_blocks(act):
        @pl.loop(0, ns)
        def _(peer):
            @pl.when(turn(peer) < my_turn)
            def _():
                act(peer)

    later_blocks(lambda peer: send_signals(barrier, "space", peer))
    n_earlier = sum(jnp.where(turn(jnp.int32(p)) < my_turn, 1, 0) for p in range(ns))

    small = [(st_hbm, st), (phi_hbm, phi), (so_hbm, so), (adj_hbm.at[0], adj), (inv_hbm, inv),
             (si_hbm, si), (vol_hbm, vol), (src_hbm.at[0], src)]
    copies = [pltpu.make_async_copy(a, b, local_sem.at[n]) for n, (a, b) in enumerate(small)]
    edge1 = pltpu.make_async_copy(jac_hbm.at[0, 1, :, :, nx - 1], jac.at[1, :, :, nx - 1], jac_sem.at[7])
    edge2 = pltpu.make_async_copy(jac_hbm.at[0, 2, :, :, 0], jac.at[2, :, :, 0], jac_sem.at[8])
    rest1 = pltpu.make_async_copy(jac_hbm.at[0, 1, :, :, 0:nx - 1], jac.at[1, :, :, 0:nx - 1], jac_sem.at[1])
    rest2 = pltpu.make_async_copy(jac_hbm.at[0, 2, :, :, 1:nx], jac.at[2, :, :, 1:nx], jac_sem.at[2])
    bulk = [pltpu.make_async_copy(jac_hbm.at[0, d], jac.at[d], jac_sem.at[d]) for d in (0, 3, 4, 5, 6)]
    for c in copies[:4] + [edge1, edge2] + copies[4:] + [rest1, rest2] + bulk:
        c.start()

    copies[0].wait()
    copies[1].wait()
    modes, stations = phi.shape
    for x in range(nx):
        where = jnp.broadcast_to(st[x:x + 1, :], (modes, nz))
        column = lax.rem(where, nz)
        taken = jnp.zeros((modes, nz), jnp.float32)
        for start in range(0, stations, nz):
            found = jnp.take_along_axis(phi[:, start:start + nz], column, axis=1, mode="promise_in_bounds")
            taken = jnp.where(where - column == start, found, taken)
        gmat[x] = taken

    copies[2].wait()
    copies[3].wait()
    col = jnp.zeros((modes, nz), jnp.float32)
    for x in range(nx):
        face = so[0, x:x + 1, :] * adj[0, x, 0:1, :]
        for j in range(1, nv):
            face = face + so[j, x:x + 1, :] * adj[j, x, 0:1, :]
        col = col + gmat[x] * face
    col = jnp.sum(col, axis=1, keepdims=True)
    diag = (lax.broadcasted_iota(jnp.int32, (modes, nz), 0)
            == lax.broadcasted_iota(jnp.int32, (modes, nz), 1))
    share = jnp.sum(jnp.where(diag, col, 0.0), axis=0, keepdims=True)
    row_out[...] = share
    row_in[sp] = share

    def product(d, j, x):
        total = jac[d, 0, j, x] * adj[0, x]
        for i in range(1, nv):
            total = total + jac[d, i, j, x] * adj[i, x]
        return total

    edge1.wait()
    edge2.wait()
    for side, d, x in ((0, 1, nx - 1), (1, 2, 0)):
        for j in range(nv):
            halo_out[side, j] = product(d, j, x)

    pl.semaphore_wait(barrier, ni - 1 + n_earlier)

    def to_block(peer):
        return pltpu.make_async_remote_copy(
            src_ref=row_out, dst_ref=row_in.at[sp],
            send_sem=m_send.at[peer], recv_sem=m_recv.at[sp],
            device_id={"space": peer}, device_id_type=MESH)

    earlier_blocks(lambda peer: send_signals(ready_space, "space", peer))
    earlier_blocks(lambda peer: to_block(peer).start())

    def to_mixer(other, cc):
        x, y = spot(other)
        return pltpu.make_async_remote_copy(
            src_ref=adj.at[pl.ds(FIRST[cc], COUNT[cc]), x, pl.ds(y, 8), :],
            dst_ref=inbox.at[me, pl.ds(0, COUNT[cc])],
            send_sem=a_send.at[other * 2 + cc], recv_sem=a_recv.at[me],
            device_id={"inst": other * 2 + cc}, device_id_type=MESH)

    def others(act):
        @pl.loop(0, nc - 1)
        def _(k):
            chosen = lax.rem(chip + 1 + lax.rem(k + nc // 2 - 1, nc - 1), nc)
            act(chosen, 0)
            act(chosen, 1)

        for cc in range(2):
            @pl.when(core != cc)
            def _():
                act(chip, cc)

    others(lambda c, cc: to_mixer(c, cc).start())

    def halo(side):
        peer = lax.rem(sp + (1 if side == 0 else ns - 1), ns)
        return peer, pltpu.make_async_remote_copy(
            src_ref=halo_out.at[side], dst_ref=halo_in.at[side],
            send_sem=h_send.at[side], recv_sem=h_recv.at[side],
            device_id={"space": peer}, device_id_type=MESH)

    def send_halo(early):
        for side in range(2):
            peer, copy = halo(side)

            @pl.when((turn(peer) < my_turn) if early else (turn(peer) > my_turn))
            def _():
                copy.start()

    send_halo(True)

    rest1.wait()
    rest2.wait()
    for c in bulk:
        c.wait()
    copies[7].wait()
    row = lax.broadcasted_iota(jnp.int32, (ny, nz), 0)
    lane = lax.broadcasted_iota(jnp.int32, (ny, nz), 1)

    def flux(j, carry):
        for x in range(nx):
            total = product(0, j, x) - src[j, x]
            if x > 0:
                total = total + product(1, j, x - 1)
            if x < nx - 1:
                total = total + product(2, j, x + 1)
            total = total + jnp.where(row == 0, 0.0, pltpu.roll(product(3, j, x), 1, 0))
            total = total + jnp.where(row == ny - 1, 0.0, pltpu.roll(product(4, j, x), ny - 1, 0))
            total = total + jnp.where(lane == 0, 0.0, pltpu.roll(product(5, j, x), 1, 1))
            total = total + jnp.where(lane == nz - 1, 0.0, pltpu.roll(product(6, j, x), nz - 1, 1))
            res[j, x] = total
        return carry

    lax.fori_loop(0, nv, flux, 0)

    my_x, my_y = spot(chip)
    for cc in range(2):
        @pl.when(core == cc)
        def _():
            inbox[me, 0:COUNT[cc]] = adj[FIRST[cc]:FIRST[cc] + COUNT[cc], my_x, pl.ds(my_y, 8), :]

            def arrival(other, oc):
                source = other * 2 + oc
                block = inbox.at[source, pl.ds(0, COUNT[cc])]
                return pltpu.make_async_remote_copy(
                    src_ref=block, dst_ref=block, send_sem=a_send.at[source], recv_sem=a_recv.at[source],
                    device_id={"inst": source}, device_id_type=MESH)

            others(lambda c, oc: arrival(c, oc).wait_recv())

    weight = time_weight(ni)
    half = ni // 2

    def mix(t, carry):
        a = [inbox[lax.rem(me + k, ni), t] for k in range(ni)]
        even = [a[k] + a[k + half] for k in range(half)]
        odd = [a[k] - a[k + half] for k in range(half)]
        for d in range(half):
            near = [float(weight[(k - d) % ni]) for k in range(half)]
            far = [float(weight[(k - d + half) % ni]) for k in range(half)]
            plus = sum(even[k] * np.float32(0.5 * (near[k] + far[k])) for k in range(half))
            minus = sum(odd[k] * np.float32(0.5 * (near[k] - far[k])) for k in range(half))
            outbox[lax.rem(me + d, ni), t] = plus + minus
            outbox[lax.rem(me + d + half, ni), t] = plus - minus
        return carry

    lax.fori_loop(0, 3 - core, mix, 0)

    def back_home(cc, other, oc):
        peer = other * 2 + oc
        return pltpu.make_async_remote_copy(
            src_ref=outbox.at[peer, pl.ds(0, COUNT[cc])],
            dst_ref=mixed.at[pl.ds(FIRST[cc], COUNT[cc]), my_x, pl.ds(my_y, 8), :],
            send_sem=b_send.at[peer], recv_sem=b_recv.at[me],
            device_id={"inst": peer}, device_id_type=MESH)

    for cc in range(2):
        @pl.when(core == cc)
        def _():
            others(lambda c, oc: back_home(cc, c, oc).start())
            mixed[FIRST[cc]:FIRST[cc] + COUNT[cc], my_x, pl.ds(my_y, 8), :] = outbox[me, 0:COUNT[cc]]

    @pl.when(n_earlier < ns - 1)
    def _():
        pl.semaphore_wait(ready_space, ns - 1 - n_earlier)

    later_blocks(lambda peer: to_block(peer).start())
    send_halo(False)

    def home_arrival(other, oc):
        x, y = spot(other)
        source = other * 2 + oc
        block = mixed.at[pl.ds(FIRST[oc], COUNT[oc]), x, pl.ds(y, 8), :]
        return pltpu.make_async_remote_copy(
            src_ref=block, dst_ref=block, send_sem=b_send.at[source], recv_sem=b_recv.at[source],
            device_id={"inst": source}, device_id_type=MESH)

    copies[4].wait()
    copies[5].wait()
    copies[6].wait()
    others(lambda c, oc: home_arrival(c, oc).wait_recv())
    for j in range(nv):
        for x in range(nx):
            res[j, x] = res[j, x] + vol[x] * mixed[j, x]

    halo(0)[1].wait_recv()
    halo(1)[1].wait_recv()
    for j in range(nv):
        res[j, 0] = res[j, 0] + halo_in[0, j]
        res[j, nx - 1] = res[j, nx - 1] + halo_in[1, j]

    def each_block(act):
        @pl.loop(0, sp)
        def _(peer):
            act(peer)

        @pl.loop(sp + 1, ns)
        def _(peer):
            act(peer)

    def row_arrival(source):
        return pltpu.make_async_remote_copy(
            src_ref=row_out, dst_ref=row_in.at[source], send_sem=m_send.at[source], recv_sem=m_recv.at[source],
            device_id={"space": source}, device_id_type=MESH)

    each_block(lambda peer: row_arrival(peer).wait_recv())
    sums = jnp.sum(row_in[...], axis=0)
    coords = sums[:, 0:modes] * inv[...]
    modal[...] = coords
    square = (lax.broadcasted_iota(jnp.int32, (modes, modes), 0)
              == lax.broadcasted_iota(jnp.int32, (modes, modes), 1))
    column = jnp.sum(jnp.where(square, coords, 0.0), axis=1, keepdims=True)
    for x in range(nx):
        back = jnp.sum(gmat[x] * column, axis=0, keepdims=True)
        for j in range(nv):
            res[j, x, 0:1, :] = res[j, x, 0:1, :] + si[j, x:x + 1, :] * back

    others(lambda c, cc: to_mixer(c, cc).wait_send())
    for cc in range(2):
        @pl.when(core == cc)
        def _():
            others(lambda c, oc: back_home(cc, c, oc).wait_send())
    halo(0)[1].wait_send()
    halo(1)[1].wait_send()
    each_block(lambda peer: to_block(peer).wait_send())


def put_out(res, modal, res_hbm, modal_hbm, sem):
    first = pltpu.make_async_copy(res, res_hbm.at[0], sem.at[0])
    second = pltpu.make_async_copy(modal, modal_hbm, sem.at[1])
    first.start()
    second.start()
    first.wait()
    second.wait()


def solution(mesh):
    ni, ns = mesh.shape["inst"], mesh.shape["space"]
    placed = (
        P("inst", None, "space", None, None),
        P("inst", None, None, None, "space", None, None),
        P("space", None, None),
        P("inst", None, "space", None, None),
        P(None, "space", None),
        P(None, "space", None),
        P("space", None),
        P(),
        P(),
    )

    def body(adjoint, jacobian, volume, source, surface_out, surface_in, station, phi, inv_stiff):
        _, nv, nx, ny, nz = adjoint.shape
        modes, stations = phi.shape
        inv_row = inv_stiff.reshape(1, modes)
        f32 = jnp.float32
        operands = (adjoint, jacobian, volume, source, surface_out, surface_in, station, phi, inv_row)
        vmem = pltpu.VMEM
        sem = pltpu.SemaphoreType.DMA
        residual, modal = pl.pallas_call(
            functools.partial(kernel, ni, ns),
            out_shape=(jax.ShapeDtypeStruct((nv, nx, ny, nz), f32), jax.ShapeDtypeStruct((1, modes), f32)),
            in_specs=[pl.BlockSpec(memory_space=pltpu.HBM)] * len(operands),
            out_specs=(pl.BlockSpec(memory_space=pltpu.VMEM), pl.BlockSpec(memory_space=pltpu.VMEM)),
            scratch_shapes=[
                vmem((nv, nx, ny, nz), f32), vmem(jacobian.shape[1:], f32), vmem((nx, ny, nz), f32),
                vmem((nv, nx, ny, nz), f32), vmem((nv, nx, nz), f32), vmem((nv, nx, nz), f32),
                vmem((nx, nz), jnp.int32), vmem((modes, stations), f32), vmem((1, modes), f32),
                vmem((ni, 3, 8, nz), f32), vmem((ni, 3, 8, nz), f32), vmem((nv, nx, ny, nz), f32),
                vmem((2, nv, ny, nz), f32), vmem((2, nv, ny, nz), f32), vmem((nx, modes, nz), f32),
                vmem((1, nz), f32), vmem((ns, 1, nz), f32),
                sem((8,)), sem((9,)), sem((ni,)), sem((ni,)), sem((ni,)), sem((ni,)),
                sem((2,)), sem((2,)), sem((ns,)), sem((ns,)),
                pltpu.SemaphoreType.REGULAR,
            ],
            compiler_params=pltpu.CompilerParams(
                collective_id=0, has_side_effects=True, vmem_limit_bytes=24 << 20),
        )(*[pltpu.with_memory_space_constraint(x, pltpu.HBM) for x in operands])
        return pl.pallas_call(
            put_out,
            out_shape=(jax.ShapeDtypeStruct((1, nv, nx, ny, nz), f32), jax.ShapeDtypeStruct((1, modes), f32)),
            in_specs=[pl.BlockSpec(memory_space=vmem)] * 2,
            out_specs=(pl.BlockSpec(memory_space=pltpu.HBM), pl.BlockSpec(memory_space=pltpu.HBM)),
            scratch_shapes=[sem((2,))],
        )(*[pltpu.with_memory_space_constraint(x, vmem) for x in (residual, modal)])

    return jax.shard_map(
        body, mesh=mesh, in_specs=placed,
        out_specs=(P("inst", None, "space", None, None), P("inst", None)), check_vma=False)
```

```python
import functools

import numpy as np
import jax
import jax.numpy as jnp
from jax import lax
from jax.experimental import pallas as pl
from jax.experimental.pallas import tpu as pltpu
from jax.sharding import PartitionSpec as P

MESH = pl.DeviceIdType.MESH
FIRST = (0, 3)
COUNT = (3, 2)


def time_weight(count):
    k = np.arange(count)
    angle = np.pi * k / count
    parity = 1.0 - 2.0 * (k % 2)
    safe = np.where(k != 0, np.sin(angle), 1.0)
    first = np.where(k != 0, 0.5 * parity * np.cos(angle) / safe, 0.0)
    second = np.where(k != 0, -0.5 * parity / (safe * safe), -(count * count + 2) / 12.0)
    return first - 0.25 * second


def turn(block):
    z, y = lax.div(block, 2), lax.rem(block, 2)
    return jnp.where(z < 4, 10 * z, 51 + z) + 16 * y


def kernel(
    ni, ns,
    adj_hbm, jac_hbm, vol_hbm, src_hbm, so_hbm, si_hbm, st_hbm, phi_hbm, inv_hbm,
    res, modal,
    adj, jac, vol, src, so, si, st, phi, inv,
    inbox, outbox, mixed, halo_out, halo_in, gmat, row_out, row_in,
    local_sem, jac_sem, a_send, a_recv, b_send, b_recv, h_send, h_recv, m_send, m_recv,
    ready_space,
):
    me = lax.axis_index("inst")
    sp = lax.axis_index("space")
    core = lax.rem(me, 2)
    chip = lax.div(me, 2)
    nc = ni // 2
    nv, nx, ny, nz = adj.shape
    halves = ny // 8

    def spot(c):
        return lax.div(c, halves), pl.multiple_of(lax.rem(c, halves) * 8, 8)

    def send_signals(semaphore, axis, peer):
        pl.semaphore_signal(semaphore, inc=1, device_id={axis: peer}, device_id_type=MESH)

    barrier = pltpu.get_barrier_semaphore()

    @pl.loop(1, ni)
    def _(k):
        send_signals(barrier, "inst", lax.rem(me + k, ni))

    my_turn = turn(sp)

    def later_blocks(act):
        @pl.loop(0, ns)
        def _(k):
            far = k - ns // 2
            peer = jnp.where(far < 0, k, ns // 2 + lax.rem(2 * far + ns, ns // 2) + lax.div(far, ns // 4))

            @pl.when(turn(peer) > my_turn)
            def _():
                act(peer)

    def earlier_blocks(act):
        @pl.loop(0, ns)
        def _(peer):
            @pl.when(turn(peer) < my_turn)
            def _():
                act(peer)

    later_blocks(lambda peer: send_signals(barrier, "space", peer))
    n_earlier = sum(jnp.where(turn(jnp.int32(p)) < my_turn, 1, 0) for p in range(ns))

    small = [(st_hbm, st), (phi_hbm, phi), (so_hbm, so), (adj_hbm.at[0], adj), (inv_hbm, inv),
             (si_hbm, si), (vol_hbm, vol), (src_hbm.at[0], src)]
    copies = [pltpu.make_async_copy(a, b, local_sem.at[n]) for n, (a, b) in enumerate(small)]
    edge1 = pltpu.make_async_copy(jac_hbm.at[0, 1, :, :, nx - 1], jac.at[1, :, :, nx - 1], jac_sem.at[7])
    edge2 = pltpu.make_async_copy(jac_hbm.at[0, 2, :, :, 0], jac.at[2, :, :, 0], jac_sem.at[8])
    rest1 = pltpu.make_async_copy(jac_hbm.at[0, 1, :, :, 0:nx - 1], jac.at[1, :, :, 0:nx - 1], jac_sem.at[1])
    rest2 = pltpu.make_async_copy(jac_hbm.at[0, 2, :, :, 1:nx], jac.at[2, :, :, 1:nx], jac_sem.at[2])
    bulk = [pltpu.make_async_copy(jac_hbm.at[0, d], jac.at[d], jac_sem.at[d]) for d in (0, 3, 4, 5, 6)]
    for c in copies[:4] + [edge1, edge2] + copies[4:] + [rest1, rest2] + bulk:
        c.start()

    copies[0].wait()
    copies[1].wait()
    modes, stations = phi.shape
    for x in range(nx):
        where = jnp.broadcast_to(st[x:x + 1, :], (modes, nz))
        column = lax.rem(where, nz)
        taken = jnp.zeros((modes, nz), jnp.float32)
        for start in range(0, stations, nz):
            found = jnp.take_along_axis(phi[:, start:start + nz], column, axis=1, mode="promise_in_bounds")
            taken = jnp.where(where - column == start, found, taken)
        gmat[x] = taken

    copies[2].wait()
    copies[3].wait()
    col = jnp.zeros((modes, nz), jnp.float32)
    for x in range(nx):
        face = so[0, x:x + 1, :] * adj[0, x, 0:1, :]
        for j in range(1, nv):
            face = face + so[j, x:x + 1, :] * adj[j, x, 0:1, :]
        col = col + gmat[x] * face
    col = jnp.sum(col, axis=1, keepdims=True)
    diag = (lax.broadcasted_iota(jnp.int32, (modes, nz), 0)
            == lax.broadcasted_iota(jnp.int32, (modes, nz), 1))
    share = jnp.sum(jnp.where(diag, col, 0.0), axis=0, keepdims=True)
    row_out[...] = share
    row_in[sp] = share

    def product(d, j, x):
        total = jac[d, 0, j, x] * adj[0, x]
        for i in range(1, nv):
            total = total + jac[d, i, j, x] * adj[i, x]
        return total

    edge1.wait()
    edge2.wait()
    for side, d, x in ((0, 1, nx - 1), (1, 2, 0)):
        for j in range(nv):
            halo_out[side, j] = product(d, j, x)

    pl.semaphore_wait(barrier, ni - 1 + n_earlier)

    def to_block(peer):
        return pltpu.make_async_remote_copy(
            src_ref=row_out, dst_ref=row_in.at[sp],
            send_sem=m_send.at[peer], recv_sem=m_recv.at[sp],
            device_id={"space": peer}, device_id_type=MESH)

    earlier_blocks(lambda peer: send_signals(ready_space.at[sp], "space", peer))
    earlier_blocks(lambda peer: to_block(peer).start())

    def to_mixer(other, cc):
        x, y = spot(other)
        return pltpu.make_async_remote_copy(
            src_ref=adj.at[pl.ds(FIRST[cc], COUNT[cc]), x, pl.ds(y, 8), :],
            dst_ref=inbox.at[me, pl.ds(0, COUNT[cc])],
            send_sem=a_send.at[other * 2 + cc], recv_sem=a_recv.at[me],
            device_id={"inst": other * 2 + cc}, device_id_type=MESH)

    def others(act):
        @pl.loop(0, nc - 1)
        def _(k):
            chosen = lax.rem(chip + 1 + lax.rem(k + nc // 2 - 1, nc - 1), nc)
            act(chosen, 0)
            act(chosen, 1)

        for cc in range(2):
            @pl.when(core != cc)
            def _():
                act(chip, cc)

    others(lambda c, cc: to_mixer(c, cc).start())

    def halo(side):
        peer = lax.rem(sp + (1 if side == 0 else ns - 1), ns)
        return peer, pltpu.make_async_remote_copy(
            src_ref=halo_out.at[side], dst_ref=halo_in.at[side],
            send_sem=h_send.at[side], recv_sem=h_recv.at[side],
            device_id={"space": peer}, device_id_type=MESH)

    for side in range(2):
        target, copy = halo(side)

        @pl.when(turn(target) < my_turn)
        def _():
            copy.start()

    rest1.wait()
    rest2.wait()
    for c in bulk:
        c.wait()
    copies[7].wait()
    row = lax.broadcasted_iota(jnp.int32, (ny, nz), 0)
    lane = lax.broadcasted_iota(jnp.int32, (ny, nz), 1)

    def flux(j, carry):
        for x in range(nx):
            total = product(0, j, x) - src[j, x]
            if x > 0:
                total = total + product(1, j, x - 1)
            if x < nx - 1:
                total = total + product(2, j, x + 1)
            total = total + jnp.where(row == 0, 0.0, pltpu.roll(product(3, j, x), 1, 0))
            total = total + jnp.where(row == ny - 1, 0.0, pltpu.roll(product(4, j, x), ny - 1, 0))
            total = total + jnp.where(lane == 0, 0.0, pltpu.roll(product(5, j, x), 1, 1))
            total = total + jnp.where(lane == nz - 1, 0.0, pltpu.roll(product(6, j, x), nz - 1, 1))
            res[j, x] = total
        return carry

    lax.fori_loop(0, nv, flux, 0)

    def is_near(peer):
        return jnp.where(jnp.where(peer > sp, peer - sp, sp - peer) == 1, 1, 0)

    for side in range(2):
        target, copy = halo(side)

        @pl.when((turn(target) > my_turn) & (is_near(target) == 1))
        def _():
            pl.semaphore_wait(ready_space.at[target], 1)
            copy.start()
            to_block(target).start()

    my_x, my_y = spot(chip)
    for cc in range(2):
        @pl.when(core == cc)
        def _():
            inbox[me, 0:COUNT[cc]] = adj[FIRST[cc]:FIRST[cc] + COUNT[cc], my_x, pl.ds(my_y, 8), :]

            def arrival(other, oc):
                source = other * 2 + oc
                block = inbox.at[source, pl.ds(0, COUNT[cc])]
                return pltpu.make_async_remote_copy(
                    src_ref=block, dst_ref=block, send_sem=a_send.at[source], recv_sem=a_recv.at[source],
                    device_id={"inst": source}, device_id_type=MESH)

            others(lambda c, oc: arrival(c, oc).wait_recv())

    weight = time_weight(ni)
    half = ni // 2

    def mix(t, carry):
        a = [inbox[lax.rem(me + k, ni), t] for k in range(ni)]
        even = [a[k] + a[k + half] for k in range(half)]
        odd = [a[k] - a[k + half] for k in range(half)]
        for d in range(half):
            near = [float(weight[(k - d) % ni]) for k in range(half)]
            far = [float(weight[(k - d + half) % ni]) for k in range(half)]
            plus = sum(even[k] * np.float32(0.5 * (near[k] + far[k])) for k in range(half))
            minus = sum(odd[k] * np.float32(0.5 * (near[k] - far[k])) for k in range(half))
            outbox[lax.rem(me + d, ni), t] = plus + minus
            outbox[lax.rem(me + d + half, ni), t] = plus - minus
        return carry

    lax.fori_loop(0, 3 - core, mix, 0)

    def back_home(cc, other, oc):
        peer = other * 2 + oc
        return pltpu.make_async_remote_copy(
            src_ref=outbox.at[peer, pl.ds(0, COUNT[cc])],
            dst_ref=mixed.at[pl.ds(FIRST[cc], COUNT[cc]), my_x, pl.ds(my_y, 8), :],
            send_sem=b_send.at[peer], recv_sem=b_recv.at[me],
            device_id={"inst": peer}, device_id_type=MESH)

    for cc in range(2):
        @pl.when(core == cc)
        def _():
            others(lambda c, oc: back_home(cc, c, oc).start())
            mixed[FIRST[cc]:FIRST[cc] + COUNT[cc], my_x, pl.ds(my_y, 8), :] = outbox[me, 0:COUNT[cc]]

    def late(peer):
        @pl.when(is_near(peer) == 0)
        def _():
            pl.semaphore_wait(ready_space.at[peer], 1)
            to_block(peer).start()

    later_blocks(late)
    for side in range(2):
        target, copy = halo(side)

        @pl.when((turn(target) > my_turn) & (is_near(target) == 0))
        def _():
            copy.start()

    others(lambda c, cc: to_mixer(c, cc).wait_send())

    def home_arrival(other, oc):
        x, y = spot(other)
        source = other * 2 + oc
        block = mixed.at[pl.ds(FIRST[oc], COUNT[oc]), x, pl.ds(y, 8), :]
        return pltpu.make_async_remote_copy(
            src_ref=block, dst_ref=block, send_sem=b_send.at[source], recv_sem=b_recv.at[source],
            device_id={"inst": source}, device_id_type=MESH)

    copies[4].wait()
    copies[5].wait()
    copies[6].wait()
    halo(0)[1].wait_recv()
    halo(1)[1].wait_recv()
    for j in range(nv):
        res[j, 0] = res[j, 0] + halo_in[0, j]
        res[j, nx - 1] = res[j, nx - 1] + halo_in[1, j]

    def each_block(act):
        @pl.loop(0, sp)
        def _(peer):
            act(peer)

        @pl.loop(sp + 1, ns)
        def _(peer):
            act(peer)

    def row_arrival(source):
        return pltpu.make_async_remote_copy(
            src_ref=row_out, dst_ref=row_in.at[source], send_sem=m_send.at[source], recv_sem=m_recv.at[source],
            device_id={"space": source}, device_id_type=MESH)

    each_block(lambda peer: row_arrival(peer).wait_recv())
    sums = jnp.sum(row_in[...], axis=0)
    coords = sums[:, 0:modes] * inv[...]
    modal[...] = coords
    square = (lax.broadcasted_iota(jnp.int32, (modes, modes), 0)
              == lax.broadcasted_iota(jnp.int32, (modes, modes), 1))
    column = jnp.sum(jnp.where(square, coords, 0.0), axis=1, keepdims=True)
    for x in range(nx):
        back = jnp.sum(gmat[x] * column, axis=0, keepdims=True)
        for j in range(nv):
            res[j, x, 0:1, :] = res[j, x, 0:1, :] + si[j, x:x + 1, :] * back

    halo(0)[1].wait_send()
    halo(1)[1].wait_send()
    each_block(lambda peer: to_block(peer).wait_send())
    for cc in range(2):
        @pl.when(core == cc)
        def _():
            others(lambda c, oc: back_home(cc, c, oc).wait_send())

    others(lambda c, oc: home_arrival(c, oc).wait_recv())
    for j in range(nv):
        for x in range(nx):
            res[j, x] = res[j, x] + vol[x] * mixed[j, x]


def put_out(res, modal, res_hbm, modal_hbm, sem):
    first = pltpu.make_async_copy(res, res_hbm.at[0], sem.at[0])
    second = pltpu.make_async_copy(modal, modal_hbm, sem.at[1])
    first.start()
    second.start()
    first.wait()
    second.wait()


def solution(mesh):
    ni, ns = mesh.shape["inst"], mesh.shape["space"]
    placed = (
        P("inst", None, "space", None, None),
        P("inst", None, None, None, "space", None, None),
        P("space", None, None),
        P("inst", None, "space", None, None),
        P(None, "space", None),
        P(None, "space", None),
        P("space", None),
        P(),
        P(),
    )

    def body(adjoint, jacobian, volume, source, surface_out, surface_in, station, phi, inv_stiff):
        _, nv, nx, ny, nz = adjoint.shape
        modes, stations = phi.shape
        inv_row = inv_stiff.reshape(1, modes)
        f32 = jnp.float32
        operands = (adjoint, jacobian, volume, source, surface_out, surface_in, station, phi, inv_row)
        vmem = pltpu.VMEM
        sem = pltpu.SemaphoreType.DMA
        residual, modal = pl.pallas_call(
            functools.partial(kernel, ni, ns),
            out_shape=(jax.ShapeDtypeStruct((nv, nx, ny, nz), f32), jax.ShapeDtypeStruct((1, modes), f32)),
            in_specs=[pl.BlockSpec(memory_space=pltpu.HBM)] * len(operands),
            out_specs=(pl.BlockSpec(memory_space=pltpu.VMEM), pl.BlockSpec(memory_space=pltpu.VMEM)),
            scratch_shapes=[
                vmem((nv, nx, ny, nz), f32), vmem(jacobian.shape[1:], f32), vmem((nx, ny, nz), f32),
                vmem((nv, nx, ny, nz), f32), vmem((nv, nx, nz), f32), vmem((nv, nx, nz), f32),
                vmem((nx, nz), jnp.int32), vmem((modes, stations), f32), vmem((1, modes), f32),
                vmem((ni, 3, 8, nz), f32), vmem((ni, 3, 8, nz), f32), vmem((nv, nx, ny, nz), f32),
                vmem((2, nv, ny, nz), f32), vmem((2, nv, ny, nz), f32), vmem((nx, modes, nz), f32),
                vmem((1, nz), f32), vmem((ns, 1, nz), f32),
                sem((8,)), sem((9,)), sem((ni,)), sem((ni,)), sem((ni,)), sem((ni,)),
                sem((2,)), sem((2,)), sem((ns,)), sem((ns,)),
                pltpu.SemaphoreType.REGULAR((ns,)),
            ],
            compiler_params=pltpu.CompilerParams(
                collective_id=0, has_side_effects=True, vmem_limit_bytes=24 << 20),
        )(*[pltpu.with_memory_space_constraint(x, pltpu.HBM) for x in operands])
        return pl.pallas_call(
            put_out,
            out_shape=(jax.ShapeDtypeStruct((1, nv, nx, ny, nz), f32), jax.ShapeDtypeStruct((1, modes), f32)),
            in_specs=[pl.BlockSpec(memory_space=vmem)] * 2,
            out_specs=(pl.BlockSpec(memory_space=pltpu.HBM), pl.BlockSpec(memory_space=pltpu.HBM)),
            scratch_shapes=[sem((2,))],
        )(*[pltpu.with_memory_space_constraint(x, vmem) for x in (residual, modal)])

    return jax.shard_map(
        body, mesh=mesh, in_specs=placed,
        out_specs=(P("inst", None, "space", None, None), P("inst", None)), check_vma=False)
```

```python
import functools

import numpy as np
import jax
import jax.numpy as jnp
from jax import lax
from jax.experimental import pallas as pl
from jax.experimental.pallas import tpu as pltpu
from jax.sharding import PartitionSpec as P

MESH = pl.DeviceIdType.MESH
FIRST = (0, 3)
COUNT = (3, 2)


def time_weight(count):
    k = np.arange(count)
    angle = np.pi * k / count
    parity = 1.0 - 2.0 * (k % 2)
    safe = np.where(k != 0, np.sin(angle), 1.0)
    first = np.where(k != 0, 0.5 * parity * np.cos(angle) / safe, 0.0)
    second = np.where(k != 0, -0.5 * parity / (safe * safe), -(count * count + 2) / 12.0)
    return first - 0.25 * second


SOON = 20


def turn(block):
    z, y = lax.div(block, 2), lax.rem(block, 2)
    return jnp.where(z < 4, 10 * z, 51 + z) + 16 * y


def kernel(
    ni, ns,
    adj_hbm, jac_hbm, vol_hbm, src_hbm, so_hbm, si_hbm, st_hbm, phi_hbm, inv_hbm,
    res, modal,
    adj, jac, vol, src, so, si, st, phi, inv,
    inbox, outbox, mixed, halo_out, halo_in, gmat, row_out, row_in,
    local_sem, jac_sem, a_send, a_recv, b_send, b_recv, h_send, h_recv, m_send, m_recv,
    ready_space,
):
    me = lax.axis_index("inst")
    sp = lax.axis_index("space")
    core = lax.rem(me, 2)
    chip = lax.div(me, 2)
    nc = ni // 2
    nv, nx, ny, nz = adj.shape
    halves = ny // 8

    def spot(c):
        return lax.div(c, halves), pl.multiple_of(lax.rem(c, halves) * 8, 8)

    def send_signals(semaphore, axis, peer):
        pl.semaphore_signal(semaphore, inc=1, device_id={axis: peer}, device_id_type=MESH)

    barrier = pltpu.get_barrier_semaphore()

    @pl.loop(1, ni)
    def _(k):
        send_signals(barrier, "inst", lax.rem(me + k, ni))

    my_turn = turn(sp)

    def later_blocks(act):
        @pl.loop(0, ns)
        def _(k):
            far = k - ns // 2
            peer = jnp.where(far < 0, k, ns // 2 + lax.rem(2 * far + ns, ns // 2) + lax.div(far, ns // 4))

            @pl.when(turn(peer) > my_turn)
            def _():
                act(peer)

    def earlier_blocks(act):
        @pl.loop(0, ns)
        def _(peer):
            @pl.when(turn(peer) < my_turn)
            def _():
                act(peer)

    later_blocks(lambda peer: send_signals(barrier, "space", peer))
    n_earlier = sum(jnp.where(turn(jnp.int32(p)) < my_turn, 1, 0) for p in range(ns))

    small = [(st_hbm, st), (phi_hbm, phi), (so_hbm, so), (adj_hbm.at[0], adj), (inv_hbm, inv),
             (si_hbm, si), (vol_hbm, vol), (src_hbm.at[0], src)]
    copies = [pltpu.make_async_copy(a, b, local_sem.at[n]) for n, (a, b) in enumerate(small)]
    edge1 = pltpu.make_async_copy(jac_hbm.at[0, 1, :, :, nx - 1], jac.at[1, :, :, nx - 1], jac_sem.at[7])
    edge2 = pltpu.make_async_copy(jac_hbm.at[0, 2, :, :, 0], jac.at[2, :, :, 0], jac_sem.at[8])
    rest1 = pltpu.make_async_copy(jac_hbm.at[0, 1, :, :, 0:nx - 1], jac.at[1, :, :, 0:nx - 1], jac_sem.at[1])
    rest2 = pltpu.make_async_copy(jac_hbm.at[0, 2, :, :, 1:nx], jac.at[2, :, :, 1:nx], jac_sem.at[2])
    bulk = [pltpu.make_async_copy(jac_hbm.at[0, d], jac.at[d], jac_sem.at[d]) for d in (0, 3, 4, 5, 6)]
    for c in copies[:4] + [edge1, edge2] + copies[4:] + [rest1, rest2] + bulk:
        c.start()

    copies[0].wait()
    copies[1].wait()
    modes, stations = phi.shape
    for x in range(nx):
        where = jnp.broadcast_to(st[x:x + 1, :], (modes, nz))
        column = lax.rem(where, nz)
        taken = jnp.zeros((modes, nz), jnp.float32)
        for start in range(0, stations, nz):
            found = jnp.take_along_axis(phi[:, start:start + nz], column, axis=1, mode="promise_in_bounds")
            taken = jnp.where(where - column == start, found, taken)
        gmat[x] = taken

    copies[2].wait()
    copies[3].wait()
    col = jnp.zeros((modes, nz), jnp.float32)
    for x in range(nx):
        face = so[0, x:x + 1, :] * adj[0, x, 0:1, :]
        for j in range(1, nv):
            face = face + so[j, x:x + 1, :] * adj[j, x, 0:1, :]
        col = col + gmat[x] * face
    col = jnp.sum(col, axis=1, keepdims=True)
    diag = (lax.broadcasted_iota(jnp.int32, (modes, nz), 0)
            == lax.broadcasted_iota(jnp.int32, (modes, nz), 1))
    share = jnp.sum(jnp.where(diag, col, 0.0), axis=0, keepdims=True)
    row_out[...] = share
    row_in[sp] = share

    def product(d, j, x):
        total = jac[d, 0, j, x] * adj[0, x]
        for i in range(1, nv):
            total = total + jac[d, i, j, x] * adj[i, x]
        return total

    edge1.wait()
    edge2.wait()
    for side, d, x in ((0, 1, nx - 1), (1, 2, 0)):
        for j in range(nv):
            halo_out[side, j] = product(d, j, x)

    pl.semaphore_wait(barrier, ni - 1 + n_earlier)

    def to_block(peer):
        return pltpu.make_async_remote_copy(
            src_ref=row_out, dst_ref=row_in.at[sp],
            send_sem=m_send.at[peer], recv_sem=m_recv.at[sp],
            device_id={"space": peer}, device_id_type=MESH)

    earlier_blocks(lambda peer: send_signals(ready_space.at[sp], "space", peer))
    earlier_blocks(lambda peer: to_block(peer).start())

    def halo(side):
        peer = lax.rem(sp + (1 if side == 0 else ns - 1), ns)
        return peer, pltpu.make_async_remote_copy(
            src_ref=halo_out.at[side], dst_ref=halo_in.at[side],
            send_sem=h_send.at[side], recv_sem=h_recv.at[side],
            device_id={"space": peer}, device_id_type=MESH)

    for side in range(2):
        target, copy = halo(side)

        @pl.when(turn(target) < my_turn)
        def _():
            copy.start()

    def to_mixer(other, cc):
        x, y = spot(other)
        return pltpu.make_async_remote_copy(
            src_ref=adj.at[pl.ds(FIRST[cc], COUNT[cc]), x, pl.ds(y, 8), :],
            dst_ref=inbox.at[me, pl.ds(0, COUNT[cc])],
            send_sem=a_send.at[other * 2 + cc], recv_sem=a_recv.at[me],
            device_id={"inst": other * 2 + cc}, device_id_type=MESH)

    def others(act):
        @pl.loop(0, nc - 1)
        def _(k):
            chosen = lax.rem(chip + 1 + lax.rem(k + nc // 2 - 1, nc - 1), nc)
            act(chosen, 0)
            act(chosen, 1)

        for cc in range(2):
            @pl.when(core != cc)
            def _():
                act(chip, cc)

    others(lambda c, cc: to_mixer(c, cc).start())

    rest1.wait()
    rest2.wait()
    for c in bulk:
        c.wait()
    copies[7].wait()
    row = lax.broadcasted_iota(jnp.int32, (ny, nz), 0)
    lane = lax.broadcasted_iota(jnp.int32, (ny, nz), 1)

    def flux(j, carry):
        for x in range(nx):
            total = product(0, j, x) - src[j, x]
            if x > 0:
                total = total + product(1, j, x - 1)
            if x < nx - 1:
                total = total + product(2, j, x + 1)
            total = total + jnp.where(row == 0, 0.0, pltpu.roll(product(3, j, x), 1, 0))
            total = total + jnp.where(row == ny - 1, 0.0, pltpu.roll(product(4, j, x), ny - 1, 0))
            total = total + jnp.where(lane == 0, 0.0, pltpu.roll(product(5, j, x), 1, 1))
            total = total + jnp.where(lane == nz - 1, 0.0, pltpu.roll(product(6, j, x), nz - 1, 1))
            res[j, x] = total
        return carry

    lax.fori_loop(0, nv, flux, 0)

    def is_soon(peer):
        return turn(peer) - my_turn <= SOON

    def to_later(soon):
        def act(peer):
            @pl.when(is_soon(peer) if soon else jnp.logical_not(is_soon(peer)))
            def _():
                pl.semaphore_wait(ready_space.at[peer], 1)
                to_block(peer).start()

        later_blocks(act)
        for side in range(2):
            target, copy = halo(side)
            chosen = is_soon(target) if soon else jnp.logical_not(is_soon(target))

            @pl.when((turn(target) > my_turn) & chosen)
            def _():
                copy.start()

    to_later(True)

    my_x, my_y = spot(chip)
    for cc in range(2):
        @pl.when(core == cc)
        def _():
            inbox[me, 0:COUNT[cc]] = adj[FIRST[cc]:FIRST[cc] + COUNT[cc], my_x, pl.ds(my_y, 8), :]

            def arrival(other, oc):
                source = other * 2 + oc
                block = inbox.at[source, pl.ds(0, COUNT[cc])]
                return pltpu.make_async_remote_copy(
                    src_ref=block, dst_ref=block, send_sem=a_send.at[source], recv_sem=a_recv.at[source],
                    device_id={"inst": source}, device_id_type=MESH)

            others(lambda c, oc: arrival(c, oc).wait_recv())

    weight = time_weight(ni)
    half = ni // 2

    def mix(t, carry):
        a = [inbox[lax.rem(me + k, ni), t] for k in range(ni)]
        even = [a[k] + a[k + half] for k in range(half)]
        odd = [a[k] - a[k + half] for k in range(half)]
        for d in range(half):
            near = [float(weight[(k - d) % ni]) for k in range(half)]
            far = [float(weight[(k - d + half) % ni]) for k in range(half)]
            plus = sum(even[k] * np.float32(0.5 * (near[k] + far[k])) for k in range(half))
            minus = sum(odd[k] * np.float32(0.5 * (near[k] - far[k])) for k in range(half))
            outbox[lax.rem(me + d, ni), t] = plus + minus
            outbox[lax.rem(me + d + half, ni), t] = plus - minus
        return carry

    lax.fori_loop(0, 3 - core, mix, 0)

    def back_home(cc, other, oc):
        peer = other * 2 + oc
        return pltpu.make_async_remote_copy(
            src_ref=outbox.at[peer, pl.ds(0, COUNT[cc])],
            dst_ref=mixed.at[pl.ds(FIRST[cc], COUNT[cc]), my_x, pl.ds(my_y, 8), :],
            send_sem=b_send.at[peer], recv_sem=b_recv.at[me],
            device_id={"inst": peer}, device_id_type=MESH)

    for cc in range(2):
        @pl.when(core == cc)
        def _():
            others(lambda c, oc: back_home(cc, c, oc).start())
            mixed[FIRST[cc]:FIRST[cc] + COUNT[cc], my_x, pl.ds(my_y, 8), :] = outbox[me, 0:COUNT[cc]]

    to_later(False)
    others(lambda c, cc: to_mixer(c, cc).wait_send())

    def home_arrival(other, oc):
        x, y = spot(other)
        source = other * 2 + oc
        block = mixed.at[pl.ds(FIRST[oc], COUNT[oc]), x, pl.ds(y, 8), :]
        return pltpu.make_async_remote_copy(
            src_ref=block, dst_ref=block, send_sem=b_send.at[source], recv_sem=b_recv.at[source],
            device_id={"inst": source}, device_id_type=MESH)

    copies[4].wait()
    copies[5].wait()
    copies[6].wait()
    halo(0)[1].wait_recv()
    halo(1)[1].wait_recv()
    for j in range(nv):
        res[j, 0] = res[j, 0] + halo_in[0, j]
        res[j, nx - 1] = res[j, nx - 1] + halo_in[1, j]

    def each_block(act):
        @pl.loop(0, sp)
        def _(peer):
            act(peer)

        @pl.loop(sp + 1, ns)
        def _(peer):
            act(peer)

    def row_arrival(source):
        return pltpu.make_async_remote_copy(
            src_ref=row_out, dst_ref=row_in.at[source], send_sem=m_send.at[source], recv_sem=m_recv.at[source],
            device_id={"space": source}, device_id_type=MESH)

    each_block(lambda peer: row_arrival(peer).wait_recv())
    sums = jnp.sum(row_in[...], axis=0)
    coords = sums[:, 0:modes] * inv[...]
    modal[...] = coords
    square = (lax.broadcasted_iota(jnp.int32, (modes, modes), 0)
              == lax.broadcasted_iota(jnp.int32, (modes, modes), 1))
    column = jnp.sum(jnp.where(square, coords, 0.0), axis=1, keepdims=True)
    for x in range(nx):
        back = jnp.sum(gmat[x] * column, axis=0, keepdims=True)
        for j in range(nv):
            res[j, x, 0:1, :] = res[j, x, 0:1, :] + si[j, x:x + 1, :] * back

    halo(0)[1].wait_send()
    halo(1)[1].wait_send()
    each_block(lambda peer: to_block(peer).wait_send())
    for cc in range(2):
        @pl.when(core == cc)
        def _():
            others(lambda c, oc: back_home(cc, c, oc).wait_send())

    others(lambda c, oc: home_arrival(c, oc).wait_recv())
    for j in range(nv):
        for x in range(nx):
            res[j, x] = res[j, x] + vol[x] * mixed[j, x]


def put_out(res, modal, res_hbm, modal_hbm, sem):
    first = pltpu.make_async_copy(res, res_hbm.at[0], sem.at[0])
    second = pltpu.make_async_copy(modal, modal_hbm, sem.at[1])
    first.start()
    second.start()
    first.wait()
    second.wait()


def solution(mesh):
    ni, ns = mesh.shape["inst"], mesh.shape["space"]
    placed = (
        P("inst", None, "space", None, None),
        P("inst", None, None, None, "space", None, None),
        P("space", None, None),
        P("inst", None, "space", None, None),
        P(None, "space", None),
        P(None, "space", None),
        P("space", None),
        P(),
        P(),
    )

    def body(adjoint, jacobian, volume, source, surface_out, surface_in, station, phi, inv_stiff):
        _, nv, nx, ny, nz = adjoint.shape
        modes, stations = phi.shape
        inv_row = inv_stiff.reshape(1, modes)
        f32 = jnp.float32
        operands = (adjoint, jacobian, volume, source, surface_out, surface_in, station, phi, inv_row)
        vmem = pltpu.VMEM
        sem = pltpu.SemaphoreType.DMA
        residual, modal = pl.pallas_call(
            functools.partial(kernel, ni, ns),
            out_shape=(jax.ShapeDtypeStruct((nv, nx, ny, nz), f32), jax.ShapeDtypeStruct((1, modes), f32)),
            in_specs=[pl.BlockSpec(memory_space=pltpu.HBM)] * len(operands),
            out_specs=(pl.BlockSpec(memory_space=pltpu.VMEM), pl.BlockSpec(memory_space=pltpu.VMEM)),
            scratch_shapes=[
                vmem((nv, nx, ny, nz), f32), vmem(jacobian.shape[1:], f32), vmem((nx, ny, nz), f32),
                vmem((nv, nx, ny, nz), f32), vmem((nv, nx, nz), f32), vmem((nv, nx, nz), f32),
                vmem((nx, nz), jnp.int32), vmem((modes, stations), f32), vmem((1, modes), f32),
                vmem((ni, 3, 8, nz), f32), vmem((ni, 3, 8, nz), f32), vmem((nv, nx, ny, nz), f32),
                vmem((2, nv, ny, nz), f32), vmem((2, nv, ny, nz), f32), vmem((nx, modes, nz), f32),
                vmem((1, nz), f32), vmem((ns, 1, nz), f32),
                sem((8,)), sem((9,)), sem((ni,)), sem((ni,)), sem((ni,)), sem((ni,)),
                sem((2,)), sem((2,)), sem((ns,)), sem((ns,)),
                pltpu.SemaphoreType.REGULAR((ns,)),
            ],
            compiler_params=pltpu.CompilerParams(
                collective_id=0, has_side_effects=True, vmem_limit_bytes=24 << 20),
        )(*[pltpu.with_memory_space_constraint(x, pltpu.HBM) for x in operands])
        return pl.pallas_call(
            put_out,
            out_shape=(jax.ShapeDtypeStruct((1, nv, nx, ny, nz), f32), jax.ShapeDtypeStruct((1, modes), f32)),
            in_specs=[pl.BlockSpec(memory_space=vmem)] * 2,
            out_specs=(pl.BlockSpec(memory_space=pltpu.HBM), pl.BlockSpec(memory_space=pltpu.HBM)),
            scratch_shapes=[sem((2,))],
        )(*[pltpu.with_memory_space_constraint(x, vmem) for x in (residual, modal)])

    return jax.shard_map(
        body, mesh=mesh, in_specs=placed,
        out_specs=(P("inst", None, "space", None, None), P("inst", None)), check_vma=False)
```

```python
import functools

import numpy as np
import jax
import jax.numpy as jnp
from jax import lax
from jax.experimental import pallas as pl
from jax.experimental.pallas import tpu as pltpu
from jax.sharding import PartitionSpec as P

MESH = pl.DeviceIdType.MESH
FIRST = (0, 3)
COUNT = (3, 2)


def time_weight(count):
    k = np.arange(count)
    angle = np.pi * k / count
    parity = 1.0 - 2.0 * (k % 2)
    safe = np.where(k != 0, np.sin(angle), 1.0)
    first = np.where(k != 0, 0.5 * parity * np.cos(angle) / safe, 0.0)
    second = np.where(k != 0, -0.5 * parity / (safe * safe), -(count * count + 2) / 12.0)
    return first - 0.25 * second


SOON = 20
LATE = 40


def turn(block):
    z, y = lax.div(block, 2), lax.rem(block, 2)
    return jnp.where(z < 4, 10 * z, 51 + z) + 16 * y


def kernel(
    ni, ns,
    adj_hbm, jac_hbm, vol_hbm, src_hbm, so_hbm, si_hbm, st_hbm, phi_hbm, inv_hbm,
    res, modal,
    adj, jac, vol, src, so, si, st, phi, inv,
    inbox, outbox, mixed, gauge, halo_out, halo_in, gmat, row_out, row_in,
    local_sem, jac_sem, a_send, a_recv, b_send, b_recv, h_send, h_recv, m_send, m_recv,
    ready_space,
):
    me = lax.axis_index("inst")
    sp = lax.axis_index("space")
    core = lax.rem(me, 2)
    chip = lax.div(me, 2)
    nc = ni // 2
    nv, nx, ny, nz = adj.shape
    halves = ny // 8

    def spot(c):
        return lax.div(c, halves), pl.multiple_of(lax.rem(c, halves) * 8, 8)

    def send_signals(semaphore, axis, peer):
        pl.semaphore_signal(semaphore, inc=1, device_id={axis: peer}, device_id_type=MESH)

    barrier = pltpu.get_barrier_semaphore()

    @pl.loop(1, ni)
    def _(k):
        send_signals(barrier, "inst", lax.rem(me + k, ni))

    my_turn = turn(sp)

    def later_blocks(act):
        @pl.loop(0, ns)
        def _(k):
            far = k - ns // 2
            peer = jnp.where(far < 0, k, ns // 2 + lax.rem(2 * far + ns, ns // 2) + lax.div(far, ns // 4))

            @pl.when(turn(peer) > my_turn)
            def _():
                act(peer)

    later_blocks(lambda peer: send_signals(barrier, "space", peer))
    n_earlier = sum(jnp.where(turn(jnp.int32(p)) < my_turn, 1, 0) for p in range(ns))

    small = [(st_hbm, st), (phi_hbm, phi), (so_hbm, so), (adj_hbm.at[0], adj), (inv_hbm, inv),
             (si_hbm, si), (vol_hbm, vol), (src_hbm.at[0], src)]
    copies = [pltpu.make_async_copy(a, b, local_sem.at[n]) for n, (a, b) in enumerate(small)]
    edge1 = pltpu.make_async_copy(jac_hbm.at[0, 1, :, :, nx - 1], jac.at[1, :, :, nx - 1], jac_sem.at[7])
    edge2 = pltpu.make_async_copy(jac_hbm.at[0, 2, :, :, 0], jac.at[2, :, :, 0], jac_sem.at[8])
    rest1 = pltpu.make_async_copy(jac_hbm.at[0, 1, :, :, 0:nx - 1], jac.at[1, :, :, 0:nx - 1], jac_sem.at[1])
    rest2 = pltpu.make_async_copy(jac_hbm.at[0, 2, :, :, 1:nx], jac.at[2, :, :, 1:nx], jac_sem.at[2])
    bulk = [pltpu.make_async_copy(jac_hbm.at[0, d], jac.at[d], jac_sem.at[d]) for d in (0, 3, 4, 5, 6)]
    for c in copies[:4] + [edge1, edge2] + copies[4:] + [rest1, rest2] + bulk:
        c.start()

    copies[0].wait()
    copies[1].wait()
    modes, stations = phi.shape
    for x in range(nx):
        where = jnp.broadcast_to(st[x:x + 1, :], (modes, nz))
        column = lax.rem(where, nz)
        taken = jnp.zeros((modes, nz), jnp.float32)
        for start in range(0, stations, nz):
            found = jnp.take_along_axis(phi[:, start:start + nz], column, axis=1, mode="promise_in_bounds")
            taken = jnp.where(where - column == start, found, taken)
        gmat[x] = taken

    copies[2].wait()
    copies[3].wait()
    col = jnp.zeros((modes, nz), jnp.float32)
    for x in range(nx):
        face = so[0, x:x + 1, :] * adj[0, x, 0:1, :]
        for j in range(1, nv):
            face = face + so[j, x:x + 1, :] * adj[j, x, 0:1, :]
        col = col + gmat[x] * face
    col = jnp.sum(col, axis=1, keepdims=True)
    diag = (lax.broadcasted_iota(jnp.int32, (modes, nz), 0)
            == lax.broadcasted_iota(jnp.int32, (modes, nz), 1))
    share = jnp.sum(jnp.where(diag, col, 0.0), axis=0, keepdims=True)
    row_out[...] = share
    row_in[sp] = share

    def product(d, j, x):
        total = jac[d, 0, j, x] * adj[0, x]
        for i in range(1, nv):
            total = total + jac[d, i, j, x] * adj[i, x]
        return total

    edge1.wait()
    edge2.wait()
    for side, d, x in ((0, 1, nx - 1), (1, 2, 0)):
        for j in range(nv):
            halo_out[side, j] = product(d, j, x)

    pl.semaphore_wait(barrier, ni - 1 + n_earlier)

    def to_block(peer):
        return pltpu.make_async_remote_copy(
            src_ref=row_out, dst_ref=row_in.at[sp],
            send_sem=m_send, recv_sem=m_recv,
            device_id={"space": peer}, device_id_type=MESH)

    for peer in range(ns):
        @pl.when(turn(jnp.int32(peer)) < my_turn)
        def _():
            to_block(peer).start()
            send_signals(ready_space.at[sp], "space", peer)


    def halo(side):
        peer = lax.rem(sp + (1 if side == 0 else ns - 1), ns)
        return peer, pltpu.make_async_remote_copy(
            src_ref=halo_out.at[side], dst_ref=halo_in.at[side],
            send_sem=h_send.at[side], recv_sem=h_recv.at[side],
            device_id={"space": peer}, device_id_type=MESH)

    for side in range(2):
        target, copy = halo(side)

        @pl.when(turn(target) < my_turn)
        def _():
            copy.start()

    def to_mixer(other, cc):
        x, y = spot(other)
        return pltpu.make_async_remote_copy(
            src_ref=adj.at[pl.ds(FIRST[cc], COUNT[cc]), x, pl.ds(y, 8), :],
            dst_ref=inbox.at[me, pl.ds(0, COUNT[cc])],
            send_sem=a_send, recv_sem=a_recv,
            device_id={"inst": other * 2 + cc}, device_id_type=MESH)

    def others(act):
        @pl.loop(0, nc - 1)
        def _(k):
            chosen = lax.rem(chip + 1 + lax.rem(k + nc // 2 - 1, nc - 1), nc)
            act(chosen, 0)
            act(chosen, 1)

        for cc in range(2):
            @pl.when(core != cc)
            def _():
                act(chip, cc)

    others(lambda c, cc: to_mixer(c, cc).start())

    rest1.wait()
    rest2.wait()
    for c in bulk:
        c.wait()
    copies[7].wait()
    row = lax.broadcasted_iota(jnp.int32, (ny, nz), 0)
    lane = lax.broadcasted_iota(jnp.int32, (ny, nz), 1)

    def flux(j, carry):
        for x in range(nx):
            total = product(0, j, x) - src[j, x]
            if x > 0:
                total = total + product(1, j, x - 1)
            if x < nx - 1:
                total = total + product(2, j, x + 1)
            total = total + jnp.where(row == 0, 0.0, pltpu.roll(product(3, j, x), 1, 0))
            total = total + jnp.where(row == ny - 1, 0.0, pltpu.roll(product(4, j, x), ny - 1, 0))
            total = total + jnp.where(lane == 0, 0.0, pltpu.roll(product(5, j, x), 1, 1))
            total = total + jnp.where(lane == nz - 1, 0.0, pltpu.roll(product(6, j, x), nz - 1, 1))
            res[j, x] = total
        return carry

    lax.fori_loop(0, nv, flux, 0)

    def is_soon(peer):
        return turn(peer) - my_turn <= SOON

    def to_later(soon):
        def act(peer):
            @pl.when(is_soon(peer) if soon else jnp.logical_not(is_soon(peer)))
            def _():
                pl.semaphore_wait(ready_space.at[peer], 1)
                to_block(peer).start()

        later_blocks(act)
        for side in range(2):
            target, copy = halo(side)
            chosen = is_soon(target) if soon else jnp.logical_not(is_soon(target))

            @pl.when((turn(target) > my_turn) & chosen)
            def _():
                copy.start()

    to_later(True)

    def arrived(block, semaphore):
        pltpu.make_async_copy(block, block, semaphore).wait()

    my_x, my_y = spot(chip)
    for cc in range(2):
        @pl.when(core == cc)
        def _():
            inbox[me, 0:COUNT[cc]] = adj[FIRST[cc]:FIRST[cc] + COUNT[cc], my_x, pl.ds(my_y, 8), :]

            arrived(inbox.at[pl.ds(0, ni - 1), pl.ds(0, COUNT[cc])], a_recv)

    weight = time_weight(ni)
    half = ni // 2

    def mix(t, carry):
        a = [inbox[lax.rem(me + k, ni), t] for k in range(ni)]
        even = [a[k] + a[k + half] for k in range(half)]
        odd = [a[k] - a[k + half] for k in range(half)]
        for d in range(half):
            near = [float(weight[(k - d) % ni]) for k in range(half)]
            far = [float(weight[(k - d + half) % ni]) for k in range(half)]
            plus = sum(even[k] * np.float32(0.5 * (near[k] + far[k])) for k in range(half))
            minus = sum(odd[k] * np.float32(0.5 * (near[k] - far[k])) for k in range(half))
            outbox[lax.rem(me + d, ni), t] = plus + minus
            outbox[lax.rem(me + d + half, ni), t] = plus - minus
        return carry

    lax.fori_loop(0, 3 - core, mix, 0)

    def back_home(cc, other, oc):
        peer = other * 2 + oc
        return pltpu.make_async_remote_copy(
            src_ref=outbox.at[peer, pl.ds(0, COUNT[cc])],
            dst_ref=mixed.at[pl.ds(FIRST[cc], COUNT[cc]), my_x, pl.ds(my_y, 8), :],
            send_sem=b_send, recv_sem=b_recv,
            device_id={"inst": peer}, device_id_type=MESH)

    for cc in range(2):
        @pl.when(core == cc)
        def _():
            others(lambda c, oc: back_home(cc, c, oc).start())
            mixed[FIRST[cc]:FIRST[cc] + COUNT[cc], my_x, pl.ds(my_y, 8), :] = outbox[me, 0:COUNT[cc]]

    to_later(False)
    for cc in range(2):
        @pl.when(core == cc)
        def _():
            arrived(gauge.at[pl.ds(0, nv * nx * halves - COUNT[cc])], a_send)

    arrived(row_in.at[pl.ds(0, ns - 1)], m_send)
    copies[4].wait()
    copies[5].wait()
    copies[6].wait()

    def add_mixed():
        for cc in range(2):
            @pl.when(core == cc)
            def _():
                arrived(gauge.at[pl.ds(0, nv * nx * halves - COUNT[cc])], b_recv)

        for j in range(nv):
            for x in range(nx):
                res[j, x] = res[j, x] + vol[x] * mixed[j, x]

    def add_halo():
        halo(0)[1].wait_recv()
        halo(1)[1].wait_recv()
        for j in range(nv):
            res[j, 0] = res[j, 0] + halo_in[0, j]
            res[j, nx - 1] = res[j, nx - 1] + halo_in[1, j]

    def add_back():
        arrived(row_in.at[pl.ds(0, ns - 1)], m_recv)
        sums = jnp.sum(row_in[...], axis=0)
        coords = sums[:, 0:modes] * inv[...]
        modal[...] = coords
        square = (lax.broadcasted_iota(jnp.int32, (modes, modes), 0)
                  == lax.broadcasted_iota(jnp.int32, (modes, modes), 1))
        column = jnp.sum(jnp.where(square, coords, 0.0), axis=1, keepdims=True)
        for x in range(nx):
            back = jnp.sum(gmat[x] * column, axis=0, keepdims=True)
            for j in range(nv):
                res[j, x, 0:1, :] = res[j, x, 0:1, :] + si[j, x:x + 1, :] * back

    @pl.when(my_turn < LATE)
    def _():
        add_mixed()
        add_halo()
        add_back()

    @pl.when(my_turn >= LATE)
    def _():
        add_back()
        add_halo()
        add_mixed()

    halo(0)[1].wait_send()
    halo(1)[1].wait_send()
    for cc in range(2):
        @pl.when(core == cc)
        def _():
            arrived(inbox.at[pl.ds(0, ni - 1), pl.ds(0, COUNT[cc])], b_send)


def put_out(res, modal, res_hbm, modal_hbm, sem):
    first = pltpu.make_async_copy(res, res_hbm.at[0], sem.at[0])
    second = pltpu.make_async_copy(modal, modal_hbm, sem.at[1])
    first.start()
    second.start()
    first.wait()
    second.wait()


def solution(mesh):
    ni, ns = mesh.shape["inst"], mesh.shape["space"]
    placed = (
        P("inst", None, "space", None, None),
        P("inst", None, None, None, "space", None, None),
        P("space", None, None),
        P("inst", None, "space", None, None),
        P(None, "space", None),
        P(None, "space", None),
        P("space", None),
        P(),
        P(),
    )

    def body(adjoint, jacobian, volume, source, surface_out, surface_in, station, phi, inv_stiff):
        _, nv, nx, ny, nz = adjoint.shape
        modes, stations = phi.shape
        inv_row = inv_stiff.reshape(1, modes)
        f32 = jnp.float32
        operands = (adjoint, jacobian, volume, source, surface_out, surface_in, station, phi, inv_row)
        vmem = pltpu.VMEM
        sem = pltpu.SemaphoreType.DMA
        residual, modal = pl.pallas_call(
            functools.partial(kernel, ni, ns),
            out_shape=(jax.ShapeDtypeStruct((nv, nx, ny, nz), f32), jax.ShapeDtypeStruct((1, modes), f32)),
            in_specs=[pl.BlockSpec(memory_space=pltpu.HBM)] * len(operands),
            out_specs=(pl.BlockSpec(memory_space=pltpu.VMEM), pl.BlockSpec(memory_space=pltpu.VMEM)),
            scratch_shapes=[
                vmem((nv, nx, ny, nz), f32), vmem(jacobian.shape[1:], f32), vmem((nx, ny, nz), f32),
                vmem((nv, nx, ny, nz), f32), vmem((nv, nx, nz), f32), vmem((nv, nx, nz), f32),
                vmem((nx, nz), jnp.int32), vmem((modes, stations), f32), vmem((1, modes), f32),
                vmem((ni, 3, 8, nz), f32), vmem((ni, 3, 8, nz), f32), vmem((nv, nx, ny, nz), f32),
                vmem((nv * nx * ny // 8, 8, nz), f32),
                vmem((2, nv, ny, nz), f32), vmem((2, nv, ny, nz), f32), vmem((nx, modes, nz), f32),
                vmem((1, nz), f32), vmem((ns, 1, nz), f32),
                sem((8,)), sem((9,)), sem, sem, sem, sem, sem((2,)), sem((2,)), sem, sem,
                pltpu.SemaphoreType.REGULAR((ns,)),
            ],
            compiler_params=pltpu.CompilerParams(
                collective_id=0, has_side_effects=True, vmem_limit_bytes=24 << 20),
        )(*[pltpu.with_memory_space_constraint(x, pltpu.HBM) for x in operands])
        return pl.pallas_call(
            put_out,
            out_shape=(jax.ShapeDtypeStruct((1, nv, nx, ny, nz), f32), jax.ShapeDtypeStruct((1, modes), f32)),
            in_specs=[pl.BlockSpec(memory_space=vmem)] * 2,
            out_specs=(pl.BlockSpec(memory_space=pltpu.HBM), pl.BlockSpec(memory_space=pltpu.HBM)),
            scratch_shapes=[sem((2,))],
        )(*[pltpu.with_memory_space_constraint(x, vmem) for x in (residual, modal)])

    return jax.shard_map(
        body, mesh=mesh, in_specs=placed,
        out_specs=(P("inst", None, "space", None, None), P("inst", None)), check_vma=False)
```

```python
import functools

import numpy as np
import jax
import jax.numpy as jnp
from jax import lax
from jax.experimental import pallas as pl
from jax.experimental.pallas import tpu as pltpu
from jax.sharding import PartitionSpec as P

MESH = pl.DeviceIdType.MESH
FIRST = (0, 3)
COUNT = (3, 2)


def time_weight(count):
    k = np.arange(count)
    angle = np.pi * k / count
    parity = 1.0 - 2.0 * (k % 2)
    safe = np.where(k != 0, np.sin(angle), 1.0)
    first = np.where(k != 0, 0.5 * parity * np.cos(angle) / safe, 0.0)
    second = np.where(k != 0, -0.5 * parity / (safe * safe), -(count * count + 2) / 12.0)
    return first - 0.25 * second


LATE = 40


def turn(block):
    z, y = lax.div(block, 2), lax.rem(block, 2)
    return jnp.where(z < 4, 10 * z, 51 + z) + 16 * y


def turn_of(block):
    z, y = divmod(block, 2)
    return (10 * z if z < 4 else 51 + z) + 16 * y


def kernel(
    ni, ns,
    adj_hbm, jac_hbm, vol_hbm, src_hbm, so_hbm, si_hbm, st_hbm, phi_hbm, inv_hbm,
    res, modal,
    adj, jac, vol, src, so, si, st, phi, inv,
    inbox, outbox, mixed, gauge, halo_out, halo_in, gmat, row_out, row_in,
    local_sem, jac_sem, a_send, a_recv, b_send, b_recv, h_send, h_recv, m_send, m_recv,
    ready_space,
):
    me = lax.axis_index("inst")
    sp = lax.axis_index("space")
    core = lax.rem(me, 2)
    chip = lax.div(me, 2)
    nc = ni // 2
    nv, nx, ny, nz = adj.shape
    halves = ny // 8

    far_first = sorted(range(1, nc), key=lambda k: abs(k - nc // 2))

    def spot(c):
        return lax.div(c, halves), pl.multiple_of(lax.rem(c, halves) * 8, 8)

    def send_signals(semaphore, axis, peer):
        pl.semaphore_signal(semaphore, inc=1, device_id={axis: peer}, device_id_type=MESH)

    barrier = pltpu.get_barrier_semaphore()

    for k in sorted(range(1, ni), key=lambda k: abs(k - ni // 2)):
        send_signals(barrier, "inst", lax.rem(me + k, ni))

    my_turn = turn(sp)

    def later_blocks(act):
        for peer in sorted(range(ns), key=turn_of):
            @pl.when(turn_of(peer) > my_turn)
            def _():
                act(peer)

    later_blocks(lambda peer: send_signals(barrier, "space", peer))
    n_earlier = sum(jnp.where(turn_of(p) < my_turn, 1, 0) for p in range(ns))

    small = [(st_hbm, st), (phi_hbm, phi), (so_hbm, so), (adj_hbm.at[0], adj), (inv_hbm, inv),
             (si_hbm, si), (vol_hbm, vol), (src_hbm.at[0], src)]
    copies = [pltpu.make_async_copy(a, b, local_sem.at[n]) for n, (a, b) in enumerate(small)]
    edge1 = pltpu.make_async_copy(jac_hbm.at[0, 1, :, :, nx - 1], jac.at[1, :, :, nx - 1], jac_sem.at[7])
    edge2 = pltpu.make_async_copy(jac_hbm.at[0, 2, :, :, 0], jac.at[2, :, :, 0], jac_sem.at[8])
    rest1 = pltpu.make_async_copy(jac_hbm.at[0, 1, :, :, 0:nx - 1], jac.at[1, :, :, 0:nx - 1], jac_sem.at[1])
    rest2 = pltpu.make_async_copy(jac_hbm.at[0, 2, :, :, 1:nx], jac.at[2, :, :, 1:nx], jac_sem.at[2])
    bulk = [pltpu.make_async_copy(jac_hbm.at[0, d], jac.at[d], jac_sem.at[d]) for d in (0, 3, 4, 5, 6)]
    for c in copies[:4] + [edge1, edge2] + copies[4:] + [rest1, rest2] + bulk:
        c.start()

    copies[0].wait()
    copies[1].wait()
    modes, stations = phi.shape
    for x in range(nx):
        where = jnp.broadcast_to(st[x:x + 1, :], (modes, nz))
        column = lax.rem(where, nz)
        taken = jnp.zeros((modes, nz), jnp.float32)
        for start in range(0, stations, nz):
            found = jnp.take_along_axis(phi[:, start:start + nz], column, axis=1, mode="promise_in_bounds")
            taken = jnp.where(where - column == start, found, taken)
        gmat[x] = taken

    copies[2].wait()
    copies[3].wait()
    col = jnp.zeros((modes, nz), jnp.float32)
    for x in range(nx):
        face = so[0, x:x + 1, :] * adj[0, x, 0:1, :]
        for j in range(1, nv):
            face = face + so[j, x:x + 1, :] * adj[j, x, 0:1, :]
        col = col + gmat[x] * face
    col = jnp.sum(col, axis=1, keepdims=True)
    diag = (lax.broadcasted_iota(jnp.int32, (modes, nz), 0)
            == lax.broadcasted_iota(jnp.int32, (modes, nz), 1))
    share = jnp.sum(jnp.where(diag, col, 0.0), axis=0, keepdims=True)
    row_out[...] = share
    row_in[sp] = share

    def product(d, j, x):
        total = jac[d, 0, j, x] * adj[0, x]
        for i in range(1, nv):
            total = total + jac[d, i, j, x] * adj[i, x]
        return total

    edge1.wait()
    edge2.wait()
    for side, d, x in ((0, 1, nx - 1), (1, 2, 0)):
        for j in range(nv):
            halo_out[side, j] = product(d, j, x)

    pl.semaphore_wait(barrier, ni - 1 + n_earlier)

    def to_block(peer):
        return pltpu.make_async_remote_copy(
            src_ref=row_out, dst_ref=row_in.at[sp],
            send_sem=m_send, recv_sem=m_recv,
            device_id={"space": peer}, device_id_type=MESH)

    for peer in sorted(range(ns), key=turn_of):
        @pl.when(turn_of(peer) < my_turn)
        def _():
            to_block(peer).start()
            send_signals(ready_space.at[sp], "space", peer)


    def halo(side):
        peer = lax.rem(sp + (1 if side == 0 else ns - 1), ns)
        return peer, pltpu.make_async_remote_copy(
            src_ref=halo_out.at[side], dst_ref=halo_in.at[side],
            send_sem=h_send.at[side], recv_sem=h_recv.at[side],
            device_id={"space": peer}, device_id_type=MESH)

    for side in range(2):
        target, copy = halo(side)

        @pl.when(turn(target) < my_turn)
        def _():
            copy.start()

    def to_mixer(other, cc):
        x, y = spot(other)
        return pltpu.make_async_remote_copy(
            src_ref=adj.at[pl.ds(FIRST[cc], COUNT[cc]), x, pl.ds(y, 8), :],
            dst_ref=inbox.at[me, pl.ds(0, COUNT[cc])],
            send_sem=a_send, recv_sem=a_recv,
            device_id={"inst": other * 2 + cc}, device_id_type=MESH)

    def others(act):
        for k in far_first:
            chosen = lax.rem(chip + k, nc)
            act(chosen, 0)
            act(chosen, 1)

        for cc in range(2):
            @pl.when(core != cc)
            def _():
                act(chip, cc)

    others(lambda c, cc: to_mixer(c, cc).start())

    rest1.wait()
    rest2.wait()
    for c in bulk:
        c.wait()
    copies[7].wait()
    row = lax.broadcasted_iota(jnp.int32, (ny, nz), 0)
    lane = lax.broadcasted_iota(jnp.int32, (ny, nz), 1)

    def flux(j, carry):
        for x in range(nx):
            total = product(0, j, x) - src[j, x]
            if x > 0:
                total = total + product(1, j, x - 1)
            if x < nx - 1:
                total = total + product(2, j, x + 1)
            total = total + jnp.where(row == 0, 0.0, pltpu.roll(product(3, j, x), 1, 0))
            total = total + jnp.where(row == ny - 1, 0.0, pltpu.roll(product(4, j, x), ny - 1, 0))
            total = total + jnp.where(lane == 0, 0.0, pltpu.roll(product(5, j, x), 1, 1))
            total = total + jnp.where(lane == nz - 1, 0.0, pltpu.roll(product(6, j, x), nz - 1, 1))
            res[j, x] = total
        return carry

    lax.fori_loop(0, nv, flux, 0)

    def is_near(peer):
        return jnp.where(peer > sp, peer - sp, sp - peer) == 1

    def to_later(near):
        def act(peer):
            @pl.when(is_near(peer) if near else jnp.logical_not(is_near(peer)))
            def _():
                pl.semaphore_wait(ready_space.at[peer], 1)
                to_block(peer).start()

        later_blocks(act)
        for side in range(2):
            target, copy = halo(side)
            chosen = is_near(target) if near else jnp.logical_not(is_near(target))

            @pl.when((turn(target) > my_turn) & chosen)
            def _():
                copy.start()

    to_later(True)

    def arrived(block, semaphore):
        pltpu.make_async_copy(block, block, semaphore).wait()

    my_x, my_y = spot(chip)
    for cc in range(2):
        @pl.when(core == cc)
        def _():
            inbox[me, 0:COUNT[cc]] = adj[FIRST[cc]:FIRST[cc] + COUNT[cc], my_x, pl.ds(my_y, 8), :]

            arrived(inbox.at[pl.ds(0, ni - 1), pl.ds(0, COUNT[cc])], a_recv)

    weight = time_weight(ni)
    half = ni // 2

    def home(cc, d):
        peer = lax.rem(me + d, ni)
        return pltpu.make_async_remote_copy(
            src_ref=outbox.at[peer, pl.ds(0, COUNT[cc])],
            dst_ref=mixed.at[pl.ds(FIRST[cc], COUNT[cc]), my_x, pl.ds(my_y, 8), :],
            send_sem=b_send, recv_sem=b_recv,
            device_id={"inst": peer}, device_id_type=MESH)

    def mix(cc):
        n = COUNT[cc]
        a = [inbox[lax.rem(me + k, ni), 0:n] for k in range(ni)]
        even = [a[k] + a[k + half] for k in range(half)]
        odd = [a[k] - a[k + half] for k in range(half)]
        for d in sorted(range(half), key=lambda d: d == 0):
            near = [float(weight[(k - d) % ni]) for k in range(half)]
            far = [float(weight[(k - d + half) % ni]) for k in range(half)]
            plus = sum(even[k] * np.float32(0.5 * (near[k] + far[k])) for k in range(half))
            minus = sum(odd[k] * np.float32(0.5 * (near[k] - far[k])) for k in range(half))
            outbox[lax.rem(me + d + half, ni), 0:n] = plus - minus
            home(cc, d + half).start()
            if d:
                outbox[lax.rem(me + d, ni), 0:n] = plus + minus
                home(cc, d).start()
            else:
                mixed[FIRST[cc]:FIRST[cc] + n, my_x, pl.ds(my_y, 8), :] = plus + minus

    for cc in range(2):
        @pl.when(core == cc)
        def _():
            mix(cc)

    to_later(False)
    for cc in range(2):
        @pl.when(core == cc)
        def _():
            arrived(gauge.at[pl.ds(0, nv * nx * halves - COUNT[cc])], a_send)

    arrived(row_in.at[pl.ds(0, ns - 1)], m_send)
    copies[4].wait()
    copies[5].wait()
    copies[6].wait()

    def add_mixed():
        for cc in range(2):
            @pl.when(core == cc)
            def _():
                arrived(gauge.at[pl.ds(0, nv * nx * halves - COUNT[cc])], b_recv)

        for j in range(nv):
            for x in range(nx):
                res[j, x] = res[j, x] + vol[x] * mixed[j, x]

    def add_halo():
        halo(0)[1].wait_recv()
        halo(1)[1].wait_recv()
        for j in range(nv):
            res[j, 0] = res[j, 0] + halo_in[0, j]
            res[j, nx - 1] = res[j, nx - 1] + halo_in[1, j]

    def add_back():
        arrived(row_in.at[pl.ds(0, ns - 1)], m_recv)
        sums = jnp.sum(row_in[...], axis=0)
        coords = sums[:, 0:modes] * inv[...]
        modal[...] = coords
        square = (lax.broadcasted_iota(jnp.int32, (modes, modes), 0)
                  == lax.broadcasted_iota(jnp.int32, (modes, modes), 1))
        column = jnp.sum(jnp.where(square, coords, 0.0), axis=1, keepdims=True)
        for x in range(nx):
            back = jnp.sum(gmat[x] * column, axis=0, keepdims=True)
            for j in range(nv):
                res[j, x, 0:1, :] = res[j, x, 0:1, :] + si[j, x:x + 1, :] * back

    @pl.when(my_turn < LATE)
    def _():
        add_mixed()
        add_halo()
        add_back()

    @pl.when(my_turn >= LATE)
    def _():
        add_back()
        add_halo()
        add_mixed()

    halo(0)[1].wait_send()
    halo(1)[1].wait_send()
    for cc in range(2):
        @pl.when(core == cc)
        def _():
            arrived(inbox.at[pl.ds(0, ni - 1), pl.ds(0, COUNT[cc])], b_send)


def put_out(res, modal, res_hbm, modal_hbm, sem):
    first = pltpu.make_async_copy(res, res_hbm.at[0], sem.at[0])
    second = pltpu.make_async_copy(modal, modal_hbm, sem.at[1])
    first.start()
    second.start()
    first.wait()
    second.wait()


def solution(mesh):
    ni, ns = mesh.shape["inst"], mesh.shape["space"]
    placed = (
        P("inst", None, "space", None, None),
        P("inst", None, None, None, "space", None, None),
        P("space", None, None),
        P("inst", None, "space", None, None),
        P(None, "space", None),
        P(None, "space", None),
        P("space", None),
        P(),
        P(),
    )

    def body(adjoint, jacobian, volume, source, surface_out, surface_in, station, phi, inv_stiff):
        _, nv, nx, ny, nz = adjoint.shape
        modes, stations = phi.shape
        inv_row = inv_stiff.reshape(1, modes)
        f32 = jnp.float32
        operands = (adjoint, jacobian, volume, source, surface_out, surface_in, station, phi, inv_row)
        vmem = pltpu.VMEM
        sem = pltpu.SemaphoreType.DMA
        residual, modal = pl.pallas_call(
            functools.partial(kernel, ni, ns),
            out_shape=(jax.ShapeDtypeStruct((nv, nx, ny, nz), f32), jax.ShapeDtypeStruct((1, modes), f32)),
            in_specs=[pl.BlockSpec(memory_space=pltpu.HBM)] * len(operands),
            out_specs=(pl.BlockSpec(memory_space=pltpu.VMEM), pl.BlockSpec(memory_space=pltpu.VMEM)),
            scratch_shapes=[
                vmem((nv, nx, ny, nz), f32), vmem(jacobian.shape[1:], f32), vmem((nx, ny, nz), f32),
                vmem((nv, nx, ny, nz), f32), vmem((nv, nx, nz), f32), vmem((nv, nx, nz), f32),
                vmem((nx, nz), jnp.int32), vmem((modes, stations), f32), vmem((1, modes), f32),
                vmem((ni, 3, 8, nz), f32), vmem((ni, 3, 8, nz), f32), vmem((nv, nx, ny, nz), f32),
                vmem((nv * nx * ny // 8, 8, nz), f32),
                vmem((2, nv, ny, nz), f32), vmem((2, nv, ny, nz), f32), vmem((nx, modes, nz), f32),
                vmem((1, nz), f32), vmem((ns, 1, nz), f32),
                sem((8,)), sem((9,)), sem, sem, sem, sem, sem((2,)), sem((2,)), sem, sem,
                pltpu.SemaphoreType.REGULAR((ns,)),
            ],
            compiler_params=pltpu.CompilerParams(
                collective_id=0, has_side_effects=True, vmem_limit_bytes=24 << 20),
        )(*[pltpu.with_memory_space_constraint(x, pltpu.HBM) for x in operands])
        return pl.pallas_call(
            put_out,
            out_shape=(jax.ShapeDtypeStruct((1, nv, nx, ny, nz), f32), jax.ShapeDtypeStruct((1, modes), f32)),
            in_specs=[pl.BlockSpec(memory_space=vmem)] * 2,
            out_specs=(pl.BlockSpec(memory_space=pltpu.HBM), pl.BlockSpec(memory_space=pltpu.HBM)),
            scratch_shapes=[sem((2,))],
        )(*[pltpu.with_memory_space_constraint(x, vmem) for x in (residual, modal)])

    return jax.shard_map(
        body, mesh=mesh, in_specs=placed,
        out_specs=(P("inst", None, "space", None, None), P("inst", None)), check_vma=False)
```

```python
import functools

import numpy as np
import jax
import jax.numpy as jnp
from jax import lax
from jax.experimental import pallas as pl
from jax.experimental.pallas import tpu as pltpu
from jax.sharding import PartitionSpec as P

MESH = pl.DeviceIdType.MESH
FIRST = (0, 3)
COUNT = (3, 2)


def time_weight(count):
    k = np.arange(count)
    angle = np.pi * k / count
    parity = 1.0 - 2.0 * (k % 2)
    safe = np.where(k != 0, np.sin(angle), 1.0)
    first = np.where(k != 0, 0.5 * parity * np.cos(angle) / safe, 0.0)
    second = np.where(k != 0, -0.5 * parity / (safe * safe), -(count * count + 2) / 12.0)
    return first - 0.25 * second


LATE = 40
LEAN = 71


def turn(block):
    z, y = lax.div(block, 2), lax.rem(block, 2)
    return jnp.where(z < 4, 10 * z, 51 + z) + 16 * y


def turn_of(block):
    z, y = divmod(block, 2)
    return (10 * z if z < 4 else 51 + z) + 16 * y


def kernel(
    ni, ns,
    adj_hbm, jac_hbm, vol_hbm, src_hbm, so_hbm, si_hbm, st_hbm, phi_hbm, inv_hbm,
    res, modal,
    adj, jac, vol, src, so, si, st, phi, inv,
    inbox, outbox, mixed, gauge, halo_out, halo_in, gmat, row_out, row_in,
    local_sem, jac_sem, a_send, a_recv, b_send, b_recv, h_send, h_recv, m_send, m_recv,
    ready_space, relay,
):
    me = lax.axis_index("inst")
    sp = lax.axis_index("space")
    core = lax.rem(me, 2)
    chip = lax.div(me, 2)
    nc = ni // 2
    nv, nx, ny, nz = adj.shape
    halves = ny // 8

    cx, cy, wide = lax.div(chip, 2), lax.rem(chip, 2), nc // 2
    across = [lax.rem(cx + 2, wide) * 2 + y for y in range(2)]
    beside = [lax.rem(cx + d, wide) * 2 + y for d in (1, wide - 1) for y in range(2)] + [cx * 2 + 1 - cy]

    def spot(c):
        return lax.div(c, halves), pl.multiple_of(lax.rem(c, halves) * 8, 8)

    def send_signals(semaphore, axis, peer):
        pl.semaphore_signal(semaphore, inc=1, device_id={axis: peer}, device_id_type=MESH)

    barrier = pltpu.get_barrier_semaphore()

    my_turn = turn(sp)
    lean = my_turn >= LEAN

    @pl.when(jnp.logical_not(lean))
    def _():
        for c in across:
            for cc in range(2):
                send_signals(barrier, "inst", c * 2 + cc)

    for c in beside:
        for cc in range(2):
            send_signals(barrier, "inst", c * 2 + cc)
    send_signals(barrier, "inst", chip * 2 + 1 - core)

    def later_blocks(act):
        for peer in sorted(range(ns), key=turn_of):
            @pl.when(turn_of(peer) > my_turn)
            def _():
                act(peer)

    later_blocks(lambda peer: send_signals(barrier, "space", peer))
    n_earlier = sum(jnp.where(turn_of(p) < my_turn, 1, 0) for p in range(ns))

    small = [(st_hbm, st), (phi_hbm, phi), (so_hbm, so), (adj_hbm.at[0], adj), (inv_hbm, inv),
             (si_hbm, si), (vol_hbm, vol), (src_hbm.at[0], src)]
    copies = [pltpu.make_async_copy(a, b, local_sem.at[n]) for n, (a, b) in enumerate(small)]
    edge1 = pltpu.make_async_copy(jac_hbm.at[0, 1, :, :, nx - 1], jac.at[1, :, :, nx - 1], jac_sem.at[7])
    edge2 = pltpu.make_async_copy(jac_hbm.at[0, 2, :, :, 0], jac.at[2, :, :, 0], jac_sem.at[8])
    rest1 = pltpu.make_async_copy(jac_hbm.at[0, 1, :, :, 0:nx - 1], jac.at[1, :, :, 0:nx - 1], jac_sem.at[1])
    rest2 = pltpu.make_async_copy(jac_hbm.at[0, 2, :, :, 1:nx], jac.at[2, :, :, 1:nx], jac_sem.at[2])
    bulk = [pltpu.make_async_copy(jac_hbm.at[0, d], jac.at[d], jac_sem.at[d]) for d in (0, 3, 4, 5, 6)]
    for c in copies[:4] + [edge1, edge2] + copies[4:] + [rest1, rest2] + bulk:
        c.start()

    copies[0].wait()
    copies[1].wait()
    modes, stations = phi.shape
    for x in range(nx):
        where = jnp.broadcast_to(st[x:x + 1, :], (modes, nz))
        column = lax.rem(where, nz)
        taken = jnp.zeros((modes, nz), jnp.float32)
        for start in range(0, stations, nz):
            found = jnp.take_along_axis(phi[:, start:start + nz], column, axis=1, mode="promise_in_bounds")
            taken = jnp.where(where - column == start, found, taken)
        gmat[x] = taken

    copies[2].wait()
    copies[3].wait()
    col = jnp.zeros((modes, nz), jnp.float32)
    for x in range(nx):
        face = so[0, x:x + 1, :] * adj[0, x, 0:1, :]
        for j in range(1, nv):
            face = face + so[j, x:x + 1, :] * adj[j, x, 0:1, :]
        col = col + gmat[x] * face
    col = jnp.sum(col, axis=1, keepdims=True)
    diag = (lax.broadcasted_iota(jnp.int32, (modes, nz), 0)
            == lax.broadcasted_iota(jnp.int32, (modes, nz), 1))
    share = jnp.sum(jnp.where(diag, col, 0.0), axis=0, keepdims=True)
    row_out[...] = share
    row_in[sp] = share

    def product(d, j, x):
        total = jac[d, 0, j, x] * adj[0, x]
        for i in range(1, nv):
            total = total + jac[d, i, j, x] * adj[i, x]
        return total

    edge1.wait()
    edge2.wait()
    for side, d, x in ((0, 1, nx - 1), (1, 2, 0)):
        for j in range(nv):
            halo_out[side, j] = product(d, j, x)

    pl.semaphore_wait(barrier, ni - 1 + n_earlier - jnp.where(lean, 2 * len(across), 0))

    @pl.when(lean)
    def _():
        send_signals(relay, "inst", lax.rem(me + ni - 4, ni))

    def to_block(peer):
        return pltpu.make_async_remote_copy(
            src_ref=row_out, dst_ref=row_in.at[sp],
            send_sem=m_send, recv_sem=m_recv,
            device_id={"space": peer}, device_id_type=MESH)

    for peer in sorted(range(ns), key=turn_of):
        @pl.when(turn_of(peer) < my_turn)
        def _():
            to_block(peer).start()
            send_signals(ready_space.at[sp], "space", peer)


    def halo(side):
        peer = lax.rem(sp + (1 if side == 0 else ns - 1), ns)
        return peer, pltpu.make_async_remote_copy(
            src_ref=halo_out.at[side], dst_ref=halo_in.at[side],
            send_sem=h_send.at[side], recv_sem=h_recv.at[side],
            device_id={"space": peer}, device_id_type=MESH)

    for side in range(2):
        target, copy = halo(side)

        @pl.when(turn(target) < my_turn)
        def _():
            copy.start()

    def to_mixer(other, cc):
        x, y = spot(other)
        return pltpu.make_async_remote_copy(
            src_ref=adj.at[pl.ds(FIRST[cc], COUNT[cc]), x, pl.ds(y, 8), :],
            dst_ref=inbox.at[me, pl.ds(0, COUNT[cc])],
            send_sem=a_send, recv_sem=a_recv,
            device_id={"inst": other * 2 + cc}, device_id_type=MESH)

    def send_across():
        for c in across:
            for cc in range(2):
                to_mixer(c, cc).start()

    @pl.when(jnp.logical_not(lean))
    def _():
        send_across()

    for c in beside:
        for cc in range(2):
            to_mixer(c, cc).start()
    for cc in range(2):
        @pl.when(core != cc)
        def _():
            to_mixer(chip, cc).start()

    @pl.when(lean)
    def _():
        pl.semaphore_wait(relay, 1)
        send_across()

    rest1.wait()
    rest2.wait()
    for c in bulk:
        c.wait()
    copies[7].wait()
    row = lax.broadcasted_iota(jnp.int32, (ny, nz), 0)
    lane = lax.broadcasted_iota(jnp.int32, (ny, nz), 1)

    def flux(j, carry):
        for x in range(nx):
            total = product(0, j, x) - src[j, x]
            if x > 0:
                total = total + product(1, j, x - 1)
            if x < nx - 1:
                total = total + product(2, j, x + 1)
            total = total + jnp.where(row == 0, 0.0, pltpu.roll(product(3, j, x), 1, 0))
            total = total + jnp.where(row == ny - 1, 0.0, pltpu.roll(product(4, j, x), ny - 1, 0))
            total = total + jnp.where(lane == 0, 0.0, pltpu.roll(product(5, j, x), 1, 1))
            total = total + jnp.where(lane == nz - 1, 0.0, pltpu.roll(product(6, j, x), nz - 1, 1))
            res[j, x] = total
        return carry

    lax.fori_loop(0, nv, flux, 0)

    def is_near(peer):
        return jnp.where(peer > sp, peer - sp, sp - peer) == 1

    def to_later(near):
        def act(peer):
            @pl.when(is_near(peer) if near else jnp.logical_not(is_near(peer)))
            def _():
                pl.semaphore_wait(ready_space.at[peer], 1)
                to_block(peer).start()

        later_blocks(act)
        for side in range(2):
            target, copy = halo(side)
            chosen = is_near(target) if near else jnp.logical_not(is_near(target))

            @pl.when((turn(target) > my_turn) & chosen)
            def _():
                copy.start()

    to_later(True)

    def arrived(block, semaphore):
        pltpu.make_async_copy(block, block, semaphore).wait()

    my_x, my_y = spot(chip)
    for cc in range(2):
        @pl.when(core == cc)
        def _():
            inbox[me, 0:COUNT[cc]] = adj[FIRST[cc]:FIRST[cc] + COUNT[cc], my_x, pl.ds(my_y, 8), :]

            arrived(inbox.at[pl.ds(0, ni - 1), pl.ds(0, COUNT[cc])], a_recv)

    weight = time_weight(ni)
    half = ni // 2

    def home(cc, d):
        peer = lax.rem(me + d, ni)
        return pltpu.make_async_remote_copy(
            src_ref=outbox.at[peer, pl.ds(0, COUNT[cc])],
            dst_ref=mixed.at[pl.ds(FIRST[cc], COUNT[cc]), my_x, pl.ds(my_y, 8), :],
            send_sem=b_send, recv_sem=b_recv,
            device_id={"inst": peer}, device_id_type=MESH)

    def mix(cc):
        n = COUNT[cc]
        a = [inbox[lax.rem(me + k, ni), 0:n] for k in range(ni)]
        even = [a[k] + a[k + half] for k in range(half)]
        odd = [a[k] - a[k + half] for k in range(half)]
        for d in sorted(range(half), key=lambda d: d == 0):
            near = [float(weight[(k - d) % ni]) for k in range(half)]
            far = [float(weight[(k - d + half) % ni]) for k in range(half)]
            plus = sum(even[k] * np.float32(0.5 * (near[k] + far[k])) for k in range(half))
            minus = sum(odd[k] * np.float32(0.5 * (near[k] - far[k])) for k in range(half))
            outbox[lax.rem(me + d + half, ni), 0:n] = plus - minus
            home(cc, d + half).start()
            if d:
                outbox[lax.rem(me + d, ni), 0:n] = plus + minus
                home(cc, d).start()
            else:
                mixed[FIRST[cc]:FIRST[cc] + n, my_x, pl.ds(my_y, 8), :] = plus + minus

    for cc in range(2):
        @pl.when(core == cc)
        def _():
            mix(cc)

    to_later(False)
    for cc in range(2):
        @pl.when(core == cc)
        def _():
            arrived(gauge.at[pl.ds(0, nv * nx * halves - COUNT[cc])], a_send)

    arrived(row_in.at[pl.ds(0, ns - 1)], m_send)
    copies[4].wait()
    copies[5].wait()
    copies[6].wait()

    def add_mixed():
        for cc in range(2):
            @pl.when(core == cc)
            def _():
                arrived(gauge.at[pl.ds(0, nv * nx * halves - COUNT[cc])], b_recv)

        for j in range(nv):
            for x in range(nx):
                res[j, x] = res[j, x] + vol[x] * mixed[j, x]

    def add_halo():
        halo(0)[1].wait_recv()
        halo(1)[1].wait_recv()
        for j in range(nv):
            res[j, 0] = res[j, 0] + halo_in[0, j]
            res[j, nx - 1] = res[j, nx - 1] + halo_in[1, j]

    def add_back():
        arrived(row_in.at[pl.ds(0, ns - 1)], m_recv)
        sums = jnp.sum(row_in[...], axis=0)
        coords = sums[:, 0:modes] * inv[...]
        modal[...] = coords
        square = (lax.broadcasted_iota(jnp.int32, (modes, modes), 0)
                  == lax.broadcasted_iota(jnp.int32, (modes, modes), 1))
        column = jnp.sum(jnp.where(square, coords, 0.0), axis=1, keepdims=True)
        for x in range(nx):
            back = jnp.sum(gmat[x] * column, axis=0, keepdims=True)
            for j in range(nv):
                res[j, x, 0:1, :] = res[j, x, 0:1, :] + si[j, x:x + 1, :] * back

    @pl.when(my_turn < LATE)
    def _():
        add_mixed()
        add_halo()
        add_back()

    @pl.when(my_turn >= LATE)
    def _():
        add_back()
        add_halo()
        add_mixed()

    halo(0)[1].wait_send()
    halo(1)[1].wait_send()
    for cc in range(2):
        @pl.when(core == cc)
        def _():
            arrived(inbox.at[pl.ds(0, ni - 1), pl.ds(0, COUNT[cc])], b_send)


def put_out(res, modal, res_hbm, modal_hbm, sem):
    first = pltpu.make_async_copy(res, res_hbm.at[0], sem.at[0])
    second = pltpu.make_async_copy(modal, modal_hbm, sem.at[1])
    first.start()
    second.start()
    first.wait()
    second.wait()


def solution(mesh):
    ni, ns = mesh.shape["inst"], mesh.shape["space"]
    placed = (
        P("inst", None, "space", None, None),
        P("inst", None, None, None, "space", None, None),
        P("space", None, None),
        P("inst", None, "space", None, None),
        P(None, "space", None),
        P(None, "space", None),
        P("space", None),
        P(),
        P(),
    )

    def body(adjoint, jacobian, volume, source, surface_out, surface_in, station, phi, inv_stiff):
        _, nv, nx, ny, nz = adjoint.shape
        modes, stations = phi.shape
        inv_row = inv_stiff.reshape(1, modes)
        f32 = jnp.float32
        operands = (adjoint, jacobian, volume, source, surface_out, surface_in, station, phi, inv_row)
        vmem = pltpu.VMEM
        sem = pltpu.SemaphoreType.DMA
        residual, modal = pl.pallas_call(
            functools.partial(kernel, ni, ns),
            out_shape=(jax.ShapeDtypeStruct((nv, nx, ny, nz), f32), jax.ShapeDtypeStruct((1, modes), f32)),
            in_specs=[pl.BlockSpec(memory_space=pltpu.HBM)] * len(operands),
            out_specs=(pl.BlockSpec(memory_space=pltpu.VMEM), pl.BlockSpec(memory_space=pltpu.VMEM)),
            scratch_shapes=[
                vmem((nv, nx, ny, nz), f32), vmem(jacobian.shape[1:], f32), vmem((nx, ny, nz), f32),
                vmem((nv, nx, ny, nz), f32), vmem((nv, nx, nz), f32), vmem((nv, nx, nz), f32),
                vmem((nx, nz), jnp.int32), vmem((modes, stations), f32), vmem((1, modes), f32),
                vmem((ni, 3, 8, nz), f32), vmem((ni, 3, 8, nz), f32), vmem((nv, nx, ny, nz), f32),
                vmem((nv * nx * ny // 8, 8, nz), f32),
                vmem((2, nv, ny, nz), f32), vmem((2, nv, ny, nz), f32), vmem((nx, modes, nz), f32),
                vmem((1, nz), f32), vmem((ns, 1, nz), f32),
                sem((8,)), sem((9,)), sem, sem, sem, sem, sem((2,)), sem((2,)), sem, sem,
                pltpu.SemaphoreType.REGULAR((ns,)), pltpu.SemaphoreType.REGULAR,
            ],
            compiler_params=pltpu.CompilerParams(
                collective_id=0, has_side_effects=True, vmem_limit_bytes=24 << 20),
        )(*[pltpu.with_memory_space_constraint(x, pltpu.HBM) for x in operands])
        return pl.pallas_call(
            put_out,
            out_shape=(jax.ShapeDtypeStruct((1, nv, nx, ny, nz), f32), jax.ShapeDtypeStruct((1, modes), f32)),
            in_specs=[pl.BlockSpec(memory_space=vmem)] * 2,
            out_specs=(pl.BlockSpec(memory_space=pltpu.HBM), pl.BlockSpec(memory_space=pltpu.HBM)),
            scratch_shapes=[sem((2,))],
        )(*[pltpu.with_memory_space_constraint(x, vmem) for x in (residual, modal)])

    return jax.shard_map(
        body, mesh=mesh, in_specs=placed,
        out_specs=(P("inst", None, "space", None, None), P("inst", None)), check_vma=False)
```

```python
import functools

import numpy as np
import jax
import jax.numpy as jnp
from jax import lax
from jax.experimental import pallas as pl
from jax.experimental.pallas import tpu as pltpu
from jax.sharding import PartitionSpec as P

MESH = pl.DeviceIdType.MESH
FIRST = (0, 3)
COUNT = (3, 2)


def time_weight(count):
    k = np.arange(count)
    angle = np.pi * k / count
    parity = 1.0 - 2.0 * (k % 2)
    safe = np.where(k != 0, np.sin(angle), 1.0)
    first = np.where(k != 0, 0.5 * parity * np.cos(angle) / safe, 0.0)
    second = np.where(k != 0, -0.5 * parity / (safe * safe), -(count * count + 2) / 12.0)
    return first - 0.25 * second


LATE = 40
LEAN = 71


def turn(block):
    z, y = lax.div(block, 2), lax.rem(block, 2)
    return jnp.where(z < 4, 10 * z, 51 + z) + 16 * y


def turn_of(block):
    z, y = divmod(block, 2)
    return (10 * z if z < 4 else 51 + z) + 16 * y


def kernel(
    ni, ns,
    adj_hbm, jac_hbm, vol_hbm, src_hbm, so_hbm, si_hbm, st_hbm, phi_hbm, inv_hbm,
    res, modal,
    adj, jac, vol, src, so, si, st, phi, inv,
    inbox, outbox, mixed, gauge, halo_out, halo_in, gmat, row_out, row_in,
    local_sem, jac_sem, a_send, a_recv, b_send, b_recv, h_send, h_recv, m_send, m_recv,
    ready_space, relay,
):
    me = lax.axis_index("inst")
    sp = lax.axis_index("space")
    core = lax.rem(me, 2)
    chip = lax.div(me, 2)
    nc = ni // 2
    nv, nx, ny, nz = adj.shape
    halves = ny // 8

    cx, cy, wide = lax.div(chip, 2), lax.rem(chip, 2), nc // 2
    across = [lax.rem(cx + 2, wide) * 2 + y for y in range(2)]
    beside = [lax.rem(cx + d, wide) * 2 + y for d in (1, wide - 1) for y in range(2)] + [cx * 2 + 1 - cy]

    def spot(c):
        return lax.div(c, halves), pl.multiple_of(lax.rem(c, halves) * 8, 8)

    def send_signals(semaphore, axis, peer):
        pl.semaphore_signal(semaphore, inc=1, device_id={axis: peer}, device_id_type=MESH)

    barrier = pltpu.get_barrier_semaphore()

    my_turn = turn(sp)
    lean = my_turn >= LEAN

    @pl.when(jnp.logical_not(lean))
    def _():
        for c in across:
            for cc in range(2):
                send_signals(barrier, "inst", c * 2 + cc)

    for c in beside:
        for cc in range(2):
            send_signals(barrier, "inst", c * 2 + cc)
    send_signals(barrier, "inst", chip * 2 + 1 - core)

    def later_blocks(act):
        for peer in sorted(range(ns), key=turn_of):
            @pl.when(turn_of(peer) > my_turn)
            def _():
                act(peer)

    later_blocks(lambda peer: send_signals(barrier, "space", peer))
    n_earlier = sum(jnp.where(turn_of(p) < my_turn, 1, 0) for p in range(ns))

    small = [(st_hbm, st), (phi_hbm, phi), (so_hbm, so), (adj_hbm.at[0], adj), (inv_hbm, inv),
             (si_hbm, si), (vol_hbm, vol), (src_hbm.at[0], src)]
    copies = [pltpu.make_async_copy(a, b, local_sem.at[n]) for n, (a, b) in enumerate(small)]
    edge1 = pltpu.make_async_copy(jac_hbm.at[0, 1, :, :, nx - 1], jac.at[1, :, :, nx - 1], jac_sem.at[7])
    edge2 = pltpu.make_async_copy(jac_hbm.at[0, 2, :, :, 0], jac.at[2, :, :, 0], jac_sem.at[8])
    rest1 = pltpu.make_async_copy(jac_hbm.at[0, 1, :, :, 0:nx - 1], jac.at[1, :, :, 0:nx - 1], jac_sem.at[1])
    rest2 = pltpu.make_async_copy(jac_hbm.at[0, 2, :, :, 1:nx], jac.at[2, :, :, 1:nx], jac_sem.at[2])
    bulk = [pltpu.make_async_copy(jac_hbm.at[0, d], jac.at[d], jac_sem.at[d]) for d in (0, 3, 4, 5, 6)]
    for c in copies[:4] + [edge1, edge2] + copies[4:] + [rest1, rest2] + bulk:
        c.start()

    copies[0].wait()
    copies[1].wait()
    modes, stations = phi.shape
    for x in range(nx):
        where = jnp.broadcast_to(st[x:x + 1, :], (modes, nz))
        column = lax.rem(where, nz)
        taken = jnp.zeros((modes, nz), jnp.float32)
        for start in range(0, stations, nz):
            found = jnp.take_along_axis(phi[:, start:start + nz], column, axis=1, mode="promise_in_bounds")
            taken = jnp.where(where - column == start, found, taken)
        gmat[x] = taken

    copies[2].wait()
    copies[3].wait()
    col = jnp.zeros((modes, nz), jnp.float32)
    for x in range(nx):
        face = so[0, x:x + 1, :] * adj[0, x, 0:1, :]
        for j in range(1, nv):
            face = face + so[j, x:x + 1, :] * adj[j, x, 0:1, :]
        col = col + gmat[x] * face
    col = jnp.sum(col, axis=1, keepdims=True)
    diag = (lax.broadcasted_iota(jnp.int32, (modes, nz), 0)
            == lax.broadcasted_iota(jnp.int32, (modes, nz), 1))
    share = jnp.sum(jnp.where(diag, col, 0.0), axis=0, keepdims=True)
    row_out[...] = share
    row_in[sp] = share

    def product(d, j, x):
        total = jac[d, 0, j, x] * adj[0, x]
        for i in range(1, nv):
            total = total + jac[d, i, j, x] * adj[i, x]
        return total

    edge1.wait()
    edge2.wait()
    for side, d, x in ((0, 1, nx - 1), (1, 2, 0)):
        for j in range(nv):
            halo_out[side, j] = product(d, j, x)

    pl.semaphore_wait(barrier, ni - 1 + n_earlier - jnp.where(lean, 2 * len(across), 0))

    @pl.when(lean)
    def _():
        send_signals(relay, "inst", lax.rem(me + ni - 4, ni))

    def to_block(peer):
        return pltpu.make_async_remote_copy(
            src_ref=row_out, dst_ref=row_in.at[sp],
            send_sem=m_send, recv_sem=m_recv,
            device_id={"space": peer}, device_id_type=MESH)

    for peer in sorted(range(ns), key=turn_of):
        @pl.when(turn_of(peer) < my_turn)
        def _():
            to_block(peer).start()
            send_signals(ready_space.at[sp], "space", peer)


    def halo(side):
        peer = lax.rem(sp + (1 if side == 0 else ns - 1), ns)
        return peer, [pltpu.make_async_remote_copy(
            src_ref=halo_out.at[side, j], dst_ref=halo_in.at[side, j],
            send_sem=h_send.at[side], recv_sem=h_recv.at[side],
            device_id={"space": peer}, device_id_type=MESH) for j in range(nv)]

    for side in range(2):
        target, parts_of_halo = halo(side)

        @pl.when(turn(target) < my_turn)
        def _():
            for copy in parts_of_halo:
                copy.start()

    def to_mixer(other, cc):
        x, y = spot(other)
        return pltpu.make_async_remote_copy(
            src_ref=adj.at[pl.ds(FIRST[cc], COUNT[cc]), x, pl.ds(y, 8), :],
            dst_ref=inbox.at[me, pl.ds(0, COUNT[cc])],
            send_sem=a_send, recv_sem=a_recv,
            device_id={"inst": other * 2 + cc}, device_id_type=MESH)

    def send_across():
        for c in across:
            for cc in range(2):
                to_mixer(c, cc).start()

    @pl.when(jnp.logical_not(lean))
    def _():
        send_across()

    for c in beside:
        for cc in range(2):
            to_mixer(c, cc).start()
    for cc in range(2):
        @pl.when(core != cc)
        def _():
            to_mixer(chip, cc).start()

    @pl.when(lean)
    def _():
        pl.semaphore_wait(relay, 1)
        send_across()

    rest1.wait()
    rest2.wait()
    for c in bulk:
        c.wait()
    copies[7].wait()
    row = lax.broadcasted_iota(jnp.int32, (ny, nz), 0)
    lane = lax.broadcasted_iota(jnp.int32, (ny, nz), 1)

    def flux(j, carry):
        for x in range(nx):
            total = product(0, j, x) - src[j, x]
            if x > 0:
                total = total + product(1, j, x - 1)
            if x < nx - 1:
                total = total + product(2, j, x + 1)
            total = total + jnp.where(row == 0, 0.0, pltpu.roll(product(3, j, x), 1, 0))
            total = total + jnp.where(row == ny - 1, 0.0, pltpu.roll(product(4, j, x), ny - 1, 0))
            total = total + jnp.where(lane == 0, 0.0, pltpu.roll(product(5, j, x), 1, 1))
            total = total + jnp.where(lane == nz - 1, 0.0, pltpu.roll(product(6, j, x), nz - 1, 1))
            res[j, x] = total
        return carry

    lax.fori_loop(0, nv, flux, 0)

    def is_near(peer):
        return jnp.where(peer > sp, peer - sp, sp - peer) == 1

    def to_later(near):
        def act(peer):
            @pl.when(is_near(peer) if near else jnp.logical_not(is_near(peer)))
            def _():
                pl.semaphore_wait(ready_space.at[peer], 1)
                to_block(peer).start()

        later_blocks(act)
        for side in range(2):
            target, parts_of_halo = halo(side)
            chosen = is_near(target) if near else jnp.logical_not(is_near(target))

            @pl.when((turn(target) > my_turn) & chosen)
            def _():
                for copy in parts_of_halo:
                    copy.start()

    to_later(True)

    def arrived(block, semaphore):
        pltpu.make_async_copy(block, block, semaphore).wait()

    my_x, my_y = spot(chip)
    for cc in range(2):
        @pl.when(core == cc)
        def _():
            inbox[me, 0:COUNT[cc]] = adj[FIRST[cc]:FIRST[cc] + COUNT[cc], my_x, pl.ds(my_y, 8), :]

            arrived(inbox.at[pl.ds(0, ni - 1), pl.ds(0, COUNT[cc])], a_recv)

    weight = time_weight(ni)
    half = ni // 2

    def home(cc, d):
        peer = lax.rem(me + d, ni)
        return pltpu.make_async_remote_copy(
            src_ref=outbox.at[peer, pl.ds(0, COUNT[cc])],
            dst_ref=mixed.at[pl.ds(FIRST[cc], COUNT[cc]), my_x, pl.ds(my_y, 8), :],
            send_sem=b_send, recv_sem=b_recv,
            device_id={"inst": peer}, device_id_type=MESH)

    def mix(cc):
        n = COUNT[cc]
        a = [inbox[lax.rem(me + k, ni), 0:n] for k in range(ni)]
        even = [a[k] + a[k + half] for k in range(half)]
        odd = [a[k] - a[k + half] for k in range(half)]
        for d in sorted(range(half), key=lambda d: d == 0):
            near = [float(weight[(k - d) % ni]) for k in range(half)]
            far = [float(weight[(k - d + half) % ni]) for k in range(half)]
            plus = sum(even[k] * np.float32(0.5 * (near[k] + far[k])) for k in range(half))
            minus = sum(odd[k] * np.float32(0.5 * (near[k] - far[k])) for k in range(half))
            outbox[lax.rem(me + d + half, ni), 0:n] = plus - minus
            home(cc, d + half).start()
            if d:
                outbox[lax.rem(me + d, ni), 0:n] = plus + minus
                home(cc, d).start()
            else:
                mixed[FIRST[cc]:FIRST[cc] + n, my_x, pl.ds(my_y, 8), :] = plus + minus

    for cc in range(2):
        @pl.when(core == cc)
        def _():
            mix(cc)

    to_later(False)
    for cc in range(2):
        @pl.when(core == cc)
        def _():
            arrived(gauge.at[pl.ds(0, nv * nx * halves - COUNT[cc])], a_send)

    arrived(row_in.at[pl.ds(0, ns - 1)], m_send)
    copies[4].wait()
    copies[5].wait()
    copies[6].wait()

    def add_mixed():
        for cc in range(2):
            @pl.when(core == cc)
            def _():
                arrived(gauge.at[pl.ds(0, nv * nx * halves - COUNT[cc])], b_recv)

        for j in range(nv):
            for x in range(nx):
                res[j, x] = res[j, x] + vol[x] * mixed[j, x]

    def add_halo():
        for side in range(2):
            arrived(halo_in.at[side], h_recv.at[side])
        for j in range(nv):
            res[j, 0] = res[j, 0] + halo_in[0, j]
            res[j, nx - 1] = res[j, nx - 1] + halo_in[1, j]

    def add_back():
        arrived(row_in.at[pl.ds(0, ns - 1)], m_recv)
        sums = jnp.sum(row_in[...], axis=0)
        coords = sums[:, 0:modes] * inv[...]
        modal[...] = coords
        square = (lax.broadcasted_iota(jnp.int32, (modes, modes), 0)
                  == lax.broadcasted_iota(jnp.int32, (modes, modes), 1))
        column = jnp.sum(jnp.where(square, coords, 0.0), axis=1, keepdims=True)
        for x in range(nx):
            back = jnp.sum(gmat[x] * column, axis=0, keepdims=True)
            for j in range(nv):
                res[j, x, 0:1, :] = res[j, x, 0:1, :] + si[j, x:x + 1, :] * back

    @pl.when(my_turn < LATE)
    def _():
        add_mixed()
        add_halo()
        add_back()

    @pl.when(my_turn >= LATE)
    def _():
        add_back()
        add_halo()
        add_mixed()

    for side in range(2):
        arrived(halo_out.at[side], h_send.at[side])
    for cc in range(2):
        @pl.when(core == cc)
        def _():
            arrived(inbox.at[pl.ds(0, ni - 1), pl.ds(0, COUNT[cc])], b_send)


def put_out(res, modal, res_hbm, modal_hbm, sem):
    nv, nx = res.shape[:2]
    half = nx // 2
    copies = [pltpu.make_async_copy(modal, modal_hbm, sem.at[0])]
    for j in range(nv):
        for x in range(2):
            part = pl.ds(x * half, half)
            copies.append(pltpu.make_async_copy(res.at[j, part], res_hbm.at[0, j, part], sem.at[len(copies)]))
    for copy in copies:
        copy.start()
    for copy in copies:
        copy.wait()


def solution(mesh):
    ni, ns = mesh.shape["inst"], mesh.shape["space"]
    placed = (
        P("inst", None, "space", None, None),
        P("inst", None, None, None, "space", None, None),
        P("space", None, None),
        P("inst", None, "space", None, None),
        P(None, "space", None),
        P(None, "space", None),
        P("space", None),
        P(),
        P(),
    )

    def body(adjoint, jacobian, volume, source, surface_out, surface_in, station, phi, inv_stiff):
        _, nv, nx, ny, nz = adjoint.shape
        modes, stations = phi.shape
        inv_row = inv_stiff.reshape(1, modes)
        f32 = jnp.float32
        operands = (adjoint, jacobian, volume, source, surface_out, surface_in, station, phi, inv_row)
        vmem = pltpu.VMEM
        sem = pltpu.SemaphoreType.DMA
        residual, modal = pl.pallas_call(
            functools.partial(kernel, ni, ns),
            out_shape=(jax.ShapeDtypeStruct((nv, nx, ny, nz), f32), jax.ShapeDtypeStruct((1, modes), f32)),
            in_specs=[pl.BlockSpec(memory_space=pltpu.HBM)] * len(operands),
            out_specs=(pl.BlockSpec(memory_space=pltpu.VMEM), pl.BlockSpec(memory_space=pltpu.VMEM)),
            scratch_shapes=[
                vmem((nv, nx, ny, nz), f32), vmem(jacobian.shape[1:], f32), vmem((nx, ny, nz), f32),
                vmem((nv, nx, ny, nz), f32), vmem((nv, nx, nz), f32), vmem((nv, nx, nz), f32),
                vmem((nx, nz), jnp.int32), vmem((modes, stations), f32), vmem((1, modes), f32),
                vmem((ni, 3, 8, nz), f32), vmem((ni, 3, 8, nz), f32), vmem((nv, nx, ny, nz), f32),
                vmem((nv * nx * ny // 8, 8, nz), f32),
                vmem((2, nv, ny, nz), f32), vmem((2, nv, ny, nz), f32), vmem((nx, modes, nz), f32),
                vmem((1, nz), f32), vmem((ns, 1, nz), f32),
                sem((8,)), sem((9,)), sem, sem, sem, sem, sem((2,)), sem((2,)), sem, sem,
                pltpu.SemaphoreType.REGULAR((ns,)), pltpu.SemaphoreType.REGULAR,
            ],
            compiler_params=pltpu.CompilerParams(
                collective_id=0, has_side_effects=True, vmem_limit_bytes=24 << 20),
        )(*[pltpu.with_memory_space_constraint(x, pltpu.HBM) for x in operands])
        return pl.pallas_call(
            put_out,
            out_shape=(jax.ShapeDtypeStruct((1, nv, nx, ny, nz), f32), jax.ShapeDtypeStruct((1, modes), f32)),
            in_specs=[pl.BlockSpec(memory_space=vmem)] * 2,
            out_specs=(pl.BlockSpec(memory_space=pltpu.HBM), pl.BlockSpec(memory_space=pltpu.HBM)),
            scratch_shapes=[sem((1 + 2 * nv,))],
        )(*[pltpu.with_memory_space_constraint(x, vmem) for x in (residual, modal)])

    return jax.shard_map(
        body, mesh=mesh, in_specs=placed,
        out_specs=(P("inst", None, "space", None, None), P("inst", None)), check_vma=False)
```

```python
import functools

import numpy as np
import jax
import jax.numpy as jnp
from jax import lax
from jax.experimental import pallas as pl
from jax.experimental.pallas import tpu as pltpu
from jax.sharding import PartitionSpec as P

MESH = pl.DeviceIdType.MESH
FIRST = (0, 3)
COUNT = (3, 2)


def time_weight(count):
    k = np.arange(count)
    angle = np.pi * k / count
    parity = 1.0 - 2.0 * (k % 2)
    safe = np.where(k != 0, np.sin(angle), 1.0)
    first = np.where(k != 0, 0.5 * parity * np.cos(angle) / safe, 0.0)
    second = np.where(k != 0, -0.5 * parity / (safe * safe), -(count * count + 2) / 12.0)
    return first - 0.25 * second


LATE = 40
LEAN = 71


def turn(block):
    z, y = lax.div(block, 2), lax.rem(block, 2)
    return jnp.where(z < 4, 10 * z, 51 + z) + 16 * y


def turn_of(block):
    z, y = divmod(block, 2)
    return (10 * z if z < 4 else 51 + z) + 16 * y


def kernel(
    ni, ns,
    adj_hbm, jac_hbm, vol_hbm, src_hbm, so_hbm, si_hbm, st_hbm, phi_hbm, inv_hbm,
    res, modal,
    adj, jac, vol, src, so, si, st, phi, inv,
    inbox, outbox, mixed, gauge, halo_out, halo_in, gmat, row_out, row_in,
    local_sem, jac_sem, a_send, a_recv, b_send, b_recv, h_send, h_recv, m_send, m_recv,
    ready_space, relay,
):
    me = lax.axis_index("inst")
    sp = lax.axis_index("space")
    core = lax.rem(me, 2)
    chip = lax.div(me, 2)
    nc = ni // 2
    nv, nx, ny, nz = adj.shape
    halves = ny // 8

    cx, cy, wide = lax.div(chip, 2), lax.rem(chip, 2), nc // 2
    across = [lax.rem(cx + 2, wide) * 2 + y for y in range(2)]
    beside = [lax.rem(cx + d, wide) * 2 + y for d in (1, wide - 1) for y in range(2)] + [cx * 2 + 1 - cy]

    def spot(c):
        return lax.div(c, halves), pl.multiple_of(lax.rem(c, halves) * 8, 8)

    def send_signals(semaphore, axis, peer):
        pl.semaphore_signal(semaphore, inc=1, device_id={axis: peer}, device_id_type=MESH)

    barrier = pltpu.get_barrier_semaphore()

    my_turn = turn(sp)
    lean = my_turn >= LEAN

    @pl.when(jnp.logical_not(lean))
    def _():
        for c in across:
            for cc in range(2):
                send_signals(barrier, "inst", c * 2 + cc)

    for c in beside:
        for cc in range(2):
            send_signals(barrier, "inst", c * 2 + cc)
    send_signals(barrier, "inst", chip * 2 + 1 - core)

    def later_blocks(act):
        for peer in sorted(range(ns), key=turn_of):
            @pl.when(turn_of(peer) > my_turn)
            def _():
                act(peer)

    later_blocks(lambda peer: send_signals(barrier, "space", peer))
    n_earlier = sum(jnp.where(turn_of(p) < my_turn, 1, 0) for p in range(ns))

    small = [(st_hbm, st), (phi_hbm, phi), (so_hbm, so), (adj_hbm.at[0], adj), (inv_hbm, inv),
             (si_hbm, si), (vol_hbm, vol), (src_hbm.at[0], src)]
    copies = [pltpu.make_async_copy(a, b, local_sem.at[n]) for n, (a, b) in enumerate(small)]
    edge1 = pltpu.make_async_copy(jac_hbm.at[0, 1, :, :, nx - 1], jac.at[1, :, :, nx - 1], jac_sem.at[7])
    edge2 = pltpu.make_async_copy(jac_hbm.at[0, 2, :, :, 0], jac.at[2, :, :, 0], jac_sem.at[8])
    rest1 = pltpu.make_async_copy(jac_hbm.at[0, 1, :, :, 0:nx - 1], jac.at[1, :, :, 0:nx - 1], jac_sem.at[1])
    rest2 = pltpu.make_async_copy(jac_hbm.at[0, 2, :, :, 1:nx], jac.at[2, :, :, 1:nx], jac_sem.at[2])
    bulk = [pltpu.make_async_copy(jac_hbm.at[0, d], jac.at[d], jac_sem.at[d]) for d in (0, 3, 4, 5, 6)]
    for c in copies[:4] + [edge1, edge2] + copies[4:] + [rest1, rest2] + bulk:
        c.start()

    copies[0].wait()
    copies[1].wait()
    modes, stations = phi.shape
    for x in range(nx):
        where = jnp.broadcast_to(st[x:x + 1, :], (modes, nz))
        column = lax.rem(where, nz)
        taken = jnp.zeros((modes, nz), jnp.float32)
        for start in range(0, stations, nz):
            found = jnp.take_along_axis(phi[:, start:start + nz], column, axis=1, mode="promise_in_bounds")
            taken = jnp.where(where - column == start, found, taken)
        gmat[x] = taken

    copies[2].wait()
    copies[3].wait()
    col = jnp.zeros((modes, nz), jnp.float32)
    for x in range(nx):
        face = so[0, x:x + 1, :] * adj[0, x, 0:1, :]
        for j in range(1, nv):
            face = face + so[j, x:x + 1, :] * adj[j, x, 0:1, :]
        col = col + gmat[x] * face
    col = jnp.sum(col, axis=1, keepdims=True)
    diag = (lax.broadcasted_iota(jnp.int32, (modes, nz), 0)
            == lax.broadcasted_iota(jnp.int32, (modes, nz), 1))
    share = jnp.sum(jnp.where(diag, col, 0.0), axis=0, keepdims=True)
    row_out[...] = share
    row_in[sp] = share

    def product(d, j, x):
        total = jac[d, 0, j, x] * adj[0, x]
        for i in range(1, nv):
            total = total + jac[d, i, j, x] * adj[i, x]
        return total

    edge1.wait()
    edge2.wait()
    for side, d, x in ((0, 1, nx - 1), (1, 2, 0)):
        for j in range(nv):
            halo_out[side, j] = product(d, j, x)

    pl.semaphore_wait(barrier, ni - 1 + n_earlier - jnp.where(lean, 2 * len(across), 0))

    @pl.when(lean)
    def _():
        send_signals(relay, "inst", lax.rem(me + ni - 4, ni))

    def to_block(peer):
        return pltpu.make_async_remote_copy(
            src_ref=row_out, dst_ref=row_in.at[sp],
            send_sem=m_send, recv_sem=m_recv,
            device_id={"space": peer}, device_id_type=MESH)

    for peer in sorted(range(ns), key=turn_of):
        @pl.when(turn_of(peer) < my_turn)
        def _():
            to_block(peer).start()
            send_signals(ready_space.at[sp], "space", peer)


    def halo(side):
        peer = lax.rem(sp + (1 if side == 0 else ns - 1), ns)
        return peer, [pltpu.make_async_remote_copy(
            src_ref=halo_out.at[side, j], dst_ref=halo_in.at[side, j],
            send_sem=h_send.at[side], recv_sem=h_recv.at[side],
            device_id={"space": peer}, device_id_type=MESH) for j in range(nv)]

    for side in range(2):
        target, parts_of_halo = halo(side)

        @pl.when(turn(target) < my_turn)
        def _():
            for copy in parts_of_halo:
                copy.start()

    def to_mixer(other, cc):
        x, y = spot(other)
        return pltpu.make_async_remote_copy(
            src_ref=adj.at[pl.ds(FIRST[cc], COUNT[cc]), x, pl.ds(y, 8), :],
            dst_ref=inbox.at[me, pl.ds(0, COUNT[cc])],
            send_sem=a_send, recv_sem=a_recv,
            device_id={"inst": other * 2 + cc}, device_id_type=MESH)

    def send_across():
        for c in across:
            for cc in range(2):
                to_mixer(c, cc).start()

    @pl.when(jnp.logical_not(lean))
    def _():
        send_across()

    for c in beside:
        for cc in range(2):
            to_mixer(c, cc).start()
    for cc in range(2):
        @pl.when(core != cc)
        def _():
            to_mixer(chip, cc).start()

    @pl.when(lean)
    def _():
        pl.semaphore_wait(relay, 1)
        send_across()

    rest1.wait()
    rest2.wait()
    for c in bulk:
        c.wait()
    copies[7].wait()
    row = lax.broadcasted_iota(jnp.int32, (ny, nz), 0)
    lane = lax.broadcasted_iota(jnp.int32, (ny, nz), 1)

    def flux(j, carry):
        for x in range(nx):
            total = product(0, j, x) - src[j, x]
            if x > 0:
                total = total + product(1, j, x - 1)
            if x < nx - 1:
                total = total + product(2, j, x + 1)
            total = total + jnp.where(row == 0, 0.0, pltpu.roll(product(3, j, x), 1, 0))
            total = total + jnp.where(row == ny - 1, 0.0, pltpu.roll(product(4, j, x), ny - 1, 0))
            total = total + jnp.where(lane == 0, 0.0, pltpu.roll(product(5, j, x), 1, 1))
            total = total + jnp.where(lane == nz - 1, 0.0, pltpu.roll(product(6, j, x), nz - 1, 1))
            res[j, x] = total
        return carry

    lax.fori_loop(0, nv, flux, 0)

    def is_near(peer):
        return jnp.where(peer > sp, peer - sp, sp - peer) == 1

    def to_later(near):
        def act(peer):
            @pl.when(is_near(peer) if near else jnp.logical_not(is_near(peer)))
            def _():
                pl.semaphore_wait(ready_space.at[peer], 1)
                to_block(peer).start()

        later_blocks(act)
        for side in range(2):
            target, parts_of_halo = halo(side)
            chosen = is_near(target) if near else jnp.logical_not(is_near(target))

            @pl.when((turn(target) > my_turn) & chosen)
            def _():
                for copy in parts_of_halo:
                    copy.start()

    to_later(True)

    def arrived(block, semaphore):
        pltpu.make_async_copy(block, block, semaphore).wait()

    my_x, my_y = spot(chip)
    for cc in range(2):
        @pl.when(core == cc)
        def _():
            inbox[me, 0:COUNT[cc]] = adj[FIRST[cc]:FIRST[cc] + COUNT[cc], my_x, pl.ds(my_y, 8), :]

            arrived(inbox.at[pl.ds(0, ni - 1), pl.ds(0, COUNT[cc])], a_recv)

    weight = time_weight(ni)
    half = ni // 2

    def home(cc, d):
        peer = lax.rem(me + d, ni)
        return pltpu.make_async_remote_copy(
            src_ref=outbox.at[peer, pl.ds(0, COUNT[cc])],
            dst_ref=mixed.at[pl.ds(FIRST[cc], COUNT[cc]), my_x, pl.ds(my_y, 8), :],
            send_sem=b_send, recv_sem=b_recv,
            device_id={"inst": peer}, device_id_type=MESH)

    def mix(cc):
        n = COUNT[cc]
        a = [inbox[lax.rem(me + k, ni), 0:n] for k in range(ni)]
        even = [a[k] + a[k + half] for k in range(half)]
        odd = [a[k] - a[k + half] for k in range(half)]
        for d in sorted(range(half), key=lambda d: d == 0):
            near = [float(weight[(k - d) % ni]) for k in range(half)]
            far = [float(weight[(k - d + half) % ni]) for k in range(half)]
            plus = sum(even[k] * np.float32(0.5 * (near[k] + far[k])) for k in range(half))
            minus = sum(odd[k] * np.float32(0.5 * (near[k] - far[k])) for k in range(half))
            outbox[lax.rem(me + d + half, ni), 0:n] = plus - minus
            home(cc, d + half).start()
            if d:
                outbox[lax.rem(me + d, ni), 0:n] = plus + minus
                home(cc, d).start()
            else:
                mixed[FIRST[cc]:FIRST[cc] + n, my_x, pl.ds(my_y, 8), :] = plus + minus

    for cc in range(2):
        @pl.when(core == cc)
        def _():
            mix(cc)

    to_later(False)
    for cc in range(2):
        @pl.when(core == cc)
        def _():
            arrived(gauge.at[pl.ds(0, nv * nx * halves - COUNT[cc])], a_send)

    arrived(row_in.at[pl.ds(0, ns - 1)], m_send)
    copies[4].wait()
    copies[5].wait()
    copies[6].wait()

    def add_mixed():
        for cc in range(2):
            @pl.when(core == cc)
            def _():
                arrived(gauge.at[pl.ds(0, nv * nx * halves - COUNT[cc])], b_recv)

        for j in range(nv):
            for x in range(nx):
                res[j, x] = res[j, x] + vol[x] * mixed[j, x]

    def add_halo():
        for side in range(2):
            arrived(halo_in.at[side], h_recv.at[side])
        for j in range(nv):
            res[j, 0] = res[j, 0] + halo_in[0, j]
            res[j, nx - 1] = res[j, nx - 1] + halo_in[1, j]

    def add_back():
        arrived(row_in.at[pl.ds(0, ns - 1)], m_recv)
        sums = jnp.sum(row_in[...], axis=0)
        coords = sums[:, 0:modes] * inv[...]
        modal[...] = coords
        square = (lax.broadcasted_iota(jnp.int32, (modes, modes), 0)
                  == lax.broadcasted_iota(jnp.int32, (modes, modes), 1))
        column = jnp.sum(jnp.where(square, coords, 0.0), axis=1, keepdims=True)
        for x in range(nx):
            back = jnp.sum(gmat[x] * column, axis=0, keepdims=True)
            for j in range(nv):
                res[j, x, 0:1, :] = res[j, x, 0:1, :] + si[j, x:x + 1, :] * back

    @pl.when(my_turn < LATE)
    def _():
        add_mixed()
        add_halo()
        add_back()

    @pl.when(my_turn >= LATE)
    def _():
        add_back()
        add_halo()
        add_mixed()

    for side in range(2):
        arrived(halo_out.at[side], h_send.at[side])
    for cc in range(2):
        @pl.when(core == cc)
        def _():
            arrived(inbox.at[pl.ds(0, ni - 1), pl.ds(0, COUNT[cc])], b_send)


def put_out(res, modal, res_hbm, modal_hbm, sem):
    first = pltpu.make_async_copy(res, res_hbm.at[0], sem.at[0])
    second = pltpu.make_async_copy(modal, modal_hbm, sem.at[1])
    first.start()
    second.start()
    first.wait()
    second.wait()


def solution(mesh):
    ni, ns = mesh.shape["inst"], mesh.shape["space"]
    placed = (
        P("inst", None, "space", None, None),
        P("inst", None, None, None, "space", None, None),
        P("space", None, None),
        P("inst", None, "space", None, None),
        P(None, "space", None),
        P(None, "space", None),
        P("space", None),
        P(),
        P(),
    )

    def body(adjoint, jacobian, volume, source, surface_out, surface_in, station, phi, inv_stiff):
        _, nv, nx, ny, nz = adjoint.shape
        modes, stations = phi.shape
        inv_row = inv_stiff.reshape(1, modes)
        f32 = jnp.float32
        operands = (adjoint, jacobian, volume, source, surface_out, surface_in, station, phi, inv_row)
        vmem = pltpu.VMEM
        sem = pltpu.SemaphoreType.DMA
        residual, modal = pl.pallas_call(
            functools.partial(kernel, ni, ns),
            out_shape=(jax.ShapeDtypeStruct((nv, nx, ny, nz), f32), jax.ShapeDtypeStruct((1, modes), f32)),
            in_specs=[pl.BlockSpec(memory_space=pltpu.HBM)] * len(operands),
            out_specs=(pl.BlockSpec(memory_space=pltpu.VMEM), pl.BlockSpec(memory_space=pltpu.VMEM)),
            scratch_shapes=[
                vmem((nv, nx, ny, nz), f32), vmem(jacobian.shape[1:], f32), vmem((nx, ny, nz), f32),
                vmem((nv, nx, ny, nz), f32), vmem((nv, nx, nz), f32), vmem((nv, nx, nz), f32),
                vmem((nx, nz), jnp.int32), vmem((modes, stations), f32), vmem((1, modes), f32),
                vmem((ni, 3, 8, nz), f32), vmem((ni, 3, 8, nz), f32), vmem((nv, nx, ny, nz), f32),
                vmem((nv * nx * ny // 8, 8, nz), f32),
                vmem((2, nv, ny, nz), f32), vmem((2, nv, ny, nz), f32), vmem((nx, modes, nz), f32),
                vmem((1, nz), f32), vmem((ns, 1, nz), f32),
                sem((8,)), sem((9,)), sem, sem, sem, sem, sem((2,)), sem((2,)), sem, sem,
                pltpu.SemaphoreType.REGULAR((ns,)), pltpu.SemaphoreType.REGULAR,
            ],
            compiler_params=pltpu.CompilerParams(
                collective_id=0, has_side_effects=True, vmem_limit_bytes=24 << 20),
        )(*[pltpu.with_memory_space_constraint(x, pltpu.HBM) for x in operands])
        return pl.pallas_call(
            put_out,
            out_shape=(jax.ShapeDtypeStruct((1, nv, nx, ny, nz), f32), jax.ShapeDtypeStruct((1, modes), f32)),
            in_specs=[pl.BlockSpec(memory_space=vmem)] * 2,
            out_specs=(pl.BlockSpec(memory_space=pltpu.HBM), pl.BlockSpec(memory_space=pltpu.HBM)),
            scratch_shapes=[sem((2,))],
        )(*[pltpu.with_memory_space_constraint(x, vmem) for x in (residual, modal)])

    return jax.shard_map(
        body, mesh=mesh, in_specs=placed,
        out_specs=(P("inst", None, "space", None, None), P("inst", None)), check_vma=False)
```

```python
import functools

import numpy as np
import jax
import jax.numpy as jnp
from jax import lax
from jax.experimental import pallas as pl
from jax.experimental.pallas import tpu as pltpu
from jax.sharding import PartitionSpec as P

MESH = pl.DeviceIdType.MESH
FIRST = (0, 3)
COUNT = (3, 2)


def time_weight(count):
    k = np.arange(count)
    angle = np.pi * k / count
    parity = 1.0 - 2.0 * (k % 2)
    safe = np.where(k != 0, np.sin(angle), 1.0)
    first = np.where(k != 0, 0.5 * parity * np.cos(angle) / safe, 0.0)
    second = np.where(k != 0, -0.5 * parity / (safe * safe), -(count * count + 2) / 12.0)
    return first - 0.25 * second


LATE = 40
LEAN = 71
CLOSE = 55


def turn(block):
    z, y = lax.div(block, 2), lax.rem(block, 2)
    return jnp.where(z < 4, 10 * z, 51 + z) + 16 * y


def turn_of(block):
    z, y = divmod(block, 2)
    return (10 * z if z < 4 else 51 + z) + 16 * y


def kernel(
    ni, ns,
    adj_hbm, jac_hbm, vol_hbm, src_hbm, so_hbm, si_hbm, st_hbm, phi_hbm, inv_hbm,
    res, modal,
    adj, jac, vol, src, so, si, st, phi, inv,
    inbox, outbox, mixed, gauge, halo_out, halo_in, gmat, row_out, row_in,
    local_sem, jac_sem, a_send, a_recv, b_send, b_recv, h_send, h_recv, m_send, m_recv,
    ready_space, relay,
):
    me = lax.axis_index("inst")
    sp = lax.axis_index("space")
    core = lax.rem(me, 2)
    chip = lax.div(me, 2)
    nc = ni // 2
    nv, nx, ny, nz = adj.shape
    halves = ny // 8

    cx, cy, wide = lax.div(chip, 2), lax.rem(chip, 2), nc // 2
    across = [lax.rem(cx + 2, wide) * 2 + y for y in range(2)]
    beside = [lax.rem(cx + d, wide) * 2 + y for d in (1, wide - 1) for y in range(2)] + [cx * 2 + 1 - cy]

    def spot(c):
        return lax.div(c, halves), pl.multiple_of(lax.rem(c, halves) * 8, 8)

    def send_signals(semaphore, axis, peer):
        pl.semaphore_signal(semaphore, inc=1, device_id={axis: peer}, device_id_type=MESH)

    barrier = pltpu.get_barrier_semaphore()

    my_turn = turn(sp)
    lean = my_turn >= LEAN

    def later_blocks(act):
        for peer in sorted(range(ns), key=turn_of):
            @pl.when(turn_of(peer) > my_turn)
            def _():
                act(peer)

    @pl.when(my_turn >= CLOSE)
    def _():
        later_blocks(lambda peer: send_signals(barrier, "space", peer))

    @pl.when(jnp.logical_not(lean))
    def _():
        for c in across:
            for cc in range(2):
                send_signals(barrier, "inst", c * 2 + cc)

    for c in beside:
        for cc in range(2):
            send_signals(barrier, "inst", c * 2 + cc)
    send_signals(barrier, "inst", chip * 2 + 1 - core)

    @pl.when(my_turn < CLOSE)
    def _():
        later_blocks(lambda peer: send_signals(barrier, "space", peer))

    n_earlier = sum(jnp.where(turn_of(p) < my_turn, 1, 0) for p in range(ns))

    small = [(st_hbm, st), (phi_hbm, phi), (so_hbm, so), (adj_hbm.at[0], adj), (inv_hbm, inv),
             (si_hbm, si), (vol_hbm, vol), (src_hbm.at[0], src)]
    copies = [pltpu.make_async_copy(a, b, local_sem.at[n]) for n, (a, b) in enumerate(small)]
    edge1 = pltpu.make_async_copy(jac_hbm.at[0, 1, :, :, nx - 1], jac.at[1, :, :, nx - 1], jac_sem.at[7])
    edge2 = pltpu.make_async_copy(jac_hbm.at[0, 2, :, :, 0], jac.at[2, :, :, 0], jac_sem.at[8])
    rest1 = pltpu.make_async_copy(jac_hbm.at[0, 1, :, :, 0:nx - 1], jac.at[1, :, :, 0:nx - 1], jac_sem.at[1])
    rest2 = pltpu.make_async_copy(jac_hbm.at[0, 2, :, :, 1:nx], jac.at[2, :, :, 1:nx], jac_sem.at[2])
    bulk = [pltpu.make_async_copy(jac_hbm.at[0, d], jac.at[d], jac_sem.at[d]) for d in (0, 3, 4, 5, 6)]
    for c in copies[:4] + [edge1, edge2] + copies[4:] + [rest1, rest2] + bulk:
        c.start()

    copies[0].wait()
    copies[1].wait()
    modes, stations = phi.shape
    for x in range(nx):
        where = jnp.broadcast_to(st[x:x + 1, :], (modes, nz))
        column = lax.rem(where, nz)
        taken = jnp.zeros((modes, nz), jnp.float32)
        for start in range(0, stations, nz):
            found = jnp.take_along_axis(phi[:, start:start + nz], column, axis=1, mode="promise_in_bounds")
            taken = jnp.where(where - column == start, found, taken)
        gmat[x] = taken

    copies[2].wait()
    copies[3].wait()
    col = jnp.zeros((modes, nz), jnp.float32)
    for x in range(nx):
        face = so[0, x:x + 1, :] * adj[0, x, 0:1, :]
        for j in range(1, nv):
            face = face + so[j, x:x + 1, :] * adj[j, x, 0:1, :]
        col = col + gmat[x] * face
    col = jnp.sum(col, axis=1, keepdims=True)
    diag = (lax.broadcasted_iota(jnp.int32, (modes, nz), 0)
            == lax.broadcasted_iota(jnp.int32, (modes, nz), 1))
    share = jnp.sum(jnp.where(diag, col, 0.0), axis=0, keepdims=True)
    row_out[...] = share
    row_in[sp] = share

    def product(d, j, x):
        total = jac[d, 0, j, x] * adj[0, x]
        for i in range(1, nv):
            total = total + jac[d, i, j, x] * adj[i, x]
        return total

    edge1.wait()
    edge2.wait()
    for side, d, x in ((0, 1, nx - 1), (1, 2, 0)):
        for j in range(nv):
            halo_out[side, j] = product(d, j, x)

    pl.semaphore_wait(barrier, ni - 1 + n_earlier - jnp.where(lean, 2 * len(across), 0))

    @pl.when(lean)
    def _():
        send_signals(relay, "inst", lax.rem(me + ni - 4, ni))

    def to_block(peer):
        return pltpu.make_async_remote_copy(
            src_ref=row_out, dst_ref=row_in.at[sp],
            send_sem=m_send, recv_sem=m_recv,
            device_id={"space": peer}, device_id_type=MESH)

    def report(peers):
        for peer in peers:
            @pl.when(turn_of(peer) < my_turn)
            def _():
                to_block(peer).start()
                send_signals(ready_space.at[sp], "space", peer)

    in_turn = sorted(range(ns), key=turn_of)
    report(in_turn[:1])

    def halo(side):
        peer = lax.rem(sp + (1 if side == 0 else ns - 1), ns)
        return peer, [pltpu.make_async_remote_copy(
            src_ref=halo_out.at[side, j], dst_ref=halo_in.at[side, j],
            send_sem=h_send.at[side], recv_sem=h_recv.at[side],
            device_id={"space": peer}, device_id_type=MESH) for j in range(nv)]

    for side in range(2):
        target, parts_of_halo = halo(side)

        @pl.when(turn(target) < my_turn)
        def _():
            for copy in parts_of_halo:
                copy.start()

    report(in_turn[1:])

    def to_mixer(other, cc):
        x, y = spot(other)
        return pltpu.make_async_remote_copy(
            src_ref=adj.at[pl.ds(FIRST[cc], COUNT[cc]), x, pl.ds(y, 8), :],
            dst_ref=inbox.at[me, pl.ds(0, COUNT[cc])],
            send_sem=a_send, recv_sem=a_recv,
            device_id={"inst": other * 2 + cc}, device_id_type=MESH)

    def send_across():
        for c in across:
            for cc in range(2):
                to_mixer(c, cc).start()

    @pl.when(jnp.logical_not(lean))
    def _():
        send_across()

    for c in beside:
        for cc in range(2):
            to_mixer(c, cc).start()
    for cc in range(2):
        @pl.when(core != cc)
        def _():
            to_mixer(chip, cc).start()

    @pl.when(lean)
    def _():
        pl.semaphore_wait(relay, 1)
        send_across()

    rest1.wait()
    rest2.wait()
    for c in bulk:
        c.wait()
    copies[7].wait()
    row = lax.broadcasted_iota(jnp.int32, (ny, nz), 0)
    lane = lax.broadcasted_iota(jnp.int32, (ny, nz), 1)

    def flux(j, carry):
        for x in range(nx):
            total = product(0, j, x) - src[j, x]
            if x > 0:
                total = total + product(1, j, x - 1)
            if x < nx - 1:
                total = total + product(2, j, x + 1)
            total = total + jnp.where(row == 0, 0.0, pltpu.roll(product(3, j, x), 1, 0))
            total = total + jnp.where(row == ny - 1, 0.0, pltpu.roll(product(4, j, x), ny - 1, 0))
            total = total + jnp.where(lane == 0, 0.0, pltpu.roll(product(5, j, x), 1, 1))
            total = total + jnp.where(lane == nz - 1, 0.0, pltpu.roll(product(6, j, x), nz - 1, 1))
            res[j, x] = total
        return carry

    lax.fori_loop(0, nv, flux, 0)

    def is_near(peer):
        return jnp.where(peer > sp, peer - sp, sp - peer) == 1

    def to_later(near):
        def act(peer):
            @pl.when(is_near(peer) if near else jnp.logical_not(is_near(peer)))
            def _():
                pl.semaphore_wait(ready_space.at[peer], 1)
                to_block(peer).start()

        later_blocks(act)
        for side in range(2):
            target, parts_of_halo = halo(side)
            chosen = is_near(target) if near else jnp.logical_not(is_near(target))

            @pl.when((turn(target) > my_turn) & chosen)
            def _():
                for copy in parts_of_halo:
                    copy.start()

    to_later(True)

    def arrived(block, semaphore):
        pltpu.make_async_copy(block, block, semaphore).wait()

    my_x, my_y = spot(chip)
    for cc in range(2):
        @pl.when(core == cc)
        def _():
            inbox[me, 0:COUNT[cc]] = adj[FIRST[cc]:FIRST[cc] + COUNT[cc], my_x, pl.ds(my_y, 8), :]

            arrived(inbox.at[pl.ds(0, ni - 1), pl.ds(0, COUNT[cc])], a_recv)

    weight = time_weight(ni)
    half = ni // 2

    def home(cc, d):
        peer = lax.rem(me + d, ni)
        return pltpu.make_async_remote_copy(
            src_ref=outbox.at[peer, pl.ds(0, COUNT[cc])],
            dst_ref=mixed.at[pl.ds(FIRST[cc], COUNT[cc]), my_x, pl.ds(my_y, 8), :],
            send_sem=b_send, recv_sem=b_recv,
            device_id={"inst": peer}, device_id_type=MESH)

    def mix(cc):
        n = COUNT[cc]
        a = [inbox[lax.rem(me + k, ni), 0:n] for k in range(ni)]
        even = [a[k] + a[k + half] for k in range(half)]
        odd = [a[k] - a[k + half] for k in range(half)]
        for d in sorted(range(half), key=lambda d: d == 0):
            near = [float(weight[(k - d) % ni]) for k in range(half)]
            far = [float(weight[(k - d + half) % ni]) for k in range(half)]
            plus = sum(even[k] * np.float32(0.5 * (near[k] + far[k])) for k in range(half))
            minus = sum(odd[k] * np.float32(0.5 * (near[k] - far[k])) for k in range(half))
            outbox[lax.rem(me + d + half, ni), 0:n] = plus - minus
            home(cc, d + half).start()
            if d:
                outbox[lax.rem(me + d, ni), 0:n] = plus + minus
                home(cc, d).start()
            else:
                mixed[FIRST[cc]:FIRST[cc] + n, my_x, pl.ds(my_y, 8), :] = plus + minus

    for cc in range(2):
        @pl.when(core == cc)
        def _():
            mix(cc)

    to_later(False)
    for cc in range(2):
        @pl.when(core == cc)
        def _():
            arrived(gauge.at[pl.ds(0, nv * nx * halves - COUNT[cc])], a_send)

    arrived(row_in.at[pl.ds(0, ns - 1)], m_send)
    copies[4].wait()
    copies[5].wait()
    copies[6].wait()

    def add_mixed():
        for cc in range(2):
            @pl.when(core == cc)
            def _():
                arrived(gauge.at[pl.ds(0, nv * nx * halves - COUNT[cc])], b_recv)

        for j in range(nv):
            for x in range(nx):
                res[j, x] = res[j, x] + vol[x] * mixed[j, x]

    def add_halo():
        for side in range(2):
            arrived(halo_in.at[side], h_recv.at[side])
        for j in range(nv):
            res[j, 0] = res[j, 0] + halo_in[0, j]
            res[j, nx - 1] = res[j, nx - 1] + halo_in[1, j]

    def add_back():
        arrived(row_in.at[pl.ds(0, ns - 1)], m_recv)
        sums = jnp.sum(row_in[...], axis=0)
        coords = sums[:, 0:modes] * inv[...]
        modal[...] = coords
        square = (lax.broadcasted_iota(jnp.int32, (modes, modes), 0)
                  == lax.broadcasted_iota(jnp.int32, (modes, modes), 1))
        column = jnp.sum(jnp.where(square, coords, 0.0), axis=1, keepdims=True)
        for x in range(nx):
            back = jnp.sum(gmat[x] * column, axis=0, keepdims=True)
            for j in range(nv):
                res[j, x, 0:1, :] = res[j, x, 0:1, :] + si[j, x:x + 1, :] * back

    @pl.when(my_turn < LATE)
    def _():
        add_mixed()
        add_halo()
        add_back()

    @pl.when(my_turn >= LATE)
    def _():
        add_back()
        add_halo()
        add_mixed()

    for side in range(2):
        arrived(halo_out.at[side], h_send.at[side])
    for cc in range(2):
        @pl.when(core == cc)
        def _():
            arrived(inbox.at[pl.ds(0, ni - 1), pl.ds(0, COUNT[cc])], b_send)


def put_out(res, modal, res_hbm, modal_hbm, sem):
    first = pltpu.make_async_copy(res, res_hbm.at[0], sem.at[0])
    second = pltpu.make_async_copy(modal, modal_hbm, sem.at[1])
    first.start()
    second.start()
    first.wait()
    second.wait()


def solution(mesh):
    ni, ns = mesh.shape["inst"], mesh.shape["space"]
    placed = (
        P("inst", None, "space", None, None),
        P("inst", None, None, None, "space", None, None),
        P("space", None, None),
        P("inst", None, "space", None, None),
        P(None, "space", None),
        P(None, "space", None),
        P("space", None),
        P(),
        P(),
    )

    def body(adjoint, jacobian, volume, source, surface_out, surface_in, station, phi, inv_stiff):
        _, nv, nx, ny, nz = adjoint.shape
        modes, stations = phi.shape
        inv_row = inv_stiff.reshape(1, modes)
        f32 = jnp.float32
        operands = (adjoint, jacobian, volume, source, surface_out, surface_in, station, phi, inv_row)
        vmem = pltpu.VMEM
        sem = pltpu.SemaphoreType.DMA
        residual, modal = pl.pallas_call(
            functools.partial(kernel, ni, ns),
            out_shape=(jax.ShapeDtypeStruct((nv, nx, ny, nz), f32), jax.ShapeDtypeStruct((1, modes), f32)),
            in_specs=[pl.BlockSpec(memory_space=pltpu.HBM)] * len(operands),
            out_specs=(pl.BlockSpec(memory_space=pltpu.VMEM), pl.BlockSpec(memory_space=pltpu.VMEM)),
            scratch_shapes=[
                vmem((nv, nx, ny, nz), f32), vmem(jacobian.shape[1:], f32), vmem((nx, ny, nz), f32),
                vmem((nv, nx, ny, nz), f32), vmem((nv, nx, nz), f32), vmem((nv, nx, nz), f32),
                vmem((nx, nz), jnp.int32), vmem((modes, stations), f32), vmem((1, modes), f32),
                vmem((ni, 3, 8, nz), f32), vmem((ni, 3, 8, nz), f32), vmem((nv, nx, ny, nz), f32),
                vmem((nv * nx * ny // 8, 8, nz), f32),
                vmem((2, nv, ny, nz), f32), vmem((2, nv, ny, nz), f32), vmem((nx, modes, nz), f32),
                vmem((1, nz), f32), vmem((ns, 1, nz), f32),
                sem((8,)), sem((9,)), sem, sem, sem, sem, sem((2,)), sem((2,)), sem, sem,
                pltpu.SemaphoreType.REGULAR((ns,)), pltpu.SemaphoreType.REGULAR,
            ],
            compiler_params=pltpu.CompilerParams(
                collective_id=0, has_side_effects=True, vmem_limit_bytes=24 << 20),
        )(*[pltpu.with_memory_space_constraint(x, pltpu.HBM) for x in operands])
        return pl.pallas_call(
            put_out,
            out_shape=(jax.ShapeDtypeStruct((1, nv, nx, ny, nz), f32), jax.ShapeDtypeStruct((1, modes), f32)),
            in_specs=[pl.BlockSpec(memory_space=vmem)] * 2,
            out_specs=(pl.BlockSpec(memory_space=pltpu.HBM), pl.BlockSpec(memory_space=pltpu.HBM)),
            scratch_shapes=[sem((2,))],
        )(*[pltpu.with_memory_space_constraint(x, vmem) for x in (residual, modal)])

    return jax.shard_map(
        body, mesh=mesh, in_specs=placed,
        out_specs=(P("inst", None, "space", None, None), P("inst", None)), check_vma=False)
```
